32 devices in a mesh: wide: 16 (over z, y, x), narrow: 2 (over core).
Axes of the slice: x: 2, y: 2, z: 4, core: 2. Of those that a mesh axis runs over, the one named last changes fastest.
Arguments:
- tokens: bfloat16 [16384, 768], P(('wide', 'narrow')), may hold values from -6 to 6
- plot_slot: int32 [16384], P('wide'), may hold values from 0 to 1, as said below
- patch_mask: int32 [16384], P('wide'), may hold values from 0 to 1, as said below
- cotangent: bfloat16 [16384, 768], P(('wide', 'narrow')), may hold values from -6 to 6
- gain_attn: float32 [768], replicated, may hold values from 0.5 to 1.5
- w_qkv: bfloat16 [3, 768, 768], P(None, None, 'narrow'), may hold values from -0.21875 to 0.21875
- w_out: bfloat16 [768, 768], P('narrow'), may hold values from -2.5 to 2.5
- gain_mlp: float32 [768], replicated, may hold values from 0.5 to 1.5
- w_gu: bfloat16 [2, 768, 2048], P(None, None, 'narrow'), may hold values from -0.21875 to 0.21875
- w_down: bfloat16 [2048, 768], P('narrow'), may hold values from -0.125 to 0.125
- qkv_rows: float32 [3, 768], replicated, may hold values from 16.384 to 1638.4
- qkv_cols: float32 [3, 768], P(None, 'narrow'), may hold values from 16.384 to 1638.4
- out_rows: float32 [768], P('narrow'), may hold values from 16.384 to 1638.4
- out_cols: float32 [768], replicated, may hold values from 16.384 to 1638.4
- gu_rows: float32 [2, 768], replicated, may hold values from 16.384 to 1638.4
- gu_cols: float32 [2, 2048], P(None, 'narrow'), may hold values from 16.384 to 1638.4
- down_rows: float32 [2048], P('narrow'), may hold values from 16.384 to 1638.4
- down_cols: float32 [768], replicated, may hold values from 16.384 to 1638.4
- step_count: int32 [], replicated, may hold values from 4 to 399
- learn_rate: float32 [], replicated, may hold values from 0.02 to 0.2
Outputs:
- mixed_out: bfloat16 [16384, 768], P(('wide', 'narrow'))
- tokens_grad: float32 [16384, 768], P(('wide', 'narrow'))
- gain_attn_grad: float32 [768], P('wide')
- qkv_grad: float32 [3, 768, 768], P(None, 'wide', 'narrow')
- out_grad: float32 [768, 768], P('narrow', 'wide')
- gain_mlp_grad: float32 [768], P('wide')
- gu_grad: float32 [2, 768, 2048], P(None, 'wide', 'narrow')
- down_grad: float32 [2048, 768], P('narrow', 'wide')
- qkv_new: bfloat16 [3, 768, 768], P(None, 'wide', 'narrow')
- out_new: bfloat16 [768, 768], P('narrow', 'wide')
- gu_new: bfloat16 [2, 768, 2048], P(None, 'wide', 'narrow')
- down_new: bfloat16 [2048, 768], P('narrow', 'wide')
- qkv_rows_new: float32 [3, 768], P(None, 'wide')
- qkv_cols_new: float32 [3, 768], P(None, 'narrow')
- out_rows_new: float32 [768], P('narrow')
- out_cols_new: float32 [768], P('wide')
- gu_rows_new: float32 [2, 768], P(None, 'wide')
- gu_cols_new: float32 [2, 2048], P(None, 'narrow')
- down_rows_new: float32 [2048], P('narrow')
- down_cols_new: float32 [768], P('wide')
The draws below stay inside these ranges and needn't reach their ends.
Inputs may be any that keep to these rules, and one draw needn't show every extreme that they name: `plot_slot`: within each aligned block of 1024 tokens, plots are numbered from 0 in order; each plot holds 512 or 1024 consecutive tokens and starts at a multiple of 256; some block holds one plot of 1024 tokens and some block holds two plots. `patch_mask`: in each plot the ones form a prefix of at least half of the plot's tokens; the rest of the plot is zero.
All inputs are finite; a program needn't handle non-finite values.
Results may differ from the reference program's by a relative error of at most 0.019.
Values may be sent and summed in bfloat16 or wider, within the bound.
No kernel may reach another device: no remote copies, remote signals or barrier semaphores. Data moves between devices by JAX's collectives and lax.ppermute only.
A program may use at most 128 MiB of HBM per device.

```python
import math
import jax
import jax.numpy as jnp
import numpy as np
from jax import lax

D = 768
H = 12
DH = 64
FF = 2048
HD = 768
U = 256
TOK_DEV = 1024
TOKENS = 16384
N_WIDE = 16


def plot_layout(key):
    group_count = TOKENS // TOK_DEV
    pattern = jax.random.randint(jax.random.fold_in(key, 7), (group_count,), 0, 2)
    pattern = pattern.at[0].set(1).at[1].set(0)
    slot_table = jnp.array(np.array([[0, 0, 0, 0], [0, 0, 1, 1]], np.int32))
    start_table = jnp.array(np.array([[0, 0, 0, 0], [0, 0, 2, 2]], np.int32))
    units_table = jnp.array(np.array([4, 2], np.int32))
    unit_slot = jnp.take(slot_table, pattern, axis=0)
    unit_start = jnp.take(start_table, pattern, axis=0)
    plot_units = jnp.take(units_table, pattern, axis=0)
    half_length = (plot_units * (U // 2))[:, None]
    extra = jax.random.randint(jax.random.fold_in(key, 13), (group_count, 2), 0, half_length + 1)
    patch_counts = half_length + extra
    positions = jnp.arange(TOK_DEV, dtype=jnp.int32)
    unit_index = positions // U
    slot_tokens = jnp.take(unit_slot, unit_index, axis=1)
    start_tokens = jnp.take(unit_start, unit_index, axis=1) * U
    inside = positions[None, :] - start_tokens
    count_tokens = jnp.take_along_axis(patch_counts, slot_tokens, axis=1)
    mask_tokens = (inside < count_tokens).astype(jnp.int32)
    return (slot_tokens.reshape(-1).astype(jnp.int32), mask_tokens.reshape(-1))


def draw_plot_slot(key, part):
    return plot_layout(key)[0]


def draw_patch_mask(key, part):
    return plot_layout(key)[1]


def level_of(stream_key, shape, cuts, low, top_value):
    level, own = 1.0, jax.random.fold_in(stream_key, 6)
    for axis_at, blocks in cuts:
        steps = jnp.exp(jax.random.uniform(jax.random.fold_in(own, axis_at), (blocks,), jnp.float32, low / len(cuts), top_value / len(cuts)))
        level = level * jnp.repeat(steps, shape[axis_at] // blocks).reshape([-1 if axis == axis_at else 1 for axis in range(len(shape))])
    return level


def scatter_about(rng, extent, spread, reach, split=(), held_as=jnp.bfloat16):
    loudness = level_of(rng, extent, split, -0.22, 0.18) if split else 1.0
    values = jax.random.normal(rng, extent, jnp.float32) * spread * loudness
    return jnp.minimum(jnp.maximum(values, -reach), reach).astype(held_as)


def setup_inputs(seed: int = 0) -> dict:
    keys = jax.random.split(jax.random.key(seed), 21)
    return {
        "tokens": scatter_about(keys[0], (TOKENS, D), 1.0, 6.0, ((0, 32),)),
        "plot_slot": draw_plot_slot(jax.random.fold_in(keys[20], 71), 0),
        "patch_mask": draw_patch_mask(jax.random.fold_in(keys[20], 71), 0),
        "cotangent": scatter_about(keys[3], (TOKENS, D), 1.0, 6.0, ((0, 32),)),
        "gain_attn": jnp.clip(1.0 + 0.1 * jax.random.normal(keys[4], (D,), jnp.float32), 0.5, 1.5),
        "w_qkv": scatter_about(keys[5], (3, D, HD), D ** -0.5, 0.21875, ((2, 2),)),
        "w_out": scatter_about(keys[6], (HD, D), (HD * 2 // U) ** -0.5, 2.5, ((0, 2),)),
        "gain_mlp": jnp.clip(1.0 + 0.1 * jax.random.normal(keys[7], (D,), jnp.float32), 0.5, 1.5),
        "w_gu": scatter_about(keys[8], (2, D, FF), D ** -0.5, 0.21875, ((2, 2),)),
        "w_down": scatter_about(keys[9], (FF, D), FF ** -0.5, 0.125, ((0, 2),)),
        "qkv_rows": jnp.clip(jnp.exp(jax.random.uniform(keys[10], (3, D), jnp.float32, math.log(16.384), math.log(1638.4))), 16.384, 1638.4),
        "qkv_cols": jnp.clip(jnp.exp(math.log(1638.4) - 4.6051702 * jax.random.uniform(keys[11], (3, HD), jnp.float32) ** level_of(keys[11], (3, HD), ((1, 2),), -0.2, 0.2)), 16.384, 1638.4),
        "out_rows": jnp.clip(jnp.exp(math.log(1638.4) - 4.6051702 * jax.random.uniform(keys[12], (HD,), jnp.float32) ** level_of(keys[12], (HD,), ((0, 2),), -0.2, 0.2)), 16.384, 1638.4),
        "out_cols": jnp.clip(jnp.exp(jax.random.uniform(keys[13], (D,), jnp.float32, math.log(16.384), math.log(1638.4))), 16.384, 1638.4),
        "gu_rows": jnp.clip(jnp.exp(jax.random.uniform(keys[14], (2, D), jnp.float32, math.log(16.384), math.log(1638.4))), 16.384, 1638.4),
        "gu_cols": jnp.clip(jnp.exp(math.log(1638.4) - 4.6051702 * jax.random.uniform(keys[15], (2, FF), jnp.float32) ** level_of(keys[15], (2, FF), ((1, 2),), -0.2, 0.2)), 16.384, 1638.4),
        "down_rows": jnp.clip(jnp.exp(math.log(1638.4) - 4.6051702 * jax.random.uniform(keys[16], (FF,), jnp.float32) ** level_of(keys[16], (FF,), ((0, 2),), -0.2, 0.2)), 16.384, 1638.4),
        "down_cols": jnp.clip(jnp.exp(jax.random.uniform(keys[17], (D,), jnp.float32, math.log(16.384), math.log(1638.4))), 16.384, 1638.4),
        "step_count": jax.random.randint(keys[18], (), 4, 400).astype(jnp.int32),
        "learn_rate": jnp.clip(jax.random.uniform(keys[19], (), jnp.float32, 0.02, 0.2), 0.02, 0.2),
    }


@jax.custom_vjp
def low(v):
    return lax.optimization_barrier(v.astype(jnp.bfloat16)).astype(jnp.float32)

@jax.custom_vjp
def low_back(v):
    return v

def low_keep(v):
    return (low(v), None)

def low_pass(kept, grad):
    return (grad,)

def back_keep(v):
    return (v, None)

def back_low(kept, grad):
    return (low(grad),)
low.defvjp(low_keep, low_pass)
low_back.defvjp(back_keep, back_low)
EPSILON = 1e-06
TINIEST = 1e-30
NEGATIVE = -1e+30
PRECISE = lax.Precision.HIGHEST

def normed(rows_in, gain_row):
    return rows_in * lax.rsqrt(lax.optimization_barrier(jnp.mean(rows_in * rows_in, axis=-1, keepdims=True)) + EPSILON) * gain_row

def attend(queries, keys_all, values_all, slot_rows, mask_rows):
    token_count = queries.shape[0]
    block_count = token_count // U
    query_blocks = queries.reshape(block_count, U, H, DH)
    slot_blocks = slot_rows.reshape(block_count, U)
    live_keys = mask_rows > 0
    head_scale = 1.0 / math.sqrt(DH)

    def one_block(block_pair):
        query_rows, query_slots = block_pair
        scores = low_back(jnp.einsum('qhd,khd->hqk', query_rows, keys_all, precision=PRECISE) * head_scale)
        allowed = (query_slots[:, None] == slot_rows[None, :]) & live_keys[None, :]
        scores = jnp.where(allowed[None], scores, NEGATIVE)
        highest = lax.optimization_barrier(jnp.max(scores, axis=-1, keepdims=True))
        exp_scores = jnp.exp(scores - highest)
        softmax_rows = exp_scores / lax.optimization_barrier(jnp.sum(exp_scores, axis=-1, keepdims=True))
        return jnp.einsum('hqk,khd->qhd', low(softmax_rows), values_all, precision=PRECISE)
    outputs = lax.map(jax.checkpoint(one_block), (query_blocks, slot_blocks))
    return outputs.reshape(token_count, H * DH)

def layer(rows_in, w_qkv, w_out, w_gu, w_down, gain_attn, gain_mlp, slot_rows, mask_rows):
    token_count = rows_in.shape[0]
    attn_normed = low(normed(rows_in, gain_attn))
    projected = low_back(low(jnp.einsum('td,kde->kte', attn_normed, w_qkv, precision=PRECISE)))
    attn_mixed = attend(projected[0].reshape(token_count, H, DH), projected[1].reshape(token_count, H, DH), projected[2].reshape(token_count, H, DH), slot_rows, mask_rows)
    attn_mixed = low_back(low(attn_mixed))
    middle = rows_in + low_back(jnp.dot(attn_mixed, w_out, precision=PRECISE))
    mlp_normed = low(normed(middle, gain_mlp))
    paired = low_back(jnp.einsum('td,kdf->ktf', mlp_normed, w_gu, precision=PRECISE))
    hidden = low(jax.nn.gelu(paired[0], approximate=True) * paired[1])
    return middle + low_back(jnp.dot(hidden, w_down, precision=PRECISE))

def adapt(gradient, weight, row_stats, col_stats, decay_beta, learn_rate):
    squares = gradient * gradient + TINIEST
    row_new = decay_beta * row_stats + (1.0 - decay_beta) * lax.optimization_barrier(jnp.mean(squares, axis=1))
    col_new = decay_beta * col_stats + (1.0 - decay_beta) * lax.optimization_barrier(jnp.mean(squares, axis=0))
    scaled = gradient * lax.rsqrt(row_new[:, None] * col_new[None, :] / jnp.mean(row_new))
    weight_f32 = weight.astype(jnp.float32)
    step_size = learn_rate * jnp.sqrt(jnp.mean(weight_f32 * weight_f32))
    return ((weight_f32 - step_size * scaled).astype(jnp.bfloat16), row_new, col_new)

def reference(tokens, plot_slot, patch_mask, cotangent, gain_attn, w_qkv, w_out, gain_mlp, w_gu, w_down, qkv_rows, qkv_cols, out_rows, out_cols, gu_rows, gu_cols, down_rows, down_cols, step_count, learn_rate):
    weights = (w_qkv.astype(jnp.float32), w_out.astype(jnp.float32), w_gu.astype(jnp.float32), w_down.astype(jnp.float32), gain_attn.astype(jnp.float32), gain_mlp.astype(jnp.float32))
    inputs = tokens.astype(jnp.float32).reshape(N_WIDE, TOK_DEV, D)
    live_rows = patch_mask.astype(jnp.float32)
    seeds = (cotangent.astype(jnp.float32) * live_rows[:, None]).reshape(N_WIDE, TOK_DEV, D)
    slot_groups = plot_slot.reshape(N_WIDE, TOK_DEV)
    mask_groups = patch_mask.reshape(N_WIDE, TOK_DEV)

    def one_group(totals, group_item):
        rows_in, seed_rows, slot_rows, mask_rows = group_item

        def layer_of(rows_x, weight_a, weight_b, weight_c, weight_d, gain_a, gain_b):
            return layer(rows_x, weight_a, weight_b, weight_c, weight_d, gain_a, gain_b, slot_rows, mask_rows)
        result, pullback = jax.vjp(layer_of, rows_in, *weights)
        grad_parts = pullback(seed_rows)
        totals = tuple((left + right for left, right in zip(totals, grad_parts[1:])))
        return (totals, (result.astype(jnp.bfloat16), grad_parts[0]))
    zero_grads = tuple((jnp.zeros_like(weight) for weight in weights))
    totals, (mixed_out, tokens_grad) = lax.scan(one_group, zero_grads, (inputs, seeds, slot_groups, mask_groups))
    qkv_grad, out_grad, gu_grad, down_grad, gain_attn_grad, gain_mlp_grad = totals
    decay_beta = 1.0 - lax.rsqrt(step_count.astype(jnp.float32))
    stacked_adapt = jax.vmap(adapt, in_axes=(0, 0, 0, 0, None, None))
    qkv_new, qkv_rows_new, qkv_cols_new = stacked_adapt(qkv_grad, w_qkv, qkv_rows, qkv_cols, decay_beta, learn_rate)
    out_new, out_rows_new, out_cols_new = adapt(out_grad, w_out, out_rows, out_cols, decay_beta, learn_rate)
    gu_new, gu_rows_new, gu_cols_new = stacked_adapt(gu_grad, w_gu, gu_rows, gu_cols, decay_beta, learn_rate)
    down_new, down_rows_new, down_cols_new = adapt(down_grad, w_down, down_rows, down_cols, decay_beta, learn_rate)
    return (mixed_out.reshape(TOKENS, D), tokens_grad.reshape(TOKENS, D), gain_attn_grad, qkv_grad, out_grad, gain_mlp_grad, gu_grad, down_grad, qkv_new, out_new, gu_new, down_new, qkv_rows_new, qkv_cols_new, out_rows_new, out_cols_new, gu_rows_new, gu_cols_new, down_rows_new, down_cols_new)
```

```python
import functools
import math

import jax
import jax.numpy as jnp
from jax import lax
from jax.experimental import pallas as pl
from jax.experimental.pallas import tpu as pltpu
from jax.sharding import PartitionSpec as P

DH = 64
LANES = 128
EPSILON = 1e-06
TINIEST = 1e-30
NEGATIVE = -1e30
F32 = jnp.float32
BF16 = jnp.bfloat16
ROOT = math.sqrt(2.0 / math.pi)
CUBE = 0.044715


def mm(a, b):
    return jnp.dot(a, b, preferred_element_type=F32)


def mm_nt(a, b):
    return lax.dot_general(a, b, (((1,), (1,)), ((), ())), preferred_element_type=F32)


def whole(shape):
    return pl.BlockSpec(shape, lambda *_: (0,) * len(shape))


def cost(flops, nbytes):
    return pl.CostEstimate(flops=int(flops), bytes_accessed=int(nbytes), transcendentals=0)


def inverse_rms(rows):
    return lax.rsqrt(jnp.mean(rows * rows, axis=-1, keepdims=True) + EPSILON)


def three_terms(values):
    high = values.astype(BF16)
    rest = values - high.astype(F32)
    middle = rest.astype(BF16)
    return high, middle, (rest - middle.astype(F32)).astype(BF16)


def bit_orders(n_wide):
    bits = n_wide.bit_length() - 1
    straight = list(range(bits))
    turned = straight[1:-1] + straight[:1] + straight[-1:] if bits > 2 else straight
    return straight, turned


def slot_table(wide_index, order, n_wide):
    bits = len(order)
    entries = []
    for slot in range(n_wide):
        mask = 0
        for stage, bit in enumerate(order):
            if slot >> (bits - 1 - stage) & 1:
                mask |= 1 << bit
        entries.append(mask)
    return jnp.bitwise_xor(jnp.asarray(entries, jnp.int32), wide_index.astype(jnp.int32))


def stage_exchange(values, stage, n_wide):
    orders = bit_orders(n_wide)
    pairs = []
    for wide in range(n_wide):
        for core in range(2):
            pairs.append((wide * 2 + core, (wide ^ (1 << orders[core][stage])) * 2 + core))
    return lax.ppermute(values, ("wide", "narrow"), pairs)


def swap(values):
    return lax.ppermute(values, "narrow", [(0, 1), (1, 0)])


def write_slots(table_ref, held_ref, targets, columns, rows_each):
    if targets[0].ndim == 2:
        targets[0][:, columns] = held_ref[...].astype(BF16)
        return
    slot = 0
    for target in targets:
        for at in range(target.shape[0]):
            start = pl.multiple_of(table_ref[slot] * rows_each, 16)
            target[at, :, columns] = held_ref[pl.ds(start, rows_each), :].astype(BF16)
            slot += 1


def project_kernel(own_ref, other_ref, gain_ref, w_ref, normed_t_ref, projected_ref):
    count = own_ref.shape[0]
    for half, rows_ref in enumerate((own_ref, other_ref)):
        rows = rows_ref[...].astype(F32)
        normed = (rows * inverse_rms(rows) * gain_ref[...]).astype(BF16)
        at = slice(half * count, (half + 1) * count)
        normed_t_ref[:, at] = normed.T
        for i in range(3):
            projected_ref[i, at, :] = mm(normed, w_ref[i]).astype(BF16)


def project(own, other, gain, w_qkv):
    count, width = own.shape
    out = w_qkv.shape[2]
    return pl.pallas_call(
        project_kernel,
        out_shape=[
            jax.ShapeDtypeStruct((width, 2 * count), BF16),
            jax.ShapeDtypeStruct((3, 2 * count, out), BF16),
        ],
        cost_estimate=cost(12 * count * width * out, 8 * count * width),
        name="project",
    )(own, other, gain[None], w_qkv)


def key_constants(live, same):
    length = live.shape[0]
    first = jnp.arange(length) < length // 2
    for_own = jnp.where(live & (first | same), 0.0, NEGATIVE)
    for_other = jnp.where(live & (~first | same), 0.0, NEGATIVE)
    lane = jnp.arange(LANES) % DH
    ones = jnp.where((lane >= 2) & (lane < 5), 1.0, 0.0)
    keys = jnp.where(lane == 0, for_own[:, None], jnp.where(lane == 1, for_other[:, None], ones))
    queries = ((lane == 0) & first[:, None]) | ((lane == 1) & ~first[:, None])
    return keys.astype(BF16), queries.astype(BF16)


def attention_kernel(qkv_ref, keys_ref, queries_ref, own_ref, other_ref, kept_ref, held, *, block):
    lane = lax.broadcasted_iota(jnp.int32, (1, LANES), 1)
    lows = (lane < DH, lane >= DH)
    for head in range(2):
        held[head] = jnp.where(lows[head], qkv_ref[1], keys_ref[...])
        held[2 + head] = jnp.where(lows[head], qkv_ref[2], jnp.ones((1, LANES), BF16))
    half = own_ref.shape[0]
    for part, out_ref in enumerate((own_ref, other_ref)):

        def step(i, carry, part=part, out_ref=out_ref):
            inside = pl.ds(pl.multiple_of(i * block, block), block)
            rows = pl.ds(pl.multiple_of(part * half + i * block, block), block)
            queries = qkv_ref[0, rows, :] * jnp.asarray(1.0 / math.sqrt(DH), BF16)
            constants = queries_ref[rows, :]
            results = []
            for head in range(2):
                scores = mm_nt(jnp.where(lows[head], queries, constants), held[head])
                highest = jnp.max(scores, axis=1, keepdims=True)
                weights = jnp.exp(scores - highest).astype(BF16)
                mixed = mm(weights, held[2 + head])
                results.append(mixed / pltpu.roll(mixed, DH, 1))
                high, middle, low = three_terms(highest + jnp.log(mixed))
                base = DH * (1 - head)
                constants_back = jnp.where(
                    lane == base + 2,
                    -high,
                    jnp.where(lane == base + 3, -middle, jnp.where(lane == base + 4, -low, constants)),
                )
                kept_ref[head, rows, :] = jnp.where(lows[head], queries, constants_back)
            out_ref[inside, :] = jnp.where(lows[0], results[0], results[1]).astype(BF16)
            return carry

        lax.fori_loop(0, half // block, step, 0)


def attention(qkv, keys, queries, block=512):
    length, width = qkv.shape[1:]
    pairs, half = width // LANES, length // 2
    return pl.pallas_call(
        functools.partial(attention_kernel, block=block),
        grid=(pairs,),
        in_specs=[
            pl.BlockSpec((3, length, LANES), lambda p: (0, 0, p)),
            whole((length, LANES)),
            whole((length, LANES)),
        ],
        out_specs=[
            pl.BlockSpec((half, LANES), lambda p: (0, p)),
            pl.BlockSpec((half, LANES), lambda p: (0, p)),
            pl.BlockSpec((2, length, LANES), lambda p: (p, 0, 0)),
        ],
        out_shape=[
            jax.ShapeDtypeStruct((half, width), BF16),
            jax.ShapeDtypeStruct((half, width), BF16),
            jax.ShapeDtypeStruct((2 * pairs, length, LANES), BF16),
        ],
        scratch_shapes=[pltpu.VMEM((4, length, LANES), BF16)],
        cost_estimate=cost(16 * pairs * length * length * LANES, 10 * length * width),
        name="attention",
    )(qkv, keys, queries)


def middle_kernel(first, rows_each, *refs):
    refs = list(refs)
    table_ref = refs.pop(0)
    if first:
        (tokens_ref, own_ref, recv_ref, w_own_ref, w_recv_ref) = refs[:5]
        (gain_ref, cot_ref, live_ref, gu_ref, down_ref, middle_ref, total_ref, back_ref, part_ref) = refs[5:14]
        (normed, normed_t, seed, seed_t, held) = refs[14:]
    else:
        (middle_ref, total_in, back_in, gain_ref, cot_ref, live_ref, gu_ref, down_ref) = refs[:8]
        (out_ref, grad_ref, attn_seed_ref, gain_part_ref, part_ref) = refs[8:13]
        (normed, normed_t, seed, seed_t, held, total_ref, back_ref) = refs[13:]
    step = pl.program_id(0)

    @pl.when(step == 0)
    def _():
        if first:
            middle = tokens_ref[...].astype(F32) + (
                mm(own_ref[...], w_own_ref[...]) + mm(recv_ref[...], w_recv_ref[...])
            )
            middle_ref[...] = middle
            total_ref[...] = middle
            back_ref[...] = jnp.zeros_like(back_ref)
        else:
            middle = middle_ref[...]
            total_ref[...] = total_in[...]
            back_ref[...] = back_in[...]
        value = (middle * inverse_rms(middle) * gain_ref[...]).astype(BF16)
        normed[...] = value
        normed_t[...] = value.T
        seed_value = (cot_ref[...].astype(F32) * live_ref[...]).astype(BF16)
        seed[...] = seed_value
        seed_t[...] = seed_value.T

    gate = mm(normed[...], gu_ref[0])
    up = mm(normed[...], gu_ref[1])
    bent = jnp.tanh(ROOT * (gate + CUBE * gate * gate * gate))
    soft = 0.5 * gate * (1.0 + bent)
    slope = 0.5 * (1.0 + bent) + 0.5 * gate * (1.0 - bent * bent) * (ROOT * (1.0 + 3.0 * CUBE * gate * gate))
    hidden = (soft * up).astype(BF16)
    hidden_grad = mm_nt(seed[...], down_ref[...])
    gate_grad = (hidden_grad * up * slope).astype(BF16)
    up_grad = (hidden_grad * soft).astype(BF16)
    total_ref[...] += mm(hidden, down_ref[...])
    back_ref[...] += mm_nt(gate_grad, gu_ref[0]) + mm_nt(up_grad, gu_ref[1])
    chunk = gate.shape[1]
    held[:, 0:chunk] = mm(normed_t[...], gate_grad)
    held[:, chunk : 2 * chunk] = mm(normed_t[...], up_grad)
    held[:, 2 * chunk : 3 * chunk] = mm(seed_t[...], hidden)
    write_slots(table_ref, held, [part_ref], slice(None), rows_each)

    if not first:

        @pl.when(step == pl.num_programs(0) - 1)
        def _():
            out_ref[...] = total_ref[...].astype(BF16)
            middle = middle_ref[...]
            factor = inverse_rms(middle)
            back = back_ref[...]
            scaled = back * gain_ref[...]
            inner = jnp.mean(scaled * middle, axis=-1, keepdims=True)
            grad = (
                cot_ref[...].astype(F32) * live_ref[...]
                + factor * scaled
                - middle * (factor * factor * factor * inner)
            )
            grad_ref[...] = grad
            attn_seed_ref[...] = grad.astype(BF16)
            gain_part_ref[...] = jnp.sum(back * middle * factor, axis=0, keepdims=True)


def middle_call(first, inputs, gain, cot, live, w_gu, w_down, table, n_wide, chunk=256):
    count, width = cot.shape
    units = w_down.shape[0]
    rows_each = width // n_wide
    steps = units // chunk
    tall = rows_each % 16 == 0
    rows = (count, width)
    if tall:
        part_spec = pl.BlockSpec((n_wide, rows_each, 3 * chunk), lambda j, *_: (0, 0, j))
        part_shape = jax.ShapeDtypeStruct((n_wide, rows_each, 3 * units), BF16)
    else:
        part_spec = pl.BlockSpec((width, 3 * chunk), lambda j, *_: (0, j))
        part_shape = jax.ShapeDtypeStruct((width, 3 * units), BF16)
    in_specs = [whole(v.shape) for v in inputs] + [
        whole((1, width)),
        whole(rows),
        whole((count, 1)),
        pl.BlockSpec((2, width, chunk), lambda j, *_: (0, 0, j)),
        pl.BlockSpec((chunk, width), lambda j, *_: (j, 0)),
    ]
    scratch = [
        pltpu.VMEM(rows, BF16),
        pltpu.VMEM((width, count), BF16),
        pltpu.VMEM(rows, BF16),
        pltpu.VMEM((width, count), BF16),
        pltpu.VMEM((width, 3 * chunk), F32),
    ]
    if first:
        out_specs = [whole(rows)] * 3
        out_shape = [jax.ShapeDtypeStruct(rows, F32)] * 3
    else:
        out_specs = [whole(rows), whole(rows), whole(rows), whole((1, width))]
        out_shape = [
            jax.ShapeDtypeStruct(rows, BF16),
            jax.ShapeDtypeStruct(rows, F32),
            jax.ShapeDtypeStruct(rows, BF16),
            jax.ShapeDtypeStruct((1, width), F32),
        ]
        scratch += [pltpu.VMEM(rows, F32)] * 2
    outs = pl.pallas_call(
        functools.partial(middle_kernel, first, rows_each),
        grid_spec=pltpu.PrefetchScalarGridSpec(
            num_scalar_prefetch=1,
            grid=(steps,),
            in_specs=in_specs,
            out_specs=out_specs + [part_spec],
            scratch_shapes=scratch,
        ),
        out_shape=out_shape + [part_shape],
        cost_estimate=cost(18 * count * width * units, 16 * width * units),
        name="middle_first" if first else "middle_last",
    )(table, *inputs, gain[None], cot, live, w_gu, w_down)
    return outs[:-1], in_slots(outs[-1], table, n_wide)


def in_slots(part, table, n_wide):
    if part.ndim == 3:
        return part
    return jnp.take(part.reshape(n_wide, -1, part.shape[-1]), table, axis=0)


def seeds_kernel(own_ref, other_ref, w_ref, grad_ref, seed_t_ref):
    count = own_ref.shape[0]
    for half, seed_ref in enumerate((own_ref, other_ref)):
        at = slice(half * count, (half + 1) * count)
        grad_ref[at, :] = mm_nt(seed_ref[...], w_ref[...]).astype(BF16)
        seed_t_ref[:, at] = seed_ref[...].T


def seeds_call(own, other, w_out):
    count, width = own.shape
    out = w_out.shape[0]
    return pl.pallas_call(
        seeds_kernel,
        out_shape=[
            jax.ShapeDtypeStruct((2 * count, out), BF16),
            jax.ShapeDtypeStruct((width, 2 * count), BF16),
        ],
        cost_estimate=cost(4 * count * width * out, 8 * count * width),
        name="seeds",
    )(own, other, w_out)


def attention_back_kernel(last, block, rows_each, split, *refs):
    refs = list(refs)
    table_ref = refs.pop(0)
    (qkv_ref, grad_ref, mixed_own_ref, mixed_other_ref, kept_ref, keys_ref) = refs[:6]
    (normed_t_ref, seed_t_ref, w_ref) = refs[6:9]
    refs = refs[9:]
    carried_ref = refs.pop(0) if last else None
    part_refs = [refs.pop(0) for _ in range(split)]
    back_refs = [refs.pop(0) for _ in range(2 if last else 1)]
    grads, queries, query_total, pieces, mixed, held, total = refs
    lane = lax.broadcasted_iota(jnp.int32, (1, LANES), 1)
    lows = (lane < DH, lane >= DH)
    nothing = jnp.zeros((1, LANES), BF16)
    length = grad_ref.shape[0]
    half = length // 2
    mixed[0:half, :] = mixed_own_ref[...]
    mixed[half:length, :] = mixed_other_ref[...]
    product = grad_ref[...].astype(F32) * mixed[...].astype(F32)
    for head in range(2):
        base = DH * (1 - head)
        dots = jnp.sum(jnp.where(lows[head], product, 0.0), axis=1, keepdims=True)
        high, middle, low = three_terms(dots)
        constants = jnp.where(
            lane == base + 2,
            -high,
            jnp.where(lane == base + 3, -middle, jnp.where(lane == base + 4, -low, nothing)),
        )
        grads[head] = jnp.where(lows[head], grad_ref[...], constants)
        grads[2 + head] = jnp.where(lows[head], grad_ref[...], nothing)
        queries[head] = jnp.where(lows[head], kept_ref[head], nothing)
    query_total[...] = jnp.zeros_like(query_total)

    def step(i, carry):
        rows = pl.ds(pl.multiple_of(i * block, block), block)
        keys, values, constants = qkv_ref[1, rows, :], qkv_ref[2, rows, :], keys_ref[rows, :]
        key_grad, value_grad = [], []
        for head in range(2):
            base = DH * (1 - head)
            ones = jnp.where((lane >= base + 2) & (lane < base + 5), 1.0, 0.0).astype(BF16)
            keys_only = jnp.where(lows[head], keys, nothing) * jnp.asarray(1.0 / math.sqrt(DH), BF16)
            weights = jnp.exp(mm_nt(jnp.where(lows[head], keys, constants), kept_ref[head]))
            score_grads = weights * mm_nt(jnp.where(lows[head], values, ones), grads[head])
            score_grads = score_grads.astype(BF16)
            value_grad.append(mm(weights.astype(BF16), grads[2 + head]))
            key_grad.append(mm(score_grads, queries[head]))
            query_total[...] += mm(keys_only.T, score_grads)
        pieces[rows, LANES : 2 * LANES] = (key_grad[0] + key_grad[1]).astype(BF16)
        pieces[rows, 2 * LANES : 3 * LANES] = (value_grad[0] + value_grad[1]).astype(BF16)
        return carry

    lax.fori_loop(0, length // block, step, 0)
    pieces[:, 0:LANES] = query_total[...].T.astype(BF16)
    held[:, 0 : 3 * LANES] = mm(normed_t_ref[...], pieces[...])
    held[:, 3 * LANES : 4 * LANES] = mm(seed_t_ref[...], mixed[...])
    write_slots(table_ref, held, part_refs, slice(None), rows_each)
    back = sum(mm_nt(pieces[:, i * LANES : (i + 1) * LANES], w_ref[i]) for i in range(3))
    pair = pl.program_id(0)

    @pl.when(pair == 0)
    def _():
        total[...] = back + carried_ref[...] if last else back

    @pl.when(pair > 0)
    def _():
        total[...] += back

    @pl.when(pair == pl.num_programs(0) - 1)
    def _():
        if last:
            back_refs[0][...] = total[0:half, :]
            back_refs[1][...] = total[half:length, :].astype(BF16)
        else:
            back_refs[0][...] = total[...]


def attention_back(first, count, last, qkv, grad, mixed_own, mixed_other, kept, keys, normed_t, seed_t, w_qkv, carried, table, n_wide, block=512):
    length = qkv.shape[1]
    half = length // 2
    width = normed_t.shape[0]
    rows_each = width // n_wide
    tall = rows_each % 16 == 0
    columns = 4 * LANES
    if tall:
        part_specs = [pl.BlockSpec((n_wide // 2, rows_each, columns), lambda p, *_: (0, 0, p))] * 2
        part_shapes = [jax.ShapeDtypeStruct((n_wide // 2, rows_each, count * columns), BF16)] * 2
    else:
        part_specs = [pl.BlockSpec((width, columns), lambda p, *_: (0, p))]
        part_shapes = [jax.ShapeDtypeStruct((width, count * columns), BF16)]
    in_specs = [
        pl.BlockSpec((3, length, LANES), lambda p, *_: (0, 0, p + first)),
        pl.BlockSpec((length, LANES), lambda p, *_: (0, p + first)),
        pl.BlockSpec((half, LANES), lambda p, *_: (0, p + first)),
        pl.BlockSpec((half, LANES), lambda p, *_: (0, p + first)),
        pl.BlockSpec((2, length, LANES), lambda p, *_: (p + first, 0, 0)),
        whole((length, LANES)),
        whole((width, length)),
        whole((width, length)),
        pl.BlockSpec((3, width, LANES), lambda p, *_: (0, 0, p + first)),
    ]
    inputs = [qkv, grad, mixed_own, mixed_other, kept, keys, normed_t, seed_t, w_qkv]
    if last:
        in_specs.append(whole((length, width)))
        inputs.append(carried)
        back_specs = [whole((half, width))] * 2
        back_shapes = [jax.ShapeDtypeStruct((half, width), F32), jax.ShapeDtypeStruct((half, width), BF16)]
    else:
        back_specs = [whole((length, width))]
        back_shapes = [jax.ShapeDtypeStruct((length, width), F32)]
    outs = pl.pallas_call(
        functools.partial(attention_back_kernel, last, block, rows_each, len(part_specs)),
        grid_spec=pltpu.PrefetchScalarGridSpec(
            num_scalar_prefetch=1,
            grid=(count,),
            in_specs=in_specs,
            out_specs=part_specs + back_specs,
            scratch_shapes=[
                pltpu.VMEM((4, length, LANES), BF16),
                pltpu.VMEM((2, length, LANES), BF16),
                pltpu.VMEM((LANES, length), F32),
                pltpu.VMEM((length, 3 * LANES), BF16),
                pltpu.VMEM((length, LANES), BF16),
                pltpu.VMEM((width, columns), F32),
                pltpu.VMEM((length, width), F32),
            ],
        ),
        out_shape=part_shapes + back_shapes,
        cost_estimate=cost(count * 50 * length * length * LANES, count * 16 * length * LANES),
        name="attention_back",
    )(table, *inputs)
    parts, backs = outs[: len(part_specs)], outs[len(part_specs) :]
    if not tall:
        slots = in_slots(parts[0], table, n_wide)
        parts = [slots[: n_wide // 2], slots[n_wide // 2 :]]
    return parts, backs


def added(arrays, low, high):
    return sum(a[low:high].astype(F32) for a in arrays)


def scatter(pieces, send, n_wide):
    slots = n_wide // 2
    stage = 0
    while True:
        pieces = pieces + [stage_exchange(send, stage, n_wide)]
        stage += 1
        if slots == 1:
            return pieces
        slots //= 2
        send = added(pieces, slots, 2 * slots).astype(BF16)


def input_grad_kernel(own_ref, recv_ref, tokens_ref, gain_ref, middle_grad_ref, out_ref, part_ref):
    back = own_ref[...] + recv_ref[...].astype(F32)
    rows = tokens_ref[...].astype(F32)
    factor = inverse_rms(rows)
    scaled = back * gain_ref[...]
    inner = jnp.mean(scaled * rows, axis=-1, keepdims=True)
    out_ref[...] = middle_grad_ref[...] + factor * scaled - rows * (factor * factor * factor * inner)
    part_ref[...] = jnp.sum(back * rows * factor, axis=0, keepdims=True)


def input_grad(own, recv, tokens, gain, middle_grad):
    count, width = tokens.shape
    return pl.pallas_call(
        input_grad_kernel,
        out_shape=[jax.ShapeDtypeStruct((count, width), F32), jax.ShapeDtypeStruct((1, width), F32)],
        cost_estimate=cost(20 * count * width, 18 * count * width),
        name="input_grad",
    )(own, recv, tokens, gain[None], middle_grad)


def gather_kernel(counts, chunk, *refs):
    refs = list(refs)
    groups = [[refs.pop(0) for _ in range(count)] for count in counts]
    qkv_ref, out_ref, gu_ref, down_ref, columns_ref, rows_ref, turned = refs
    sums = []
    for group in groups:
        total = group[0][0].astype(F32)
        for ref in group[1:]:
            total = total + ref[0].astype(F32)
        sums.append(total)
    wide_part, pair_parts = sums[0], sums[1:]
    pairs = [part[:, i : i + 4 * LANES] for part in pair_parts for i in range(0, part.shape[1], 4 * LANES)]
    mats = [
        jnp.concatenate([pair[:, i * LANES : (i + 1) * LANES] for pair in pairs], axis=1) for i in range(4)
    ]
    kinds = [
        jnp.concatenate(
            [
                wide_part[:, j + i * chunk : j + (i + 1) * chunk]
                for j in range(0, wide_part.shape[1], 3 * chunk)
            ],
            axis=1,
        )
        for i in range(3)
    ]
    rows = wide_part.shape[0]
    for i in range(3):
        qkv_ref[i] = mats[i]
    for i in range(2):
        gu_ref[i] = kinds[i]
    for value, ref in ((mats[3], out_ref), (kinds[2], down_ref)):
        count = value.shape[1]
        turned[0:rows, 0:count] = value
        ref[...] = turned[:, 0:count].T[:, 0:rows]
    columns_ref[...] = jnp.zeros_like(columns_ref)
    rows_ref[...] = jnp.zeros_like(rows_ref)
    lane = lax.broadcasted_iota(jnp.int32, (1, LANES), 1)
    row_sums = jnp.zeros((rows, LANES), F32)
    for i, value in enumerate((mats[0], mats[1], mats[2], mats[3], kinds[0], kinds[1], kinds[2])):
        squares = value * value
        columns_ref[i : i + 1, 0 : value.shape[1]] = jnp.sum(squares, axis=0, keepdims=True)
        row_sums = jnp.where(lane == i, jnp.sum(squares, axis=1, keepdims=True), row_sums)
    rows_ref[0:rows, :] = row_sums


def gather_own(groups, heads_width, units, chunk):
    rows = groups[0][0].shape[1]
    inputs = [a for group in groups for a in group]
    widest = max(heads_width, units)
    shapes = [(3, rows, heads_width), (heads_width, rows), (2, rows, units), (units, rows), (8, widest)]
    shapes.append((max(8, -(-rows // 8) * 8), LANES))
    return pl.pallas_call(
        functools.partial(gather_kernel, [len(g) for g in groups], chunk),
        grid=(1,),
        in_specs=[pl.BlockSpec((1,) + a.shape[1:], lambda *_: (0, 0, 0)) for a in inputs],
        out_specs=[whole(s) for s in shapes],
        out_shape=[jax.ShapeDtypeStruct(s, F32) for s in shapes],
        scratch_shapes=[pltpu.VMEM((LANES, widest), F32)],
        cost_estimate=cost(1 << 20, 4 << 20),
        name="gather_own",
    )(*inputs)


def update_kernel(sizes, *refs):
    (scalar_ref, qkv_ref, out_ref, gu_ref, down_ref, columns_ref, rows_ref, prior_rows_ref) = refs[:8]
    (qkv_cols, out_rows, gu_cols, down_rows, w_qkv, w_out, w_gu, w_down) = refs[8:16]
    (qkv_new, out_new, gu_new, down_new, qkv_cols_new, out_rows_new, gu_cols_new, down_rows_new, rows_new_ref) = refs[16:25]
    (turned,) = refs[25:]
    beta = scalar_ref[0]
    fresh = 1.0 - beta
    rows = qkv_ref.shape[1]
    lane = lax.broadcasted_iota(jnp.int32, (1, LANES), 1)
    all_rows = jnp.zeros((rows, LANES), F32)
    width = sizes[0]
    priors = [qkv_cols[0:1], qkv_cols[1:2], qkv_cols[2:3], out_rows[...], gu_cols[0:1], gu_cols[1:2], down_rows[...]]
    for i in range(7):
        across = sizes[1 + i]
        row_new = beta * prior_rows_ref[0:rows, i : i + 1] + fresh * (rows_ref[0:rows, i : i + 1] / across + TINIEST)
        count = priors[i].shape[1]
        col_new = beta * priors[i] + fresh * (columns_ref[i : i + 1, 0:count] / width + TINIEST)
        all_rows = jnp.where(lane == i, row_new, all_rows)
        mean, rate = scalar_ref[1 + i], scalar_ref[8 + i]
        if i in (3, 6):
            turned[0:rows, :] = jnp.broadcast_to(row_new, (rows, LANES))
            row_line = turned[...].T[0:1, 0:rows]
            gradient_ref, weight_ref, new_ref = ((out_ref, w_out, out_new), (down_ref, w_down, down_new))[i == 6]
            column = jnp.broadcast_to(col_new, (LANES, count)).T[:, 0:1]
            step = gradient_ref[...] * lax.rsqrt(row_line * column / mean)
            new_ref[...] = (weight_ref[...].astype(F32) - rate * step).astype(BF16)
            (out_rows_new, down_rows_new)[i == 6][...] = col_new
        else:
            at = i if i < 3 else i - 4
            gradient_ref, weight_ref, new_ref = (qkv_ref, w_qkv, qkv_new) if i < 3 else (gu_ref, w_gu, gu_new)
            step = gradient_ref[at] * lax.rsqrt(row_new * col_new / mean)
            new_ref[at] = (weight_ref[at].astype(F32) - rate * step).astype(BF16)
            (qkv_cols_new if i < 3 else gu_cols_new)[at : at + 1] = col_new
    turned[0:rows, :] = all_rows
    rows_new_ref[...] = turned[...].T[0:8, 0:rows]


def update(scalars, grads, columns, rows_sq, prior_rows, col_priors, weights, sizes):
    rows = grads[0].shape[1]
    new_shapes = [jax.ShapeDtypeStruct(w.shape, BF16) for w in weights]
    col_shapes = [jax.ShapeDtypeStruct(c.shape, F32) for c in col_priors]
    inputs = [*grads, columns, rows_sq, prior_rows, *col_priors, *weights]
    out_shape = new_shapes + col_shapes + [jax.ShapeDtypeStruct((8, rows), F32)]
    return pl.pallas_call(
        functools.partial(update_kernel, sizes),
        grid_spec=pltpu.PrefetchScalarGridSpec(
            num_scalar_prefetch=1,
            grid=(1,),
            in_specs=[whole(a.shape) for a in inputs],
            out_specs=[whole(s.shape) for s in out_shape],
            scratch_shapes=[pltpu.VMEM((LANES, LANES), F32)],
        ),
        out_shape=out_shape,
        cost_estimate=cost(1 << 20, 4 << 20),
        name="update",
    )(scalars, *inputs)


def square_sum(values):
    wide = values.astype(F32)
    return jnp.sum(wide * wide, axis=(-2, -1))


def body(
    n_wide,
    tokens,
    plot_slot,
    patch_mask,
    cotangent,
    gain_attn,
    w_qkv,
    w_out,
    gain_mlp,
    w_gu,
    w_down,
    qkv_rows,
    qkv_cols,
    out_rows,
    out_cols,
    gu_rows,
    gu_cols,
    down_rows,
    down_cols,
    step_count,
    learn_rate,
):
    count, width = tokens.shape
    heads_width, units = w_out.shape[0], w_down.shape[0]
    rows_each = width // n_wide
    chunk = 256
    core = lax.axis_index("narrow")
    wide = lax.axis_index("wide")
    tables = [slot_table(wide, order, n_wide) for order in bit_orders(n_wide)]
    own_table = jnp.where(core == 0, tables[0], tables[1])
    other_table = jnp.where(core == 0, tables[1], tables[0])

    tokens_other = swap(tokens)
    own_live = lax.dynamic_slice_in_dim(patch_mask, core * count, count, 0)
    other_live = lax.dynamic_slice_in_dim(patch_mask, (1 - core) * count, count, 0)
    same = plot_slot[0] == plot_slot[2 * count - 1]
    key_const, query_const = key_constants(jnp.concatenate([own_live, other_live]) > 0, same)
    live = own_live.astype(F32)[:, None]

    normed_t, qkv = project(tokens, tokens_other, gain_attn, w_qkv)
    w_out_other, w_gu_other, w_down_other = swap(w_out), swap(w_gu), swap(w_down)
    mixed_own, mixed_other, kept = attention(qkv, key_const, query_const)
    mixed_recv = swap(mixed_other)
    (middle, total, back), part_other = middle_call(
        True,
        [tokens, mixed_own, mixed_recv, w_out, w_out_other],
        gain_mlp,
        cotangent,
        live,
        w_gu_other,
        w_down_other,
        other_table,
        n_wide,
        chunk,
    )
    part_recv = swap(part_other)
    (mixed_out, middle_grad, attn_seed, mlp_gain_part), part_own = middle_call(
        False, [middle, total, back], gain_mlp, cotangent, live, w_gu, w_down, own_table, n_wide, chunk
    )
    seed_other = swap(attn_seed)
    half = n_wide // 2
    mlp_pieces = [part_own, part_recv]
    mlp_pieces = scatter(mlp_pieces, added(mlp_pieces, half, n_wide).astype(BF16), n_wide)

    mixed_grad, seed_t = seeds_call(attn_seed, seed_other, w_out)
    pairs = heads_width // LANES
    back_args = (qkv, mixed_grad, mixed_own, mixed_other, kept, key_const, normed_t, seed_t, w_qkv)
    (keep, send), (carried,) = attention_back(0, pairs - 1, False, *back_args, None, own_table, n_wide)
    first_pieces = scatter([keep], send, n_wide)
    (keep, send), (back_own, back_other) = attention_back(
        pairs - 1, 1, True, *back_args, carried, own_table, n_wide
    )
    last_pieces = scatter([keep], send, n_wide)
    tokens_grad, attn_gain_part = input_grad(back_own, swap(back_other), tokens, gain_attn, middle_grad)

    *grads, columns, rows_sq = gather_own([mlp_pieces, first_pieces, last_pieces], heads_width, units, chunk)
    qkv_grad, out_grad, gu_grad, down_grad = grads

    weight_sq = jnp.concatenate(
        [square_sum(w_qkv), square_sum(w_out)[None], square_sum(w_gu), square_sum(w_down)[None]]
    )
    prior_sums = jnp.stack([jnp.sum(out_rows), jnp.sum(down_rows)])
    widest = columns.shape[1]
    small = jnp.concatenate(
        [
            jnp.pad(attn_gain_part, ((0, 0), (0, widest - width))),
            jnp.pad(mlp_gain_part, ((0, 0), (0, widest - width))),
            jnp.pad(jnp.concatenate([weight_sq, prior_sums])[None], ((0, 0), (0, widest - 9))),
            jnp.zeros((5, widest), F32),
        ]
    )
    rows_sq, small = (lambda pair: (rows_sq + pair[0], small + pair[1]))((swap(rows_sq), swap(small)))
    totals = jnp.sum(rows_sq, axis=0)[:8]
    summed = jnp.concatenate(
        [columns[:7], jnp.pad(totals[None], ((0, 0), (0, widest - 8))), small[:2]], axis=0
    )
    for stage in range(n_wide.bit_length() - 1):
        summed = summed + stage_exchange(summed, stage, n_wide)
    columns, totals = summed[:8], summed[7, :7]
    gains = lax.dynamic_slice_in_dim(summed[8:10, :width], wide * rows_each, rows_each, 1)
    weight_sq, prior_sums = small[2, :7], small[2, 7:9]

    beta = 1.0 - lax.rsqrt(step_count.astype(F32))
    fresh = 1.0 - beta
    across = [2 * heads_width] * 4 + [2 * units] * 3
    entries = jnp.asarray([width * a for a in across], F32)
    own_prior = jnp.concatenate(
        [
            jnp.mean(qkv_rows, axis=1),
            prior_sums[:1] / (2 * heads_width),
            jnp.mean(gu_rows, axis=1),
            prior_sums[1:] / (2 * units),
        ]
    )
    means = beta * own_prior + fresh * (totals / entries + TINIEST)
    rates = learn_rate * jnp.sqrt(jnp.concatenate([weight_sq[:7]]) / entries)
    scalars = jnp.concatenate([beta[None], means, rates])

    def own_rows(values, dimension):
        return lax.dynamic_slice_in_dim(values, wide * rows_each, rows_each, dimension)

    prior_rows = jnp.concatenate([qkv_rows, out_cols[None], gu_rows, down_cols[None]], axis=0)
    prior_rows = own_rows(prior_rows, 1).T
    outs = update(
        scalars,
        grads,
        columns,
        rows_sq,
        prior_rows,
        [qkv_cols, out_rows[None], gu_cols, down_rows[None]],
        [own_rows(w_qkv, 1), own_rows(w_out, 1), own_rows(w_gu, 1), own_rows(w_down, 1)],
        [width, *across],
    )
    qkv_new, out_new, gu_new, down_new, qkv_cols_new, out_rows_new, gu_cols_new, down_rows_new, rows_new = outs
    return (
        mixed_out,
        tokens_grad,
        gains[0],
        qkv_grad,
        out_grad,
        gains[1],
        gu_grad,
        down_grad,
        qkv_new,
        out_new,
        gu_new,
        down_new,
        rows_new[0:3],
        qkv_cols_new,
        out_rows_new[0],
        rows_new[3],
        rows_new[4:6],
        gu_cols_new,
        down_rows_new[0],
        rows_new[6],
    )


def solution(mesh):
    in_specs = (
        P(("wide", "narrow"), None),
        P("wide"),
        P("wide"),
        P(("wide", "narrow"), None),
        P(),
        P(None, None, "narrow"),
        P("narrow", None),
        P(),
        P(None, None, "narrow"),
        P("narrow", None),
        P(),
        P(None, "narrow"),
        P("narrow"),
        P(),
        P(),
        P(None, "narrow"),
        P("narrow"),
        P(),
        P(),
        P(),
    )
    out_specs = (
        P(("wide", "narrow"), None),
        P(("wide", "narrow"), None),
        P("wide"),
        P(None, "wide", "narrow"),
        P("narrow", "wide"),
        P("wide"),
        P(None, "wide", "narrow"),
        P("narrow", "wide"),
        P(None, "wide", "narrow"),
        P("narrow", "wide"),
        P(None, "wide", "narrow"),
        P("narrow", "wide"),
        P(None, "wide"),
        P(None, "narrow"),
        P("narrow"),
        P("wide"),
        P(None, "wide"),
        P(None, "narrow"),
        P("narrow"),
        P("wide"),
    )
    return jax.shard_map(
        functools.partial(body, mesh.shape["wide"]),
        mesh=mesh,
        in_specs=in_specs,
        out_specs=out_specs,
        check_vma=False,
    )
```

```python
import functools
import math

import jax
import jax.numpy as jnp
from jax import lax
from jax.experimental import pallas as pl
from jax.experimental.pallas import tpu as pltpu
from jax.sharding import PartitionSpec as P

DH = 64
LANES = 128
EPSILON = 1e-06
TINIEST = 1e-30
NEGATIVE = -1e30
F32 = jnp.float32
BF16 = jnp.bfloat16
ROOT = math.sqrt(2.0 / math.pi)
CUBE = 0.044715
MIB = 1024 * 1024


def mm(a, b):
    return jnp.dot(a, b, preferred_element_type=F32)


def mm_nt(a, b):
    return lax.dot_general(a, b, (((1,), (1,)), ((), ())), preferred_element_type=F32)


def whole(shape):
    return pl.BlockSpec(shape, lambda *_: (0,) * len(shape))


def cost(flops, nbytes):
    return pl.CostEstimate(flops=int(flops), bytes_accessed=int(nbytes), transcendentals=0)


def inverse_rms(rows):
    return lax.rsqrt(jnp.mean(rows * rows, axis=-1, keepdims=True) + EPSILON)


def three_terms(values):
    high = values.astype(BF16)
    rest = values - high.astype(F32)
    middle = rest.astype(BF16)
    return high, middle, (rest - middle.astype(F32)).astype(BF16)


def bit_orders(n_wide):
    bits = n_wide.bit_length() - 1
    straight = list(range(bits))
    turned = straight[1:-1] + straight[:1] + straight[-1:] if bits > 2 else straight
    return straight, turned


def slot_table(wide_index, order, n_wide):
    bits = len(order)
    entries = []
    for slot in range(n_wide):
        mask = 0
        for stage, bit in enumerate(order):
            if slot >> (bits - 1 - stage) & 1:
                mask |= 1 << bit
        entries.append(mask)
    return jnp.bitwise_xor(jnp.asarray(entries, jnp.int32), wide_index.astype(jnp.int32))


def stage_exchange(values, stage, n_wide):
    orders = bit_orders(n_wide)
    pairs = []
    for wide in range(n_wide):
        for core in range(2):
            pairs.append((wide * 2 + core, (wide ^ (1 << orders[core][stage])) * 2 + core))
    return lax.ppermute(values, ("wide", "narrow"), pairs)


def swap(values):
    return lax.ppermute(values, "narrow", [(0, 1), (1, 0)])


def write_slots(table_ref, held_ref, targets, rows_each, more_ref=None):
    if targets[0].ndim == 2:
        more = 0.0 if more_ref is None else more_ref[...].astype(F32)
        targets[0][...] = (held_ref[...] + more).astype(BF16)
        return
    slot = 0
    for target in targets:
        for at in range(target.shape[0]):
            start = pl.multiple_of(table_ref[slot] * rows_each, 16)
            value = held_ref[pl.ds(start, rows_each), :]
            if more_ref is not None:
                value = value + more_ref[slot].astype(F32)
            target[at] = value.astype(BF16)
            slot += 1


def project_kernel(own_ref, other_ref, gain_ref, w_ref, normed_t_ref, projected_ref):
    count = own_ref.shape[0]
    for half, rows_ref in enumerate((own_ref, other_ref)):
        rows = rows_ref[...].astype(F32)
        normed = (rows * inverse_rms(rows) * gain_ref[...]).astype(BF16)
        at = slice(half * count, (half + 1) * count)
        normed_t_ref[:, at] = normed.T
        for i in range(3):
            projected_ref[i, at, :] = mm(normed, w_ref[i]).astype(BF16)


def project(own, other, gain, w_qkv):
    count, width = own.shape
    out = w_qkv.shape[2]
    return pl.pallas_call(
        project_kernel,
        out_shape=[
            jax.ShapeDtypeStruct((width, 2 * count), BF16),
            jax.ShapeDtypeStruct((3, 2 * count, out), BF16),
        ],
        cost_estimate=cost(12 * count * width * out, 8 * count * width),
        compiler_params=pltpu.CompilerParams(vmem_limit_bytes=10 * MIB),
        name="project",
    )(own, other, gain[None], w_qkv)


def key_lines(plot_slot, patch_mask, core):
    length = plot_slot.shape[0]
    turned = lambda values: jnp.roll(values, length // 2)
    live = jnp.where(core == 0, patch_mask, turned(patch_mask)) > 0
    same = plot_slot == turned(plot_slot)
    same = jnp.where(core == 0, same, turned(same))
    first = jnp.arange(length) < length // 2
    for_own = jnp.where(live & (first | same), 0.0, NEGATIVE)
    for_other = jnp.where(live & (~first | same), 0.0, NEGATIVE)
    return jnp.stack([for_own, for_other, live.astype(F32)])


def column(line):
    return jnp.broadcast_to(line, (LANES, line.shape[1])).T


def attention_kernel(qkv_ref, lines_ref, own_ref, other_ref, kept_ref, keys_ref, held, *, block):
    lane = lax.broadcasted_iota(jnp.int32, (1, LANES), 1)
    lows = (lane < DH, lane >= DH)
    within = jnp.bitwise_and(lane, DH - 1)

    @pl.when(pl.program_id(0) == 0)
    def _():
        ones = jnp.where((within >= 2) & (within < 5), 1.0, 0.0)
        bias = jnp.where(within == 1, column(lines_ref[1:2, :]), ones)
        keys_ref[...] = jnp.where(within == 0, column(lines_ref[0:1, :]), bias).astype(BF16)

    for head in range(2):
        held[head] = jnp.where(lows[head], qkv_ref[1], keys_ref[...])
        held[2 + head] = jnp.where(lows[head], qkv_ref[2], jnp.ones((1, LANES), BF16))
    half = own_ref.shape[0]
    for part, out_ref in enumerate((own_ref, other_ref)):

        def step(i, carry, part=part, out_ref=out_ref):
            inside = pl.ds(pl.multiple_of(i * block, block), block)
            rows = pl.ds(pl.multiple_of(part * half + i * block, block), block)
            queries = qkv_ref[0, rows, :] * jnp.asarray(1.0 / math.sqrt(DH), BF16)
            constants = jnp.where(within == part, 1.0, 0.0).astype(BF16)
            results = []
            for head in range(2):
                scores = mm_nt(jnp.where(lows[head], queries, constants), held[head])
                highest = jnp.max(scores, axis=1, keepdims=True)
                weights = jnp.exp(scores - highest).astype(BF16)
                mixed = mm(weights, held[2 + head])
                results.append(mixed / pltpu.roll(mixed, DH, 1))
                high, middle, low = three_terms(highest + jnp.log(mixed))
                base = DH * (1 - head)
                constants_back = jnp.where(
                    lane == base + 2,
                    -high,
                    jnp.where(lane == base + 3, -middle, jnp.where(lane == base + 4, -low, constants)),
                )
                kept_ref[head, rows, :] = jnp.where(lows[head], queries, constants_back)
            out_ref[inside, :] = jnp.where(lows[0], results[0], results[1]).astype(BF16)
            return carry

        lax.fori_loop(0, half // block, step, 0)


def attention(qkv, lines, block=512):
    length, width = qkv.shape[1:]
    pairs, half = width // LANES, length // 2
    return pl.pallas_call(
        functools.partial(attention_kernel, block=block),
        grid=(pairs,),
        in_specs=[
            pl.BlockSpec((3, length, LANES), lambda p: (0, 0, p)),
            whole(lines.shape),
        ],
        out_specs=[
            pl.BlockSpec((half, LANES), lambda p: (0, p)),
            pl.BlockSpec((half, LANES), lambda p: (0, p)),
            pl.BlockSpec((2, length, LANES), lambda p: (p, 0, 0)),
            whole((length, LANES)),
        ],
        out_shape=[
            jax.ShapeDtypeStruct((half, width), BF16),
            jax.ShapeDtypeStruct((half, width), BF16),
            jax.ShapeDtypeStruct((2 * pairs, length, LANES), BF16),
            jax.ShapeDtypeStruct((length, LANES), BF16),
        ],
        scratch_shapes=[pltpu.VMEM((4, length, LANES), BF16)],
        cost_estimate=cost(16 * pairs * length * length * LANES, 10 * length * width),
        compiler_params=pltpu.CompilerParams(vmem_limit_bytes=14 * MIB),
        name="attention",
    )(qkv, lines)


def middle_kernel(first, last, rows_each, *refs):
    refs = list(refs)
    take = lambda n: [refs.pop(0) for _ in range(n)]
    (table_ref,) = take(1)
    if first:
        (tokens_ref, own_ref, recv_ref, w_own_ref, w_recv_ref, gain_ref, cot_ref, lines_ref) = take(8)
    else:
        (normed, normed_t, seed, seed_t, total_in, back_in) = take(6)
        if last:
            (middle_ref, gain_ref) = take(2)
    (gu_ref, down_ref) = take(2)
    part_in = None if last is None else take(1)[0]
    if first:
        (middle_ref, normed, normed_t, seed, seed_t) = take(5)
    if last:
        (out_ref, grad_ref, attn_seed_ref, gain_part_ref) = take(4)
    else:
        (total_ref, back_ref) = take(2)
    part_refs = take(len(refs) - (3 if last else 1))
    (held,) = take(1)
    if last:
        (total_ref, back_ref) = take(2)
    step = pl.program_id(0)

    @pl.when(step == 0)
    def _():
        if first:
            middle = tokens_ref[...].astype(F32) + (
                mm(own_ref[...], w_own_ref[...]) + mm(recv_ref[...], w_recv_ref[...])
            )
            middle_ref[...] = middle
            total_ref[...] = middle
            back_ref[...] = jnp.zeros_like(back_ref)
            count = cot_ref.shape[0]
            live = column(lines_ref[2:3, 0:count])[:, 0:1]
            seed_value = (cot_ref[...].astype(F32) * live).astype(BF16)
            seed[...] = seed_value
            seed_t[...] = seed_value.T
            value = (middle * inverse_rms(middle) * gain_ref[...]).astype(BF16)
            normed[...] = value
            normed_t[...] = value.T
        else:
            total_ref[...] = total_in[...]
            back_ref[...] = back_in[...]

    gate = mm(normed[...], gu_ref[0])
    up = mm(normed[...], gu_ref[1])
    bent = jnp.tanh(ROOT * (gate + CUBE * gate * gate * gate))
    soft = 0.5 * gate * (1.0 + bent)
    slope = 0.5 * (1.0 + bent) + 0.5 * gate * (1.0 - bent * bent) * (ROOT * (1.0 + 3.0 * CUBE * gate * gate))
    hidden = (soft * up).astype(BF16)
    hidden_grad = mm_nt(seed[...], down_ref[...])
    gate_grad = (hidden_grad * up * slope).astype(BF16)
    up_grad = (hidden_grad * soft).astype(BF16)
    total_ref[...] += mm(hidden, down_ref[...])
    back_ref[...] += mm_nt(gate_grad, gu_ref[0]) + mm_nt(up_grad, gu_ref[1])
    chunk = gate.shape[1]
    held[:, 0:chunk] = mm(normed_t[...], gate_grad)
    held[:, chunk : 2 * chunk] = mm(normed_t[...], up_grad)
    held[:, 2 * chunk : 3 * chunk] = mm(seed_t[...], hidden)
    write_slots(table_ref, held, part_refs, rows_each, part_in)

    if last:

        @pl.when(step == pl.num_programs(0) - 1)
        def _():
            out_ref[...] = total_ref[...].astype(BF16)
            middle = middle_ref[...]
            factor = inverse_rms(middle)
            back = back_ref[...]
            scaled = back * gain_ref[...]
            inner = jnp.mean(scaled * middle, axis=-1, keepdims=True)
            grad = seed[...].astype(F32) + factor * scaled - middle * (factor * factor * factor * inner)
            grad_ref[...] = grad
            attn_seed_ref[...] = grad.astype(BF16)
            gain_part_ref[...] = jnp.sum(back * middle * factor, axis=0, keepdims=True)


def middle_call(first, last, inputs, w_gu, w_down, at, steps, part_in, table, n_wide, chunk):
    count, width = inputs[0].shape
    rows_each = width // n_wide
    tall = rows_each % 16 == 0
    rows, turned = (count, width), (width, count)
    columns = 3 * chunk * steps
    if tall:
        slots = [n_wide] if last is None else [n_wide // 2] * 2
        part_specs = [pl.BlockSpec((n, rows_each, 3 * chunk), lambda j, *_: (0, 0, j)) for n in slots]
        part_shapes = [jax.ShapeDtypeStruct((n, rows_each, columns), BF16) for n in slots]
    else:
        part_specs = [pl.BlockSpec((width, 3 * chunk), lambda j, *_: (0, j))]
        part_shapes = [jax.ShapeDtypeStruct((width, columns), BF16)]
    in_specs = [whole(v.shape) for v in inputs] + [
        pl.BlockSpec((2, width, chunk), lambda j, *_: (0, 0, at + j)),
        pl.BlockSpec((chunk, width), lambda j, *_: (at + j, 0)),
    ]
    inputs = [*inputs, w_gu, w_down]
    if last is not None:
        inputs.append(part_in)
        in_specs.append(
            pl.BlockSpec((n_wide, rows_each, 3 * chunk), lambda j, *_: (0, 0, j)) if tall else part_specs[0]
        )
    shape = jax.ShapeDtypeStruct
    scratch = [pltpu.VMEM((width, 3 * chunk), F32)]
    out_shape = []
    if first:
        out_shape += [shape(rows, F32), shape(rows, BF16), shape(turned, BF16), shape(rows, BF16), shape(turned, BF16)]
    if last:
        out_shape += [shape(rows, BF16), shape(rows, F32), shape(rows, BF16), shape((1, width), F32)]
        scratch += [pltpu.VMEM(rows, F32)] * 2
    else:
        out_shape += [shape(rows, F32)] * 2
    outs = pl.pallas_call(
        functools.partial(middle_kernel, first, last, rows_each),
        grid_spec=pltpu.PrefetchScalarGridSpec(
            num_scalar_prefetch=1,
            grid=(steps,),
            in_specs=in_specs,
            out_specs=[whole(s.shape) for s in out_shape] + part_specs,
            scratch_shapes=scratch,
        ),
        out_shape=out_shape + part_shapes,
        compiler_params=pltpu.CompilerParams(vmem_limit_bytes=24 * MIB),
        cost_estimate=cost(36 * count * width * chunk * steps, 32 * width * chunk * steps),
        name="middle",
    )(table, *inputs)
    parts = outs[len(out_shape) :]
    if not tall and last is not None:
        slots = in_slots(parts[0], table, n_wide)
        parts = [slots[: n_wide // 2], slots[n_wide // 2 :]]
    return outs[: len(out_shape)], parts


def in_slots(part, table, n_wide):
    return jnp.take(part.reshape(n_wide, -1, part.shape[-1]), table, axis=0)


def seeds_kernel(own_ref, other_ref, w_ref, grad_ref, seed_t_ref):
    count = own_ref.shape[0]
    for half, seed_ref in enumerate((own_ref, other_ref)):
        at = slice(half * count, (half + 1) * count)
        grad_ref[at, :] = mm_nt(seed_ref[...], w_ref[...]).astype(BF16)
        seed_t_ref[:, at] = seed_ref[...].T


def seeds_call(own, other, w_out):
    count, width = own.shape
    out = w_out.shape[0]
    return pl.pallas_call(
        seeds_kernel,
        out_shape=[
            jax.ShapeDtypeStruct((2 * count, out), BF16),
            jax.ShapeDtypeStruct((width, 2 * count), BF16),
        ],
        cost_estimate=cost(4 * count * width * out, 8 * count * width),
        compiler_params=pltpu.CompilerParams(vmem_limit_bytes=8 * MIB),
        name="seeds",
    )(own, other, w_out)


def attention_back_kernel(block, rows_each, split, carried, *refs):
    refs = list(refs)
    table_ref = refs.pop(0)
    (qkv_ref, grad_ref, mixed_own_ref, mixed_other_ref, kept_ref, keys_ref) = refs[:6]
    (normed_t_ref, seed_t_ref) = refs[6:8]
    refs = refs[8 + carried :]
    pieces = refs.pop(0)
    part_refs = [refs.pop(0) for _ in range(split)]
    grads, queries, query_total, mixed, held = refs
    lane = lax.broadcasted_iota(jnp.int32, (1, LANES), 1)
    lows = (lane < DH, lane >= DH)
    nothing = jnp.zeros((1, LANES), BF16)
    length = grad_ref.shape[0]
    half = length // 2
    mixed[0:half, :] = mixed_own_ref[...]
    mixed[half:length, :] = mixed_other_ref[...]
    product = grad_ref[...].astype(F32) * mixed[...].astype(F32)
    for head in range(2):
        base = DH * (1 - head)
        dots = jnp.sum(jnp.where(lows[head], product, 0.0), axis=1, keepdims=True)
        high, middle, low = three_terms(dots)
        constants = jnp.where(
            lane == base + 2,
            -high,
            jnp.where(lane == base + 3, -middle, jnp.where(lane == base + 4, -low, nothing)),
        )
        grads[head] = jnp.where(lows[head], grad_ref[...], constants)
        grads[2 + head] = jnp.where(lows[head], grad_ref[...], nothing)
        queries[head] = jnp.where(lows[head], kept_ref[head], nothing)
    query_total[...] = jnp.zeros_like(query_total)

    def step(i, carry):
        rows = pl.ds(pl.multiple_of(i * block, block), block)
        keys, values, constants = qkv_ref[1, rows, :], qkv_ref[2, rows, :], keys_ref[rows, :]
        key_grad, value_grad = [], []
        for head in range(2):
            base = DH * (1 - head)
            ones = jnp.where((lane >= base + 2) & (lane < base + 5), 1.0, 0.0).astype(BF16)
            keys_only = jnp.where(lows[head], keys, nothing) * jnp.asarray(1.0 / math.sqrt(DH), BF16)
            weights = jnp.exp(mm_nt(jnp.where(lows[head], keys, constants), kept_ref[head]))
            score_grads = weights * mm_nt(jnp.where(lows[head], values, ones), grads[head])
            score_grads = score_grads.astype(BF16)
            value_grad.append(mm(weights.astype(BF16), grads[2 + head]))
            key_grad.append(mm(score_grads, queries[head]))
            query_total[...] += mm(keys_only.T, score_grads)
        pieces[rows, LANES : 2 * LANES] = (key_grad[0] + key_grad[1]).astype(BF16)
        pieces[rows, 2 * LANES : 3 * LANES] = (value_grad[0] + value_grad[1]).astype(BF16)
        return carry

    lax.fori_loop(0, length // block, step, 0)
    pieces[:, 0:LANES] = query_total[...].T.astype(BF16)
    held[:, 0 : 3 * LANES] = mm(normed_t_ref[...], pieces[...])
    held[:, 3 * LANES : 4 * LANES] = mm(seed_t_ref[...], mixed[...])
    write_slots(table_ref, held, part_refs, rows_each)


def attention_back(pair, at, total, carried, qkv, grad, mixed_own, mixed_other, kept, keys, normed_t, seed_t, table, n_wide, block=512):
    length = qkv.shape[1]
    half = length // 2
    width = normed_t.shape[0]
    rows_each = width // n_wide
    tall = rows_each % 16 == 0
    columns = 4 * LANES
    if tall:
        part_specs = [pl.BlockSpec((n_wide // 2, rows_each, columns), lambda p, *_: (0, 0, at))] * 2
        part_shapes = [jax.ShapeDtypeStruct((n_wide // 2, rows_each, total * columns), BF16)] * 2
    else:
        part_specs = [pl.BlockSpec((width, columns), lambda p, *_: (0, at))]
        part_shapes = [jax.ShapeDtypeStruct((width, total * columns), BF16)]
    in_specs = [
        pl.BlockSpec((3, length, LANES), lambda p, *_: (0, 0, pair)),
        pl.BlockSpec((length, LANES), lambda p, *_: (0, pair)),
        pl.BlockSpec((half, LANES), lambda p, *_: (0, pair)),
        pl.BlockSpec((half, LANES), lambda p, *_: (0, pair)),
        pl.BlockSpec((2, length, LANES), lambda p, *_: (pair, 0, 0)),
        whole((length, LANES)),
        whole((width, length)),
        whole((width, length)),
    ]
    inputs = [qkv, grad, mixed_own, mixed_other, kept, keys, normed_t, seed_t]
    aliases = {1 + len(inputs) + i: 1 + i for i in range(len(carried))}
    outs = pl.pallas_call(
        functools.partial(attention_back_kernel, block, rows_each, len(part_specs), len(carried)),
        grid_spec=pltpu.PrefetchScalarGridSpec(
            num_scalar_prefetch=1,
            grid=(1,),
            in_specs=in_specs + [pl.BlockSpec(memory_space=pl.ANY)] * len(carried),
            out_specs=[whole((length, 3 * LANES))] + part_specs,
            scratch_shapes=[
                pltpu.VMEM((4, length, LANES), BF16),
                pltpu.VMEM((2, length, LANES), BF16),
                pltpu.VMEM((LANES, length), F32),
                pltpu.VMEM((length, LANES), BF16),
                pltpu.VMEM((width, columns), F32),
            ],
        ),
        out_shape=[jax.ShapeDtypeStruct((length, 3 * LANES), BF16)] + part_shapes,
        input_output_aliases=aliases,
        compiler_params=pltpu.CompilerParams(vmem_limit_bytes=24 * MIB),
        cost_estimate=cost(50 * length * length * LANES, 16 * length * LANES),
        name="attention_back",
    )(table, *inputs, *carried)
    return outs[0], list(outs[1:])


def kept_and_sent(parts, table, n_wide):
    if len(parts) == 2:
        return parts
    slots = in_slots(parts[0], table, n_wide)
    return slots[: n_wide // 2], slots[n_wide // 2 :]


def added(arrays, low, high):
    return sum(a[low:high].astype(F32) for a in arrays)


class Scatter:
    def __init__(self, keep, send, n_wide):
        self.pieces, self.send, self.n_wide, self.slots, self.stage = [keep], send, n_wide, n_wide // 2, 0

    def go(self):
        self.pieces.append(stage_exchange(self.send, self.stage, self.n_wide))
        self.stage += 1

    def turn(self):
        self.slots //= 2
        self.send = added(self.pieces, self.slots, 2 * self.slots).astype(BF16)
        return self.send

    @property
    def done(self):
        return self.slots == 1 and self.stage > 0 and self.stage == self.n_wide.bit_length() - 1

    def finish(self):
        while not self.done:
            self.turn()
            self.go()
        return [added(self.pieces[:-1], 0, 1), self.pieces[-1]]


def input_other_kernel(pairs, *refs):
    *piece_refs, w_ref, out_ref = refs
    back = 0.0
    for i in range(3):
        columns = slice(i * LANES, (i + 1) * LANES)
        back = back + mm_nt(jnp.concatenate([ref[:, columns] for ref in piece_refs], axis=1), w_ref[i])
    out_ref[...] = back.astype(BF16)


def input_other(pieces, w_qkv):
    length, columns = pieces[0].shape
    half, width = length // 2, w_qkv.shape[1]
    return pl.pallas_call(
        functools.partial(input_other_kernel, len(pieces)),
        grid=(1,),
        in_specs=[pl.BlockSpec((half, columns), lambda *_: (1, 0))] * len(pieces) + [whole(w_qkv.shape)],
        out_specs=whole((half, width)),
        out_shape=jax.ShapeDtypeStruct((half, width), BF16),
        compiler_params=pltpu.CompilerParams(vmem_limit_bytes=12 * MIB),
        cost_estimate=cost(2 * half * width * columns * len(pieces), 4 << 20),
        name="input_other",
    )(*pieces, w_qkv)


def input_grad_kernel(pairs, *refs):
    piece_refs, refs = refs[:pairs], refs[pairs:]
    w_ref, recv_ref, tokens_ref, gain_ref, middle_grad_ref, out_ref, part_ref = refs
    back = recv_ref[...].astype(F32)
    for i in range(3):
        columns = slice(i * LANES, (i + 1) * LANES)
        back = back + mm_nt(jnp.concatenate([ref[:, columns] for ref in piece_refs], axis=1), w_ref[i])
    rows = tokens_ref[...].astype(F32)
    factor = inverse_rms(rows)
    scaled = back * gain_ref[...]
    inner = jnp.mean(scaled * rows, axis=-1, keepdims=True)
    out_ref[...] = middle_grad_ref[...] + factor * scaled - rows * (factor * factor * factor * inner)
    part_ref[...] = jnp.sum(back * rows * factor, axis=0, keepdims=True)


def input_grad(pieces, w_qkv, recv, tokens, gain_line, middle_grad):
    count, width = tokens.shape
    columns = pieces[0].shape[1]
    rest = [w_qkv, recv, tokens, gain_line, middle_grad]
    return pl.pallas_call(
        functools.partial(input_grad_kernel, len(pieces)),
        grid=(1,),
        in_specs=[pl.BlockSpec((count, columns), lambda *_: (0, 0))] * len(pieces) + [whole(v.shape) for v in rest],
        out_specs=[whole((count, width)), whole((1, width))],
        out_shape=[jax.ShapeDtypeStruct((count, width), F32), jax.ShapeDtypeStruct((1, width), F32)],
        compiler_params=pltpu.CompilerParams(vmem_limit_bytes=16 * MIB),
        cost_estimate=cost(2 * count * width * columns * len(pieces), 8 << 20),
        name="input_grad",
    )(*pieces, *rest)


def padded(rows):
    return -(-rows // 8) * 8


def gather_kernel(counts, wides, chunk, *refs):
    refs = list(refs)
    groups = [[refs.pop(0) for _ in range(count)] for count in counts]
    attn_gain_ref, mlp_gain_ref, sums_ref = refs[:3]
    qkv_ref, out_ref, gu_ref, down_ref, columns_ref, pair_ref = refs[3:]
    sums = []
    for group in groups:
        total = group[0][0].astype(F32)
        for ref in group[1:]:
            total = total + ref[0].astype(F32)
        sums.append(total)
    wide_part, pair_parts = jnp.concatenate(sums[:wides], axis=1), sums[wides:]
    pairs = [part[:, i : i + 4 * LANES] for part in pair_parts for i in range(0, part.shape[1], 4 * LANES)]
    mats = [
        jnp.concatenate([pair[:, i * LANES : (i + 1) * LANES] for pair in pairs], axis=1) for i in range(4)
    ]
    kinds = [
        jnp.concatenate(
            [
                wide_part[:, j + i * chunk : j + (i + 1) * chunk]
                for j in range(0, wide_part.shape[1], 3 * chunk)
            ],
            axis=1,
        )
        for i in range(3)
    ]
    rows = wide_part.shape[0]
    for i in range(3):
        qkv_ref[i] = mats[i]
    for i in range(2):
        gu_ref[i] = kinds[i]
    out_ref[...] = mats[3]
    down_ref[...] = kinds[2]
    columns_ref[...] = jnp.zeros_like(columns_ref)
    lane = lax.broadcasted_iota(jnp.int32, (1, LANES), 1)
    row_sums = jnp.zeros((rows, LANES), F32)
    for i, value in enumerate((mats[0], mats[1], mats[2], mats[3], kinds[0], kinds[1], kinds[2])):
        squares = value * value
        columns_ref[i : i + 1, 0 : value.shape[1]] = jnp.sum(squares, axis=0, keepdims=True)
        row_sums = jnp.where(lane == i, jnp.sum(squares, axis=1, keepdims=True), row_sums)
    pair_ref[...] = jnp.zeros_like(pair_ref)
    pair_ref[0:rows, :] = row_sums
    at = padded(rows)
    for ref in (attn_gain_ref, mlp_gain_ref):
        for i in range(0, ref.shape[1], LANES):
            pair_ref[at : at + 1, :] = ref[:, i : i + LANES]
            at += 1
    pair_ref[at : at + 1, :] = sums_ref[...]


def gather_own(groups, wides, attn_gain_part, mlp_gain_part, local_sums, heads_width, units, chunk):
    rows = groups[0][0].shape[1]
    width = attn_gain_part.shape[1]
    pieces = [a for group in groups for a in group]
    lines = [attn_gain_part, mlp_gain_part, local_sums]
    shapes = [(3, rows, heads_width), (rows, heads_width), (2, rows, units), (rows, units)]
    shapes += [(8, max(heads_width, units, width)), (padded(rows) + padded(2 * width // LANES + 1), LANES)]
    return pl.pallas_call(
        functools.partial(gather_kernel, [len(g) for g in groups], wides, chunk),
        grid=(1,),
        in_specs=[pl.BlockSpec((1,) + a.shape[1:], lambda *_: (0, 0, 0)) for a in pieces]
        + [whole(a.shape) for a in lines],
        out_specs=[whole(s) for s in shapes],
        out_shape=[jax.ShapeDtypeStruct(s, F32) for s in shapes],
        compiler_params=pltpu.CompilerParams(vmem_limit_bytes=8 * MIB),
        cost_estimate=cost(1 << 20, 4 << 20),
        name="gather_own",
    )(*pieces, *lines)


def combine_kernel(rows, width, columns_ref, own_ref, recv_ref, summed_ref, pair_ref):
    pair = own_ref[...] + recv_ref[...]
    pair_ref[...] = pair
    summed_ref[...] = jnp.zeros_like(summed_ref)
    summed_ref[0:8, :] = columns_ref[...]
    summed_ref[7:8, 0:LANES] = jnp.sum(pair[0:rows, :], axis=0, keepdims=True)
    at = padded(rows)
    for line in (8, 9):
        for i in range(0, width, LANES):
            summed_ref[line : line + 1, i : i + LANES] = pair[at : at + 1, :]
            at += 1


def combine(columns, own, recv, rows, width):
    shapes = [(16, columns.shape[1]), own.shape]
    return pl.pallas_call(
        functools.partial(combine_kernel, rows, width),
        out_shape=[jax.ShapeDtypeStruct(s, F32) for s in shapes],
        compiler_params=pltpu.CompilerParams(vmem_limit_bytes=4 * MIB),
        name="combine",
    )(columns, own, recv)


def update_kernel(sizes, *refs):
    (whole_ref, scalar_ref, qkv_ref, out_ref, gu_ref, down_ref, summed_ref, pair_ref, prior_rows_ref) = refs[:9]
    (qkv_cols, out_rows, gu_cols, down_rows, w_qkv, w_out, w_gu, w_down) = refs[9:17]
    (qkv_new, out_new, gu_new, down_new, qkv_cols_new, out_rows_new, gu_cols_new, down_rows_new) = refs[17:25]
    (qkv_rows_new, out_cols_new, gu_rows_new, down_cols_new, attn_gain_ref, mlp_gain_ref, turned) = refs[25:]
    rows = qkv_ref.shape[1]
    width = sizes[0]
    lane = lax.broadcasted_iota(jnp.int32, (1, LANES), 1)
    beta = 1.0 - lax.rsqrt(jnp.full((1, 1), scalar_ref[0], F32))
    fresh = 1.0 - beta
    start = lax.rem(width - whole_ref[0] * rows, width)
    own = pltpu.roll(prior_rows_ref[...], start, 1)[:, 0:LANES]
    turned[...] = jnp.zeros_like(turned)
    turned[0:8, :] = own
    prior_columns = turned[...].T
    gains = pltpu.roll(summed_ref[8:16, 0:width], start, 1)
    attn_gain_ref[...] = jnp.reshape(gains[0:1, 0:rows], (rows,))
    mlp_gain_ref[...] = jnp.reshape(gains[1:2, 0:rows], (rows,))
    sums = pair_ref[pl.ds(padded(rows) + 2 * width // LANES, 1), :]
    totals = summed_ref[7:8, 0:LANES]
    all_rows = jnp.zeros((rows, LANES), F32)
    priors = [qkv_cols[0:1], qkv_cols[1:2], qkv_cols[2:3], out_rows[...], gu_cols[0:1], gu_cols[1:2], down_rows[...]]
    for i in range(7):
        across = sizes[1 + i]
        entries = float(across * width)
        row_new = beta * prior_columns[0:rows, i : i + 1] + fresh * (pair_ref[0:rows, i : i + 1] / across + TINIEST)
        count = priors[i].shape[1]
        col_new = beta * priors[i] + fresh * (summed_ref[i : i + 1, 0:count] / width + TINIEST)
        all_rows = jnp.where(lane == i, row_new, all_rows)
        if i in (3, 6):
            at = 7 + (i == 6)
            prior_mean = sums[:, at : at + 1] / across
        else:
            prior_mean = jnp.mean(prior_rows_ref[i : i + 1, :], axis=1, keepdims=True)
        mean = beta * prior_mean + fresh * (totals[:, i : i + 1] / entries + TINIEST)
        rate = scalar_ref[1] * jnp.sqrt(sums[:, i : i + 1] / entries)
        step = lax.rsqrt(row_new * col_new / mean)
        if i in (3, 6):
            gradient_ref, weight_ref, new_ref = ((out_ref, w_out, out_new), (down_ref, w_down, down_new))[i == 6]
            new_ref[...] = (weight_ref[...].astype(F32) - rate * (gradient_ref[...] * step)).astype(BF16)
            (out_rows_new, down_rows_new)[i == 6][...] = jnp.reshape(col_new, (count,))
        else:
            at = i if i < 3 else i - 4
            gradient_ref, weight_ref, new_ref = (qkv_ref, w_qkv, qkv_new) if i < 3 else (gu_ref, w_gu, gu_new)
            new_ref[at] = (weight_ref[at].astype(F32) - rate * (gradient_ref[at] * step)).astype(BF16)
            (qkv_cols_new if i < 3 else gu_cols_new)[at : at + 1] = col_new
    turned[0:rows, :] = all_rows
    rows_new = turned[...].T
    qkv_rows_new[...] = rows_new[0:3, 0:rows]
    out_cols_new[...] = jnp.reshape(rows_new[3:4, 0:rows], (rows,))
    gu_rows_new[...] = rows_new[4:6, 0:rows]
    down_cols_new[...] = jnp.reshape(rows_new[6:7, 0:rows], (rows,))


def update(place, scalars, grads, summed, pair, prior_rows, col_priors, weights, sizes):
    rows = grads[0].shape[1]
    inputs = [*grads, summed, pair, prior_rows, *col_priors, *weights]
    shapes = [(3, sizes[1] // 2), (sizes[4] // 2,), (2, sizes[5] // 2), (sizes[7] // 2,)]
    shapes += [(3, rows), (rows,), (2, rows), (rows,), (rows,), (rows,)]
    out_shape = [jax.ShapeDtypeStruct(w.shape, BF16) for w in weights]
    out_shape += [jax.ShapeDtypeStruct(s, F32) for s in shapes]
    return pl.pallas_call(
        functools.partial(update_kernel, sizes),
        grid_spec=pltpu.PrefetchScalarGridSpec(
            num_scalar_prefetch=2,
            grid=(1,),
            in_specs=[whole(a.shape) for a in inputs],
            out_specs=[whole(s.shape) for s in out_shape],
            scratch_shapes=[pltpu.VMEM((LANES, LANES), F32)],
        ),
        out_shape=out_shape,
        compiler_params=pltpu.CompilerParams(vmem_limit_bytes=8 * MIB),
        cost_estimate=cost(1 << 20, 4 << 20),
        name="update",
    )(place, scalars, *inputs)


def square_sum(values):
    wide = values.astype(F32)
    return jnp.sum(wide * wide, axis=(-2, -1))


def after(values, *others):
    return lax.optimization_barrier((values, *others))[0]


def body(
    n_wide,
    tokens,
    plot_slot,
    patch_mask,
    cotangent,
    gain_attn,
    w_qkv,
    w_out,
    gain_mlp,
    w_gu,
    w_down,
    qkv_rows,
    qkv_cols,
    out_rows,
    out_cols,
    gu_rows,
    gu_cols,
    down_rows,
    down_cols,
    step_count,
    learn_rate,
):
    width = tokens.shape[1]
    heads_width, units = w_out.shape[0], w_down.shape[0]
    rows_each = width // n_wide
    chunk = 256
    core = lax.axis_index("narrow")
    wide = lax.axis_index("wide")
    tables = [slot_table(wide, order, n_wide) for order in bit_orders(n_wide)]
    own_table = jnp.where(core == 0, tables[0], tables[1])
    other_table = jnp.where(core == 0, tables[1], tables[0])

    tokens_other = swap(tokens)
    lines = key_lines(plot_slot, patch_mask, core)
    normed_t, qkv = project(tokens, tokens_other, gain_attn, w_qkv)
    sent = after((w_out, w_gu, w_down), tokens_other)
    w_out_other, w_gu_other, w_down_other = swap(sent[0]), swap(sent[1]), swap(sent[2])
    mixed_own, mixed_other, kept, keys = attention(qkv, lines)
    mixed_recv = swap(mixed_other)
    gain_line = gain_mlp[None]
    steps = units // chunk // 2
    half = n_wide // 2

    (middle, *handed), (part_other,) = middle_call(
        True,
        None,
        [tokens, mixed_own, mixed_recv, w_out, w_out_other, gain_line, cotangent, lines],
        w_gu_other,
        w_down_other,
        0,
        steps,
        None,
        other_table,
        n_wide,
        chunk,
    )
    part_first = swap(part_other)
    totals, (part_other,) = middle_call(
        False, None, handed, w_gu_other, w_down_other, steps, steps, None, other_table, n_wide, chunk
    )
    part_second = swap(part_other)
    handed = [*handed[:4], *totals]
    totals, parts = middle_call(
        False, False, handed, w_gu, w_down, 0, steps, part_first, own_table, n_wide, chunk
    )
    wide_a = Scatter(*parts, n_wide)
    wide_a.go()
    handed = [*handed[:4], *totals]
    (mixed_out, middle_grad, attn_seed, mlp_gain_part), parts = middle_call(
        False, True, [*handed, middle, gain_line], w_gu, w_down, steps, steps, part_second, own_table, n_wide, chunk
    )
    wide_b = Scatter(*parts, n_wide)
    wide_b.go()
    mixed_grad, seed_t = seeds_call(attn_seed, swap(attn_seed), w_out)

    pairs = heads_width // LANES
    back = functools.partial(
        attention_back,
        qkv=qkv,
        mixed_own=mixed_own,
        mixed_other=mixed_other,
        kept=kept,
        keys=keys,
        normed_t=normed_t,
        seed_t=seed_t,
        table=own_table,
        n_wide=n_wide,
    )
    pieces = []
    piece, carried = back(0, 0, pairs - 1, [], grad=mixed_grad)
    pieces.append(piece)
    mixed_grad = after(mixed_grad, wide_a.turn())
    wide_a.go()
    for pair in range(1, pairs - 1):
        piece, carried = back(pair, pair, pairs - 1, carried, grad=mixed_grad)
        pieces.append(piece)
    first = Scatter(*kept_and_sent(carried, own_table, n_wide), n_wide)
    first.go()
    mixed_grad = after(mixed_grad, wide_a.turn(), wide_b.turn(), first.send)
    wide_a.go()
    wide_b.go()
    piece, carried = back(pairs - 1, 0, 1, [], grad=mixed_grad)
    pieces.append(piece)
    last = Scatter(*kept_and_sent(carried, own_table, n_wide), n_wide)
    last.go()
    groups = [wide_a.finish(), wide_b.finish(), first.finish(), last.finish()]
    back_other = swap(input_other(pieces, w_qkv))
    tokens_grad, attn_gain_part = input_grad(pieces, w_qkv, back_other, tokens, gain_attn[None], middle_grad)

    weights = after((w_qkv, w_out, w_gu, w_down, out_rows, down_rows, qkv_rows, out_cols, gu_rows, down_cols), piece)
    local_sums = jnp.concatenate(
        [square_sum(w.reshape(-1, *w.shape[-2:])) for w in weights[:4]]
        + [jnp.sum(weights[4])[None], jnp.sum(weights[5])[None], jnp.zeros((LANES - 9,), F32)]
    )[None]
    prior_rows = jnp.concatenate(
        [weights[6], weights[7][None], weights[8], weights[9][None], jnp.zeros((1, width), F32)], axis=0
    )

    def own_rows(values, dimension):
        return lax.dynamic_slice_in_dim(values, wide * rows_each, rows_each, dimension)

    own_weights = [own_rows(weights[0], 1), own_rows(weights[1], 1).T, own_rows(weights[2], 1), own_rows(weights[3], 1).T]

    *grads, columns, pair = gather_own(
        groups, 2, attn_gain_part, mlp_gain_part, local_sums, heads_width, units, chunk
    )
    summed, pair = combine(columns, pair, swap(pair), rows_each, width)
    for stage in range(n_wide.bit_length() - 1):
        summed = summed + stage_exchange(summed, stage, n_wide)
    outs = update(
        (wide.astype(jnp.int32))[None],
        jnp.stack([step_count.astype(F32), learn_rate]),
        grads,
        summed,
        pair,
        prior_rows,
        [qkv_cols, out_rows[None], gu_cols, down_rows[None]],
        own_weights,
        [width] + [2 * heads_width] * 4 + [2 * units] * 3,
    )
    qkv_new, out_new, gu_new, down_new, qkv_cols_new, out_rows_new, gu_cols_new, down_rows_new = outs[:8]
    qkv_rows_new, out_cols_new, gu_rows_new, down_cols_new, attn_gain_grad, mlp_gain_grad = outs[8:]
    qkv_grad, out_grad, gu_grad, down_grad = grads
    return (
        mixed_out,
        tokens_grad,
        attn_gain_grad,
        qkv_grad,
        out_grad.T,
        mlp_gain_grad,
        gu_grad,
        down_grad.T,
        qkv_new,
        out_new.T,
        gu_new,
        down_new.T,
        qkv_rows_new,
        qkv_cols_new,
        out_rows_new,
        out_cols_new,
        gu_rows_new,
        gu_cols_new,
        down_rows_new,
        down_cols_new,
    )


def solution(mesh):
    in_specs = (
        P(("wide", "narrow"), None),
        P("wide"),
        P("wide"),
        P(("wide", "narrow"), None),
        P(),
        P(None, None, "narrow"),
        P("narrow", None),
        P(),
        P(None, None, "narrow"),
        P("narrow", None),
        P(),
        P(None, "narrow"),
        P("narrow"),
        P(),
        P(),
        P(None, "narrow"),
        P("narrow"),
        P(),
        P(),
        P(),
    )
    out_specs = (
        P(("wide", "narrow"), None),
        P(("wide", "narrow"), None),
        P("wide"),
        P(None, "wide", "narrow"),
        P("narrow", "wide"),
        P("wide"),
        P(None, "wide", "narrow"),
        P("narrow", "wide"),
        P(None, "wide", "narrow"),
        P("narrow", "wide"),
        P(None, "wide", "narrow"),
        P("narrow", "wide"),
        P(None, "wide"),
        P(None, "narrow"),
        P("narrow"),
        P("wide"),
        P(None, "wide"),
        P(None, "narrow"),
        P("narrow"),
        P("wide"),
    )
    return jax.shard_map(
        functools.partial(body, mesh.shape["wide"]),
        mesh=mesh,
        in_specs=in_specs,
        out_specs=out_specs,
        check_vma=False,
    )
```

```python
import functools
import math

import jax
import jax.numpy as jnp
from jax import lax
from jax.experimental import pallas as pl
from jax.experimental.pallas import tpu as pltpu
from jax.sharding import PartitionSpec as P

DH = 64
LANES = 128
EPSILON = 1e-06
TINIEST = 1e-30
NEGATIVE = -1e30
F32 = jnp.float32
BF16 = jnp.bfloat16
ROOT = math.sqrt(2.0 / math.pi)
CUBE = 0.044715
MIB = 1024 * 1024
LIVE = 5


def mm(a, b):
    return jnp.dot(a, b, preferred_element_type=F32)


def mm_nt(a, b):
    return lax.dot_general(a, b, (((1,), (1,)), ((), ())), preferred_element_type=F32)


def whole(shape):
    return pl.BlockSpec(shape, lambda *_: (0,) * len(shape))


def cost(flops, nbytes):
    return pl.CostEstimate(flops=int(flops), bytes_accessed=int(nbytes), transcendentals=0)


def inverse_rms(rows):
    return lax.rsqrt(jnp.mean(rows * rows, axis=-1, keepdims=True) + EPSILON)


def three_terms(values):
    high = values.astype(BF16)
    rest = values - high.astype(F32)
    middle = rest.astype(BF16)
    return high, middle, (rest - middle.astype(F32)).astype(BF16)


def bit_orders(n_wide):
    bits = n_wide.bit_length() - 1
    straight = list(range(bits))
    turned = straight[1:-1] + straight[:1] + straight[-1:] if bits > 2 else straight
    return straight, turned


def slot_masks(n_wide):
    bits = n_wide.bit_length() - 1
    return [
        [sum(1 << bit for stage, bit in enumerate(order) if slot >> (bits - 1 - stage) & 1) for slot in range(n_wide)]
        for order in bit_orders(n_wide)
    ]


def slot_row(slot, n_wide, turned):
    masks = slot_masks(n_wide)
    wide, core = lax.axis_index("wide"), lax.axis_index("narrow")
    first, second = masks[turned][slot], masks[1 - turned][slot]
    return jnp.bitwise_xor(wide, first + (second - first) * core)


def stage_exchange(values, stage, n_wide):
    orders = bit_orders(n_wide)
    pairs = []
    for wide in range(n_wide):
        for core in range(2):
            pairs.append((wide * 2 + core, (wide ^ (1 << orders[core][stage])) * 2 + core))
    return lax.ppermute(values, ("wide", "narrow"), pairs)


def swap(values):
    return lax.ppermute(values, "narrow", [(0, 1), (1, 0)])


def write_slots(turned, n_wide, held_ref, targets, rows_each, more_ref=None):
    if targets[0].ndim == 2:
        more = 0.0 if more_ref is None else more_ref[...].astype(F32)
        targets[0][...] = (held_ref[...] + more).astype(BF16)
        return
    slot = 0
    for target in targets:
        for at in range(target.shape[0]):
            start = pl.multiple_of(slot_row(slot, n_wide, turned) * rows_each, 16)
            value = held_ref[pl.ds(start, rows_each), :]
            if more_ref is not None:
                value = value + more_ref[slot].astype(F32)
            target[at] = value.astype(BF16)
            slot += 1


def in_slots(part, n_wide):
    rows = jnp.stack([slot_row(slot, n_wide, 0) for slot in range(n_wide)])
    return jnp.take(part.reshape(n_wide, -1, part.shape[-1]), rows, axis=0)


def as_line(ref):
    return jnp.reshape(ref[...], (1, ref.shape[0]))


def project_kernel(carried, rows_ref, gain_ref, w_ref, *refs):
    normed_t_ref, projected_ref = refs[carried:]
    rows = rows_ref[...].astype(F32)
    normed = (rows * inverse_rms(rows) * as_line(gain_ref)).astype(BF16)
    normed_t_ref[...] = normed.T
    for i in range(3):
        projected_ref[i] = mm(normed, w_ref[i]).astype(BF16)


def project(half, tokens, gain, w_qkv, carried):
    count, width = tokens.shape
    out = w_qkv.shape[2]
    inputs = [tokens, gain, w_qkv]
    return pl.pallas_call(
        functools.partial(project_kernel, len(carried)),
        grid=(1,),
        in_specs=[whole(v.shape) for v in inputs] + [pl.BlockSpec(memory_space=pl.ANY)] * len(carried),
        out_specs=[
            pl.BlockSpec((width, count), lambda *_: (0, half)),
            pl.BlockSpec((3, count, out), lambda *_: (0, half, 0)),
        ],
        out_shape=[
            jax.ShapeDtypeStruct((width, 2 * count), BF16),
            jax.ShapeDtypeStruct((3, 2 * count, out), BF16),
        ],
        input_output_aliases={len(inputs) + i: i for i in range(len(carried))},
        cost_estimate=cost(6 * count * width * out, 4 * count * width),
        compiler_params=pltpu.CompilerParams(vmem_limit_bytes=8 * MIB),
        name="project",
    )(*inputs, *carried)


def key_lines(slot_ref, mask_ref, core):
    slot, mask = as_line(slot_ref), as_line(mask_ref)
    length = mask.shape[1]
    turned = lambda values: pltpu.roll(values, length // 2, 1)
    live = mask + (turned(mask) - mask) * core
    same = jnp.where(slot == turned(slot), live, 0)
    first = lax.broadcasted_iota(jnp.int32, (1, length), 1) < length // 2
    for_own = jnp.where(jnp.where(first, live, same) > 0, 0.0, NEGATIVE)
    for_other = jnp.where(jnp.where(first, same, live) > 0, 0.0, NEGATIVE)
    return for_own, for_other, live.astype(F32)


def column(line):
    return jnp.broadcast_to(line, (LANES, line.shape[1])).T


def attention_kernel(qkv_ref, slot_ref, mask_ref, own_ref, other_ref, kept_ref, keys_ref, held, *, block):
    lane = lax.broadcasted_iota(jnp.int32, (1, LANES), 1)
    lows = (lane < DH, lane >= DH)
    within = jnp.bitwise_and(lane, DH - 1)

    @pl.when(pl.program_id(0) == 0)
    def _():
        ones = jnp.where((within >= 2) & (within < 5), 1.0, 0.0)
        for_own, for_other, live = key_lines(slot_ref, mask_ref, lax.axis_index("narrow"))
        bias = jnp.where(within == 1, column(for_other), jnp.where(within == LIVE, column(live), ones))
        keys_ref[...] = jnp.where(within == 0, column(for_own), bias).astype(BF16)

    for head in range(2):
        held[head] = jnp.where(lows[head], qkv_ref[1], keys_ref[...])
        held[2 + head] = jnp.where(lows[head], qkv_ref[2], jnp.ones((1, LANES), BF16))
    half = own_ref.shape[0]
    for part, out_ref in enumerate((own_ref, other_ref)):

        def step(i, carry, part=part, out_ref=out_ref):
            inside = pl.ds(pl.multiple_of(i * block, block), block)
            rows = pl.ds(pl.multiple_of(part * half + i * block, block), block)
            queries = qkv_ref[0, rows, :] * jnp.asarray(1.0 / math.sqrt(DH), BF16)
            constants = jnp.where(within == part, 1.0, 0.0).astype(BF16)
            results = []
            for head in range(2):
                scores = mm_nt(jnp.where(lows[head], queries, constants), held[head])
                highest = jnp.max(scores, axis=1, keepdims=True)
                weights = jnp.exp(scores - highest).astype(BF16)
                mixed = mm(weights, held[2 + head])
                results.append(mixed / pltpu.roll(mixed, DH, 1))
                high, middle, low = three_terms(highest + jnp.log(mixed))
                base = DH * (1 - head)
                constants_back = jnp.where(
                    lane == base + 2,
                    -high,
                    jnp.where(lane == base + 3, -middle, jnp.where(lane == base + 4, -low, constants)),
                )
                kept_ref[head, rows, :] = jnp.where(lows[head], queries, constants_back)
            out_ref[inside, :] = jnp.where(lows[0], results[0], results[1]).astype(BF16)
            return carry

        lax.fori_loop(0, half // block, step, 0)


def attention(qkv, plot_slot, patch_mask, block=512):
    length, width = qkv.shape[1:]
    pairs, half = width // LANES, length // 2
    return pl.pallas_call(
        functools.partial(attention_kernel, block=block),
        grid=(pairs,),
        in_specs=[
            pl.BlockSpec((3, length, LANES), lambda p: (0, 0, p)),
            whole(plot_slot.shape),
            whole(patch_mask.shape),
        ],
        out_specs=[
            pl.BlockSpec((half, LANES), lambda p: (0, p)),
            pl.BlockSpec((half, LANES), lambda p: (0, p)),
            pl.BlockSpec((2, length, LANES), lambda p: (p, 0, 0)),
            whole((length, LANES)),
        ],
        scratch_shapes=[pltpu.VMEM((4, length, LANES), BF16)],
        out_shape=[
            jax.ShapeDtypeStruct((half, width), BF16),
            jax.ShapeDtypeStruct((half, width), BF16),
            jax.ShapeDtypeStruct((2 * pairs, length, LANES), BF16),
            jax.ShapeDtypeStruct((length, LANES), BF16),
        ],
        cost_estimate=cost(16 * pairs * length * length * LANES, 10 * length * width),
        compiler_params=pltpu.CompilerParams(vmem_limit_bytes=11 * MIB),
        name="attention",
    )(qkv, plot_slot, patch_mask)


def middle_kernel(first, last, rows_each, n_wide, *refs):
    refs = list(refs)
    take = lambda n: [refs.pop(0) for _ in range(n)]
    if first:
        (tokens_ref, own_ref, recv_ref, w_own_ref, w_recv_ref, gain_ref, cot_ref, keys_ref) = take(8)
    else:
        (normed, normed_t, seed, seed_t, total_in, back_in) = take(6)
        if last:
            (middle_ref, gain_ref) = take(2)
    (gu_ref, down_ref) = take(2)
    part_in = None if last is None else take(1)[0]
    if first:
        (middle_ref, normed, normed_t, seed, seed_t) = take(5)
    if last:
        (out_ref, grad_ref, attn_seed_ref, gain_part_ref) = take(4)
    else:
        (total_ref, back_ref) = take(2)
    part_refs = take(len(refs) - (3 if last else 1))
    (held,) = take(1)
    if last:
        (total_ref, back_ref) = take(2)
    step = pl.program_id(0)

    @pl.when(step == 0)
    def _():
        if first:
            middle = tokens_ref[...].astype(F32) + (
                mm(own_ref[...], w_own_ref[...]) + mm(recv_ref[...], w_recv_ref[...])
            )
            middle_ref[...] = middle
            total_ref[...] = middle
            back_ref[...] = jnp.zeros_like(back_ref)
            live = keys_ref[...].astype(F32)[:, LIVE : LIVE + 1]
            seed_value = (cot_ref[...].astype(F32) * live).astype(BF16)
            seed[...] = seed_value
            seed_t[...] = seed_value.T
            value = (middle * inverse_rms(middle) * as_line(gain_ref)).astype(BF16)
            normed[...] = value
            normed_t[...] = value.T
        else:
            total_ref[...] = total_in[...]
            back_ref[...] = back_in[...]

    gate = mm(normed[...], gu_ref[0])
    up = mm(normed[...], gu_ref[1])
    bent = jnp.tanh(ROOT * (gate + CUBE * gate * gate * gate))
    soft = 0.5 * gate * (1.0 + bent)
    slope = 0.5 * (1.0 + bent) + 0.5 * gate * (1.0 - bent * bent) * (ROOT * (1.0 + 3.0 * CUBE * gate * gate))
    hidden = (soft * up).astype(BF16)
    hidden_grad = mm_nt(seed[...], down_ref[...])
    gate_grad = (hidden_grad * up * slope).astype(BF16)
    up_grad = (hidden_grad * soft).astype(BF16)
    total_ref[...] += mm(hidden, down_ref[...])
    back_ref[...] += mm_nt(gate_grad, gu_ref[0]) + mm_nt(up_grad, gu_ref[1])
    chunk = gate.shape[1]
    held[:, 0:chunk] = mm(normed_t[...], gate_grad)
    held[:, chunk : 2 * chunk] = mm(normed_t[...], up_grad)
    held[:, 2 * chunk : 3 * chunk] = mm(seed_t[...], hidden)
    write_slots(int(last is None), n_wide, held, part_refs, rows_each, part_in)

    if last:

        @pl.when(step == pl.num_programs(0) - 1)
        def _():
            out_ref[...] = total_ref[...].astype(BF16)
            middle = middle_ref[...]
            factor = inverse_rms(middle)
            back = back_ref[...]
            scaled = back * as_line(gain_ref)
            inner = jnp.mean(scaled * middle, axis=-1, keepdims=True)
            grad = seed[...].astype(F32) + factor * scaled - middle * (factor * factor * factor * inner)
            grad_ref[...] = grad
            attn_seed_ref[...] = grad.astype(BF16)
            gain_part_ref[...] = jnp.sum(back * middle * factor, axis=0, keepdims=True)


def middle_call(first, last, inputs, w_gu, w_down, at, steps, part_in, n_wide, chunk):
    count, width = inputs[0].shape
    rows_each = width // n_wide
    tall = rows_each % 16 == 0
    rows, turned = (count, width), (width, count)
    columns = 3 * chunk * steps
    if tall:
        slots = [n_wide] if last is None else [n_wide // 2] * 2
        part_specs = [pl.BlockSpec((n, rows_each, 3 * chunk), lambda j, *_: (0, 0, j)) for n in slots]
        part_shapes = [jax.ShapeDtypeStruct((n, rows_each, columns), BF16) for n in slots]
    else:
        part_specs = [pl.BlockSpec((width, 3 * chunk), lambda j, *_: (0, j))]
        part_shapes = [jax.ShapeDtypeStruct((width, columns), BF16)]
    in_specs = [whole((count, LANES) if v.shape[1:] == (LANES,) else v.shape) for v in inputs] + [
        pl.BlockSpec((2, width, chunk), lambda j, *_: (0, 0, at + j)),
        pl.BlockSpec((chunk, width), lambda j, *_: (at + j, 0)),
    ]
    inputs = [*inputs, w_gu, w_down]
    if last is not None:
        inputs.append(part_in)
        in_specs.append(
            pl.BlockSpec((n_wide, rows_each, 3 * chunk), lambda j, *_: (0, 0, j)) if tall else part_specs[0]
        )
    shape = jax.ShapeDtypeStruct
    scratch = [pltpu.VMEM((width, 3 * chunk), F32)]
    out_shape = []
    if first:
        out_shape += [shape(rows, F32), shape(rows, BF16), shape(turned, BF16), shape(rows, BF16), shape(turned, BF16)]
    if last:
        out_shape += [shape(rows, BF16), shape(rows, F32), shape(rows, BF16), shape((1, width), F32)]
        scratch += [pltpu.VMEM(rows, F32)] * 2
    else:
        out_shape += [shape(rows, F32)] * 2
    outs = pl.pallas_call(
        functools.partial(middle_kernel, first, last, rows_each, n_wide),
        grid=(steps,),
        in_specs=in_specs,
        out_specs=[whole(s.shape) for s in out_shape] + part_specs,
        scratch_shapes=scratch,
        out_shape=out_shape + part_shapes,
        compiler_params=pltpu.CompilerParams(vmem_limit_bytes=(20 if last else 14) * MIB),
        cost_estimate=cost(36 * count * width * chunk * steps, 32 * width * chunk * steps),
        name="middle",
    )(*inputs)
    parts = outs[len(out_shape) :]
    if not tall and last is not None:
        slots = in_slots(parts[0], n_wide)
        parts = [slots[: n_wide // 2], slots[n_wide // 2 :]]
    return outs[: len(out_shape)], parts


def seeds_kernel(own_ref, other_ref, w_ref, grad_ref, seed_t_ref):
    count = own_ref.shape[0]
    for half, seed_ref in enumerate((own_ref, other_ref)):
        at = slice(half * count, (half + 1) * count)
        grad_ref[at, :] = mm_nt(seed_ref[...], w_ref[...]).astype(BF16)
        seed_t_ref[:, at] = seed_ref[...].T


def seeds_call(own, other, w_out):
    count, width = own.shape
    out = w_out.shape[0]
    return pl.pallas_call(
        seeds_kernel,
        out_shape=[
            jax.ShapeDtypeStruct((2 * count, out), BF16),
            jax.ShapeDtypeStruct((width, 2 * count), BF16),
        ],
        cost_estimate=cost(count * width, 8 * count),
        compiler_params=pltpu.CompilerParams(vmem_limit_bytes=4 * MIB),
        name="seeds",
    )(own, other, w_out)


def attention_back_kernel(block, rows_each, n_wide, split, carried, *refs):
    refs = list(refs)
    (qkv_ref, grad_ref, mixed_own_ref, mixed_other_ref, kept_ref, keys_ref) = refs[:6]
    (normed_t_ref, seed_t_ref) = refs[6:8]
    refs = refs[8 + carried :]
    pieces = refs.pop(0)
    part_refs = [refs.pop(0) for _ in range(split)]
    grads, queries, query_total, mixed, held = refs
    lane = lax.broadcasted_iota(jnp.int32, (1, LANES), 1)
    lows = (lane < DH, lane >= DH)
    nothing = jnp.zeros((1, LANES), BF16)
    length = grad_ref.shape[0]
    half = length // 2
    mixed[0:half, :] = mixed_own_ref[...]
    mixed[half:length, :] = mixed_other_ref[...]
    product = grad_ref[...].astype(F32) * mixed[...].astype(F32)
    for head in range(2):
        base = DH * (1 - head)
        dots = jnp.sum(jnp.where(lows[head], product, 0.0), axis=1, keepdims=True)
        high, middle, low = three_terms(dots)
        constants = jnp.where(
            lane == base + 2,
            -high,
            jnp.where(lane == base + 3, -middle, jnp.where(lane == base + 4, -low, nothing)),
        )
        grads[head] = jnp.where(lows[head], grad_ref[...], constants)
        grads[2 + head] = jnp.where(lows[head], grad_ref[...], nothing)
        queries[head] = jnp.where(lows[head], kept_ref[head], nothing)
    query_total[...] = jnp.zeros_like(query_total)

    def step(i, carry):
        rows = pl.ds(pl.multiple_of(i * block, block), block)
        keys, values, constants = qkv_ref[1, rows, :], qkv_ref[2, rows, :], keys_ref[rows, :]
        key_grad, value_grad = [], []
        for head in range(2):
            base = DH * (1 - head)
            ones = jnp.where((lane >= base + 2) & (lane < base + 5), 1.0, 0.0).astype(BF16)
            keys_only = jnp.where(lows[head], keys, nothing) * jnp.asarray(1.0 / math.sqrt(DH), BF16)
            weights = jnp.exp(mm_nt(jnp.where(lows[head], keys, constants), kept_ref[head]))
            score_grads = weights * mm_nt(jnp.where(lows[head], values, ones), grads[head])
            score_grads = score_grads.astype(BF16)
            value_grad.append(mm(weights.astype(BF16), grads[2 + head]))
            key_grad.append(mm(score_grads, queries[head]))
            query_total[...] += mm(keys_only.T, score_grads)
        pieces[rows, LANES : 2 * LANES] = (key_grad[0] + key_grad[1]).astype(BF16)
        pieces[rows, 2 * LANES : 3 * LANES] = (value_grad[0] + value_grad[1]).astype(BF16)
        return carry

    lax.fori_loop(0, length // block, step, 0)
    pieces[:, 0:LANES] = query_total[...].T.astype(BF16)
    held[:, 0 : 3 * LANES] = mm(normed_t_ref[...], pieces[...])
    held[:, 3 * LANES : 4 * LANES] = mm(seed_t_ref[...], mixed[...])
    write_slots(0, n_wide, held, part_refs, rows_each)


def attention_back(pair, at, total, carried, qkv, grad, mixed_own, mixed_other, kept, keys, normed_t, seed_t, n_wide, block=512):
    length = qkv.shape[1]
    half = length // 2
    width = normed_t.shape[0]
    rows_each = width // n_wide
    tall = rows_each % 16 == 0
    columns = 4 * LANES
    if tall:
        part_specs = [pl.BlockSpec((n_wide // 2, rows_each, columns), lambda p, *_: (0, 0, at))] * 2
        part_shapes = [jax.ShapeDtypeStruct((n_wide // 2, rows_each, total * columns), BF16)] * 2
    else:
        part_specs = [pl.BlockSpec((width, columns), lambda p, *_: (0, at))]
        part_shapes = [jax.ShapeDtypeStruct((width, total * columns), BF16)]
    in_specs = [
        pl.BlockSpec((3, length, LANES), lambda p, *_: (0, 0, pair)),
        pl.BlockSpec((length, LANES), lambda p, *_: (0, pair)),
        pl.BlockSpec((half, LANES), lambda p, *_: (0, pair)),
        pl.BlockSpec((half, LANES), lambda p, *_: (0, pair)),
        pl.BlockSpec((2, length, LANES), lambda p, *_: (pair, 0, 0)),
        whole((length, LANES)),
        whole((width, length)),
        whole((width, length)),
    ]
    inputs = [qkv, grad, mixed_own, mixed_other, kept, keys, normed_t, seed_t]
    aliases = {len(inputs) + i: 1 + i for i in range(len(carried))}
    outs = pl.pallas_call(
        functools.partial(attention_back_kernel, block, rows_each, n_wide, len(part_specs), len(carried)),
        grid=(1,),
        in_specs=in_specs + [pl.BlockSpec(memory_space=pl.ANY)] * len(carried),
        out_specs=[whole((length, 3 * LANES))] + part_specs,
        scratch_shapes=[
            pltpu.VMEM((4, length, LANES), BF16),
            pltpu.VMEM((2, length, LANES), BF16),
            pltpu.VMEM((LANES, length), F32),
            pltpu.VMEM((length, LANES), BF16),
            pltpu.VMEM((width, columns), F32),
        ],
        out_shape=[jax.ShapeDtypeStruct((length, 3 * LANES), BF16)] + part_shapes,
        input_output_aliases=aliases,
        compiler_params=pltpu.CompilerParams(vmem_limit_bytes=15 * MIB),
        cost_estimate=cost(50 * length * length * LANES, 16 * length * LANES),
        name="attention_back",
    )(*inputs, *carried)
    return outs[0], list(outs[1:])


def kept_and_sent(parts, n_wide):
    if len(parts) == 2:
        return parts
    slots = in_slots(parts[0], n_wide)
    return slots[: n_wide // 2], slots[n_wide // 2 :]


def turn_kernel(counts, *refs):
    *refs, out_ref = refs
    groups = [[refs.pop(0) for _ in range(count)] for count in counts]

    def step(slot, carry):
        at = 0
        for group in groups:
            columns = slice(at, at + group[0].shape[2])
            total = 0.0
            for ref in group:
                total = total + ref[slot].astype(F32)
            for ref in refs:
                total = total + ref[slot, :, columns].astype(F32)
            out_ref[slot, :, columns] = total.astype(BF16)
            at = columns.stop
        return carry

    lax.fori_loop(0, out_ref.shape[0], step, 0)


class Scatter:
    def __init__(self, groups, n_wide):
        self.groups, self.joint, self.n_wide, self.stage, self.slots = groups, [], n_wide, 1, n_wide // 2

    def turn(self, *earlier):
        self.slots //= 2
        pieces = [a for group in self.groups for a in group] + self.joint
        if earlier:
            pieces[-1] = after(pieces[-1], *earlier)
        rows = pieces[0].shape[1]
        shape = (self.slots, rows, sum(group[0].shape[2] for group in self.groups))
        self.send = pl.pallas_call(
            functools.partial(turn_kernel, [len(group) for group in self.groups]),
            grid=(1,),
            in_specs=[pl.BlockSpec((self.slots,) + a.shape[1:], lambda *_: (1, 0, 0)) for a in pieces],
            out_specs=whole(shape),
            out_shape=jax.ShapeDtypeStruct(shape, BF16),
            compiler_params=pltpu.CompilerParams(vmem_limit_bytes=8 * MIB),
            cost_estimate=cost(math.prod(shape), 4 * math.prod(shape)),
            name="turn",
        )(*pieces)
        return self.send

    def go(self):
        self.joint.append(stage_exchange(self.send, self.stage, self.n_wide))
        self.stage += 1

    def finish(self, other):
        while other.slots > 1:
            earlier = []
            if self.slots > 1:
                earlier = [self.turn()]
                self.go()
            other.turn(*earlier)
            other.go()
        return [(batch.groups, batch.joint) for batch in (self, other)]


def input_other_kernel(pairs, *refs):
    *piece_refs, w_ref, out_ref = refs
    back = 0.0
    for i in range(3):
        columns = slice(i * LANES, (i + 1) * LANES)
        back = back + mm_nt(jnp.concatenate([ref[:, columns] for ref in piece_refs], axis=1), w_ref[i])
    out_ref[...] = back.astype(BF16)


def input_other(pieces, w_qkv):
    length, columns = pieces[0].shape
    half, width = length // 2, w_qkv.shape[1]
    return pl.pallas_call(
        functools.partial(input_other_kernel, len(pieces)),
        grid=(1,),
        in_specs=[pl.BlockSpec((half, columns), lambda *_: (1, 0))] * len(pieces) + [whole(w_qkv.shape)],
        out_specs=whole((half, width)),
        out_shape=jax.ShapeDtypeStruct((half, width), BF16),
        compiler_params=pltpu.CompilerParams(vmem_limit_bytes=5 * MIB),
        cost_estimate=cost(2 * half * width * columns * len(pieces), 4 << 20),
        name="input_other",
    )(*pieces, w_qkv)


def input_grad_kernel(pairs, *refs):
    piece_refs, refs = refs[:pairs], refs[pairs:]
    w_ref, recv_ref, tokens_ref, gain_ref, middle_grad_ref, out_ref, part_ref = refs
    back = recv_ref[...].astype(F32)
    for i in range(3):
        columns = slice(i * LANES, (i + 1) * LANES)
        back = back + mm_nt(jnp.concatenate([ref[:, columns] for ref in piece_refs], axis=1), w_ref[i])
    rows = tokens_ref[...].astype(F32)
    factor = inverse_rms(rows)
    scaled = back * as_line(gain_ref)
    inner = jnp.mean(scaled * rows, axis=-1, keepdims=True)
    out_ref[...] = middle_grad_ref[...] + factor * scaled - rows * (factor * factor * factor * inner)
    part_ref[...] = jnp.sum(back * rows * factor, axis=0, keepdims=True)


def input_grad(pieces, w_qkv, recv, tokens, gain_line, middle_grad):
    count, width = tokens.shape
    columns = pieces[0].shape[1]
    rest = [w_qkv, recv, tokens, gain_line, middle_grad]
    return pl.pallas_call(
        functools.partial(input_grad_kernel, len(pieces)),
        grid=(1,),
        in_specs=[pl.BlockSpec((count, columns), lambda *_: (0, 0))] * len(pieces) + [whole(v.shape) for v in rest],
        out_specs=[whole((count, width)), whole((1, width))],
        out_shape=[jax.ShapeDtypeStruct((count, width), F32), jax.ShapeDtypeStruct((1, width), F32)],
        compiler_params=pltpu.CompilerParams(vmem_limit_bytes=10 * MIB),
        cost_estimate=cost(2 * count * width * columns * len(pieces), 8 << 20),
        name="input_grad",
    )(*pieces, *rest)


def padded(rows):
    return -(-rows // 8) * 8


def gather_kernel(counts, chunk, *refs):
    refs = list(refs)
    sums = []
    for group_counts, joint_count in counts:
        groups = [[refs.pop(0) for _ in range(count)] for count in group_counts]
        joint = [refs.pop(0) for _ in range(joint_count)]
        parts, at = [], 0
        for group in groups:
            columns = slice(at, at + group[0].shape[2])
            total = 0.0
            for ref in group:
                total = total + ref[0].astype(F32)
            for ref in joint:
                total = total + ref[0, :, columns].astype(F32)
            parts.append(total)
            at = columns.stop
        sums.append(jnp.concatenate(parts, axis=1))
    attn_gain_ref, mlp_gain_ref, sums_ref = refs[:3]
    qkv_ref, out_ref, gu_ref, down_ref, columns_ref, pair_ref = refs[3:]
    wide_part, pair_part = sums
    pairs = [pair_part[:, i : i + 4 * LANES] for i in range(0, pair_part.shape[1], 4 * LANES)]
    mats = [
        jnp.concatenate([pair[:, i * LANES : (i + 1) * LANES] for pair in pairs], axis=1) for i in range(4)
    ]
    kinds = [
        jnp.concatenate(
            [
                wide_part[:, j + i * chunk : j + (i + 1) * chunk]
                for j in range(0, wide_part.shape[1], 3 * chunk)
            ],
            axis=1,
        )
        for i in range(3)
    ]
    rows = wide_part.shape[0]
    for i in range(3):
        qkv_ref[i] = mats[i]
    for i in range(2):
        gu_ref[i] = kinds[i]
    out_ref[...] = mats[3]
    down_ref[...] = kinds[2]
    columns_ref[...] = jnp.zeros_like(columns_ref)
    lane = lax.broadcasted_iota(jnp.int32, (1, LANES), 1)
    row_sums = jnp.zeros((rows, LANES), F32)
    for i, value in enumerate((mats[0], mats[1], mats[2], mats[3], kinds[0], kinds[1], kinds[2])):
        squares = value * value
        columns_ref[i : i + 1, 0 : value.shape[1]] = jnp.sum(squares, axis=0, keepdims=True)
        row_sums = jnp.where(lane == i, jnp.sum(squares, axis=1, keepdims=True), row_sums)
    pair_ref[...] = jnp.zeros_like(pair_ref)
    pair_ref[0:rows, :] = row_sums
    at = padded(rows)
    for ref in (attn_gain_ref, mlp_gain_ref):
        for i in range(0, ref.shape[1], LANES):
            pair_ref[at : at + 1, :] = ref[:, i : i + LANES]
            at += 1
    pair_ref[at : at + 1, :] = sums_ref[...]


def gather_own(batches, attn_gain_part, mlp_gain_part, local_sums, heads_width, units, chunk):
    rows = batches[0][0][0][0].shape[1]
    width = attn_gain_part.shape[1]
    pieces = [a for groups, joint in batches for group in [*groups, joint] for a in group]
    counts = [([len(group) for group in groups], len(joint)) for groups, joint in batches]
    lines = [attn_gain_part, mlp_gain_part, local_sums]
    shapes = [(3, rows, heads_width), (rows, heads_width), (2, rows, units), (rows, units)]
    shapes += [(8, max(heads_width, units, width)), (padded(rows) + padded(2 * width // LANES + 1), LANES)]
    return pl.pallas_call(
        functools.partial(gather_kernel, counts, chunk),
        grid=(1,),
        in_specs=[pl.BlockSpec((1,) + a.shape[1:], lambda *_: (0, 0, 0)) for a in pieces]
        + [whole(a.shape) for a in lines],
        out_specs=[whole(s) for s in shapes],
        out_shape=[jax.ShapeDtypeStruct(s, F32) for s in shapes],
        compiler_params=pltpu.CompilerParams(vmem_limit_bytes=5 * MIB),
        cost_estimate=cost(1 << 20, 4 << 20),
        name="gather_own",
    )(*pieces, *lines)


def combine_kernel(rows, width, columns_ref, own_ref, recv_ref, summed_ref, pair_ref):
    pair = own_ref[...] + recv_ref[...]
    pair_ref[...] = pair
    summed_ref[...] = jnp.zeros_like(summed_ref)
    summed_ref[0:8, :] = columns_ref[...]
    summed_ref[7:8, 0:LANES] = jnp.sum(pair[0:rows, :], axis=0, keepdims=True)
    at = padded(rows)
    for line in (8, 9):
        for i in range(0, width, LANES):
            summed_ref[line : line + 1, i : i + LANES] = pair[at : at + 1, :]
            at += 1


def combine(columns, own, recv, rows, width):
    shapes = [(16, columns.shape[1]), own.shape]
    return pl.pallas_call(
        functools.partial(combine_kernel, rows, width),
        out_shape=[jax.ShapeDtypeStruct(s, F32) for s in shapes],
        compiler_params=pltpu.CompilerParams(vmem_limit_bytes=4 * MIB),
        name="combine",
    )(columns, own, recv)


def update_kernel(sizes, *refs):
    (scalar_ref, qkv_ref, out_ref, gu_ref, down_ref, summed_ref, pair_ref) = refs[:7]
    prior_refs, refs = refs[7:11], refs[2:]
    (qkv_cols, out_rows, gu_cols, down_rows, w_qkv, w_out, w_gu, w_down) = refs[9:17]
    (qkv_new, out_new, gu_new, down_new, qkv_cols_new, out_rows_new, gu_cols_new, down_rows_new) = refs[17:25]
    (qkv_rows_new, out_cols_new, gu_rows_new, down_cols_new, attn_gain_ref, mlp_gain_ref, turned, prior_rows_ref) = refs[25:]
    rows = qkv_ref.shape[1]
    width = sizes[0]
    lane = lax.broadcasted_iota(jnp.int32, (1, LANES), 1)
    scalars = as_line(scalar_ref)
    beta = 1.0 - lax.rsqrt(scalars[:, 0:1])
    fresh = 1.0 - beta
    start = lax.rem(width - lax.axis_index("wide") * rows, width)
    prior_rows_ref[...] = jnp.zeros_like(prior_rows_ref)
    at = 0
    for ref in prior_refs:
        value = as_line(ref) if len(ref.shape) == 1 else ref[...]
        prior_rows_ref[at : at + value.shape[0], :] = value
        at += value.shape[0]
    own = pltpu.roll(prior_rows_ref[...], start, 1)[:, 0:LANES]
    turned[...] = jnp.zeros_like(turned)
    turned[0:8, :] = own
    prior_columns = turned[...].T
    gains = pltpu.roll(summed_ref[8:16, 0:width], start, 1)
    attn_gain_ref[...] = jnp.reshape(gains[0:1, 0:rows], (rows,))
    mlp_gain_ref[...] = jnp.reshape(gains[1:2, 0:rows], (rows,))
    sums = pair_ref[pl.ds(padded(rows) + 2 * width // LANES, 1), :]
    totals = summed_ref[7:8, 0:LANES]
    all_rows = jnp.zeros((rows, LANES), F32)
    priors = [qkv_cols[0:1], qkv_cols[1:2], qkv_cols[2:3], as_line(out_rows), gu_cols[0:1], gu_cols[1:2], as_line(down_rows)]
    for i in range(7):
        across = sizes[1 + i]
        entries = float(across * width)
        row_new = beta * prior_columns[0:rows, i : i + 1] + fresh * (pair_ref[0:rows, i : i + 1] / across + TINIEST)
        count = priors[i].shape[1]
        col_new = beta * priors[i] + fresh * (summed_ref[i : i + 1, 0:count] / width + TINIEST)
        all_rows = jnp.where(lane == i, row_new, all_rows)
        if i in (3, 6):
            at = 7 + (i == 6)
            prior_mean = sums[:, at : at + 1] / across
        else:
            prior_mean = jnp.mean(prior_rows_ref[i : i + 1, :], axis=1, keepdims=True)
        mean = beta * prior_mean + fresh * (totals[:, i : i + 1] / entries + TINIEST)
        rate = scalars[:, 1:2] * jnp.sqrt(sums[:, i : i + 1] / entries)
        step = lax.rsqrt(row_new * col_new / mean)
        if i in (3, 6):
            gradient_ref, weight_ref, new_ref = ((out_ref, w_out, out_new), (down_ref, w_down, down_new))[i == 6]
            new_ref[...] = (weight_ref[...].astype(F32) - rate * (gradient_ref[...] * step)).astype(BF16)
            (out_rows_new, down_rows_new)[i == 6][...] = jnp.reshape(col_new, (count,))
        else:
            at = i if i < 3 else i - 4
            gradient_ref, weight_ref, new_ref = (qkv_ref, w_qkv, qkv_new) if i < 3 else (gu_ref, w_gu, gu_new)
            new_ref[at] = (weight_ref[at].astype(F32) - rate * (gradient_ref[at] * step)).astype(BF16)
            (qkv_cols_new if i < 3 else gu_cols_new)[at : at + 1] = col_new
    turned[0:rows, :] = all_rows
    rows_new = turned[...].T
    qkv_rows_new[...] = rows_new[0:3, 0:rows]
    out_cols_new[...] = jnp.reshape(rows_new[3:4, 0:rows], (rows,))
    gu_rows_new[...] = rows_new[4:6, 0:rows]
    down_cols_new[...] = jnp.reshape(rows_new[6:7, 0:rows], (rows,))


def update(step_count, learn_rate, grads, summed, pair, prior_rows, col_priors, weights, sizes):
    rows = grads[0].shape[1]
    scalars = jnp.where(jnp.arange(LANES) == 0, step_count.astype(F32), learn_rate)
    inputs = [scalars, *grads, summed, pair, *prior_rows, *col_priors, *weights]
    shapes = [(3, sizes[1] // 2), (sizes[4] // 2,), (2, sizes[5] // 2), (sizes[7] // 2,)]
    shapes += [(3, rows), (rows,), (2, rows), (rows,), (rows,), (rows,)]
    out_shape = [jax.ShapeDtypeStruct(w.shape, BF16) for w in weights]
    out_shape += [jax.ShapeDtypeStruct(s, F32) for s in shapes]
    return pl.pallas_call(
        functools.partial(update_kernel, sizes),
        grid=(1,),
        in_specs=[whole(a.shape) for a in inputs],
        out_specs=[whole(s.shape) for s in out_shape],
        scratch_shapes=[pltpu.VMEM((LANES, LANES), F32), pltpu.VMEM((8, sizes[0]), F32)],
        out_shape=out_shape,
        compiler_params=pltpu.CompilerParams(vmem_limit_bytes=8 * MIB),
        cost_estimate=cost(1 << 20, 4 << 20),
        name="update",
    )(*inputs)


def weights_kernel(rows, qkv_ref, out_ref, gu_ref, down_ref, out_rows_ref, down_rows_ref, line_ref, *refs):
    qkv_own, out_own, gu_own, down_own, sums, qkv_total, gu_total = refs
    step = pl.program_id(0)
    values = [qkv_ref.at[0], qkv_ref.at[1], qkv_ref.at[2], out_ref, gu_ref.at[0], gu_ref.at[1], down_ref]
    width = out_ref.shape[1]
    block = qkv_ref.shape[1]
    start = lax.axis_index("wide") * rows

    @pl.when(step == 0)
    def _():
        for ref in (sums, qkv_total, gu_total):
            ref[...] = jnp.zeros_like(ref)

    def chosen(first, count):
        shape = (qkv_total.shape[1], count)
        own = lax.broadcasted_iota(jnp.int32, shape, 0) + start
        return jnp.where(lax.broadcasted_iota(jnp.int32, shape, 1) + first == own, 1.0, 0.0).astype(BF16)

    for i, ref in enumerate(values):
        count = ref.shape[1]
        value = ref[...].astype(F32)
        sums[i : i + 1, 0:count] += jnp.sum(value * value, axis=0, keepdims=True)
    across = chosen(0, width)
    for ref, own_ref in ((out_ref, out_own), (down_ref, down_own)):
        own_ref[...] = mm_nt(across, ref[...])[0:rows].astype(BF16)
    below = chosen(step * block, block)
    for ref, total in ((qkv_ref, qkv_total), (gu_ref, gu_total)):
        for i in range(ref.shape[0]):
            total[i] += mm(below, ref[i])

    @pl.when(step == pl.num_programs(0) - 1)
    def _():
        lane = lax.broadcasted_iota(jnp.int32, (1, LANES), 1)
        line = jnp.zeros((1, LANES), F32)
        for i in range(7):
            line = jnp.where(lane == i, jnp.sum(sums[i : i + 1, :], axis=1, keepdims=True), line)
        for i, ref in enumerate((out_rows_ref, down_rows_ref)):
            line = jnp.where(lane == 7 + i, jnp.sum(as_line(ref), axis=1, keepdims=True), line)
        line_ref[...] = line
        qkv_own[...] = qkv_total[:, 0:rows, :].astype(BF16)
        gu_own[...] = gu_total[:, 0:rows, :].astype(BF16)


def weights_call(w_qkv, w_out, w_gu, w_down, out_rows, down_rows, n_wide):
    width = w_out.shape[1]
    rows, held = width // n_wide, -(-(width // n_wide) // 16) * 16
    heads_width, units = w_qkv.shape[2], w_gu.shape[2]
    steps = 3 if heads_width % (3 * LANES) == 0 and units % (3 * LANES) == 0 else 1
    each = lambda n: n // steps
    shapes = [(3, rows, heads_width), (rows, heads_width), (2, rows, units), (rows, units)]
    line, *own = pl.pallas_call(
        functools.partial(weights_kernel, rows),
        grid=(steps,),
        in_specs=[
            pl.BlockSpec((3, each(width), heads_width), lambda j: (0, j, 0)),
            pl.BlockSpec((each(heads_width), width), lambda j: (j, 0)),
            pl.BlockSpec((2, each(width), units), lambda j: (0, j, 0)),
            pl.BlockSpec((each(units), width), lambda j: (j, 0)),
            whole(out_rows.shape),
            whole(down_rows.shape),
        ],
        out_specs=[
            whole((1, LANES)),
            whole(shapes[0]),
            pl.BlockSpec((rows, each(heads_width)), lambda j: (0, j)),
            whole(shapes[2]),
            pl.BlockSpec((rows, each(units)), lambda j: (0, j)),
        ],
        out_shape=[jax.ShapeDtypeStruct((1, LANES), F32)] + [jax.ShapeDtypeStruct(shape, BF16) for shape in shapes],
        scratch_shapes=[
            pltpu.VMEM((8, max(width, units)), F32),
            pltpu.VMEM((3, held, heads_width), F32),
            pltpu.VMEM((2, held, units), F32),
        ],
        compiler_params=pltpu.CompilerParams(vmem_limit_bytes=20 * MIB),
        cost_estimate=cost(1 << 20, 7 << 20),
        name="weights",
    )(w_qkv, w_out, w_gu, w_down, out_rows, down_rows)
    return line, own


def after(values, *others):
    return lax.optimization_barrier((values, *others))[0]


def far(values):
    return pltpu.with_memory_space_constraint(values, pltpu.HBM)


def body(
    n_wide,
    tokens,
    plot_slot,
    patch_mask,
    cotangent,
    gain_attn,
    w_qkv,
    w_out,
    gain_mlp,
    w_gu,
    w_down,
    qkv_rows,
    qkv_cols,
    out_rows,
    out_cols,
    gu_rows,
    gu_cols,
    down_rows,
    down_cols,
    step_count,
    learn_rate,
):
    width = tokens.shape[1]
    heads_width, units = w_out.shape[0], w_down.shape[0]
    rows_each = width // n_wide
    chunk = 256
    tokens_other = swap(tokens)
    carried = project(0, far(tokens), far(gain_attn), far(w_qkv), [])
    normed_t, qkv = project(1, tokens_other, gain_attn, w_qkv, carried)
    sent = after((w_out, w_gu, w_down), tokens_other, *carried)
    w_out_other, w_gu_other, w_down_other = swap(sent[0]), swap(sent[1]), swap(sent[2])
    mixed_own, mixed_other, kept, keys = attention(qkv, plot_slot, patch_mask)
    mixed_recv = swap(mixed_other)
    steps = units // chunk // 2

    (middle, *handed), (part_other,) = middle_call(
        True,
        None,
        [tokens, mixed_own, mixed_recv, w_out, w_out_other, gain_mlp, cotangent, keys],
        w_gu_other,
        w_down_other,
        0,
        steps,
        None,
        n_wide,
        chunk,
    )
    part_first = swap(part_other)
    totals, (part_other,) = middle_call(
        False, None, handed, w_gu_other, w_down_other, steps, steps, None, n_wide, chunk
    )
    part_second = swap(part_other)
    handed = [*handed[:4], *totals]
    totals, parts = middle_call(
        False, False, handed, w_gu, w_down, 0, steps, part_first, n_wide, chunk
    )
    wide_a = [parts[0], stage_exchange(parts[1], 0, n_wide)]
    handed = [*handed[:4], *totals]
    (mixed_out, middle_grad, attn_seed, mlp_gain_part), parts = middle_call(
        False, True, [*handed, middle, gain_mlp], w_gu, w_down, steps, steps, part_second, n_wide, chunk
    )
    wide_b = [parts[0], stage_exchange(parts[1], 0, n_wide)]
    mixed_grad, seed_t = seeds_call(attn_seed, swap(attn_seed), w_out)
    mixed_grad = after(mixed_grad, wide_a[1])

    pairs = heads_width // LANES
    back = functools.partial(
        attention_back,
        qkv=qkv,
        mixed_own=mixed_own,
        mixed_other=mixed_other,
        kept=kept,
        keys=keys,
        normed_t=normed_t,
        seed_t=seed_t,
        n_wide=n_wide,
    )
    pieces = []
    piece, carried = back(0, 0, pairs - 1, [], grad=mixed_grad)
    pieces.append(piece)
    weights = after((w_qkv, w_out, w_gu, w_down, out_rows, down_rows), piece)
    local_sums, own_weights = weights_call(*weights, n_wide)
    wide_batch = Scatter([wide_a, wide_b], n_wide)
    mixed_grad = after(mixed_grad, wide_batch.turn(piece, local_sums))
    wide_batch.go()
    for pair in range(1, pairs - 1):
        piece, carried = back(pair, pair, pairs - 1, carried, grad=mixed_grad)
        pieces.append(piece)
    keep, send = kept_and_sent(carried, n_wide)
    first = [keep, stage_exchange(send, 0, n_wide)]
    mixed_grad = after(mixed_grad, send)
    piece, carried = back(pairs - 1, 0, 1, [], grad=mixed_grad)
    pieces.append(piece)
    keep, send = kept_and_sent(carried, n_wide)
    last = [keep, stage_exchange(send, 0, n_wide)]
    pair_batch = Scatter([first, last], n_wide)
    batches = wide_batch.finish(pair_batch)
    back_other = swap(input_other(pieces, w_qkv))
    tokens_grad, attn_gain_part = input_grad(pieces, w_qkv, back_other, tokens, gain_attn, middle_grad)

    *grads, columns, pair = gather_own(
        batches, attn_gain_part, mlp_gain_part, local_sums, heads_width, units, chunk
    )
    summed, pair = combine(columns, pair, swap(pair), rows_each, width)
    for stage in range(n_wide.bit_length() - 1):
        summed = summed + stage_exchange(summed, stage, n_wide)
    outs = update(
        step_count,
        learn_rate,
        [far(grad) for grad in grads],
        summed,
        pair,
        [qkv_rows, out_cols, gu_rows, down_cols],
        [qkv_cols, out_rows, gu_cols, down_rows],
        own_weights,
        [width] + [2 * heads_width] * 4 + [2 * units] * 3,
    )
    qkv_new, out_new, gu_new, down_new, qkv_cols_new, out_rows_new, gu_cols_new, down_rows_new = outs[:8]
    qkv_rows_new, out_cols_new, gu_rows_new, down_cols_new, attn_gain_grad, mlp_gain_grad = outs[8:]
    qkv_grad, out_grad, gu_grad, down_grad = grads
    return (
        mixed_out,
        tokens_grad,
        attn_gain_grad,
        qkv_grad,
        out_grad.T,
        mlp_gain_grad,
        gu_grad,
        down_grad.T,
        qkv_new,
        out_new.T,
        gu_new,
        down_new.T,
        qkv_rows_new,
        qkv_cols_new,
        out_rows_new,
        out_cols_new,
        gu_rows_new,
        gu_cols_new,
        down_rows_new,
        down_cols_new,
    )


def solution(mesh):
    in_specs = (
        P(("wide", "narrow"), None),
        P("wide"),
        P("wide"),
        P(("wide", "narrow"), None),
        P(),
        P(None, None, "narrow"),
        P("narrow", None),
        P(),
        P(None, None, "narrow"),
        P("narrow", None),
        P(),
        P(None, "narrow"),
        P("narrow"),
        P(),
        P(),
        P(None, "narrow"),
        P("narrow"),
        P(),
        P(),
        P(),
    )
    out_specs = (
        P(("wide", "narrow"), None),
        P(("wide", "narrow"), None),
        P("wide"),
        P(None, "wide", "narrow"),
        P("narrow", "wide"),
        P("wide"),
        P(None, "wide", "narrow"),
        P("narrow", "wide"),
        P(None, "wide", "narrow"),
        P("narrow", "wide"),
        P(None, "wide", "narrow"),
        P("narrow", "wide"),
        P(None, "wide"),
        P(None, "narrow"),
        P("narrow"),
        P("wide"),
        P(None, "wide"),
        P(None, "narrow"),
        P("narrow"),
        P("wide"),
    )
    return jax.shard_map(
        functools.partial(body, mesh.shape["wide"]),
        mesh=mesh,
        in_specs=in_specs,
        out_specs=out_specs,
        check_vma=False,
    )
```

```python
import functools
import math

import jax
import jax.numpy as jnp
from jax import lax
from jax.experimental import pallas as pl
from jax.experimental.pallas import tpu as pltpu
from jax.sharding import PartitionSpec as P

DH = 64
LANES = 128
EPSILON = 1e-06
TINIEST = 1e-30
NEGATIVE = -1e30
F32 = jnp.float32
BF16 = jnp.bfloat16
ROOT = math.sqrt(2.0 / math.pi)
CUBE = 0.044715
MIB = 1024 * 1024
LIVE = 5


def mm(a, b):
    return jnp.dot(a, b, preferred_element_type=F32)


def mm_nt(a, b):
    return lax.dot_general(a, b, (((1,), (1,)), ((), ())), preferred_element_type=F32)


def whole(shape):
    return pl.BlockSpec(shape, lambda *_: (0,) * len(shape))


def cost(flops, nbytes):
    return pl.CostEstimate(flops=int(flops), bytes_accessed=int(nbytes), transcendentals=0)


def inverse_rms(rows):
    return lax.rsqrt(jnp.mean(rows * rows, axis=-1, keepdims=True) + EPSILON)


def three_terms(values):
    high = values.astype(BF16)
    rest = values - high.astype(F32)
    middle = rest.astype(BF16)
    return high, middle, (rest - middle.astype(F32)).astype(BF16)


WIDE, PAIRS = 0, 1


def bit_orders(n_wide, kind):
    bits = n_wide.bit_length() - 1
    straight = list(range(bits))
    if bits <= 2:
        return straight, straight
    if kind == WIDE:
        return straight, [1, 0] + straight[2:]
    return straight, straight[1:-1] + straight[:1] + straight[-1:]


def slot_masks(n_wide, kind):
    bits = n_wide.bit_length() - 1
    return [
        [sum(1 << bit for stage, bit in enumerate(order) if slot >> (bits - 1 - stage) & 1) for slot in range(n_wide)]
        for order in bit_orders(n_wide, kind)
    ]


def slot_row(slot, n_wide, kind, turned=0):
    masks = slot_masks(n_wide, kind)
    wide, core = lax.axis_index("wide"), lax.axis_index("narrow")
    first, second = masks[turned][slot], masks[1 - turned][slot]
    return jnp.bitwise_xor(wide, first + (second - first) * core)


def stage_exchange(values, stage, n_wide, kind):
    orders = bit_orders(n_wide, kind)
    pairs = []
    for wide in range(n_wide):
        for core in range(2):
            pairs.append((wide * 2 + core, (wide ^ (1 << orders[core][stage])) * 2 + core))
    return lax.ppermute(values, ("wide", "narrow"), pairs)


def swap(values):
    return lax.ppermute(values, "narrow", [(0, 1), (1, 0)])


def write_slots(kind, turned, n_wide, held_ref, targets, rows_each):
    if targets[0].ndim == 2:
        targets[0][...] = held_ref[...].astype(BF16)
        return
    slot = 0
    for target in targets:
        for at in range(target.shape[0]):
            start = pl.multiple_of(slot_row(slot, n_wide, kind, turned) * rows_each, 16)
            target[at] = held_ref[pl.ds(start, rows_each), :].astype(BF16)
            slot += 1


def in_slots(part, n_wide, kind):
    rows = jnp.stack([slot_row(slot, n_wide, kind) for slot in range(n_wide)])
    return jnp.take(part.reshape(n_wide, -1, part.shape[-1]), rows, axis=0)


def as_line(ref):
    return jnp.reshape(ref[...], (1, ref.shape[0]))


def project_kernel(carried, rows_ref, gain_ref, w_ref, *refs):
    normed_t_ref, projected_ref = refs[carried:]
    rows = rows_ref[...].astype(F32)
    normed = (rows * inverse_rms(rows) * as_line(gain_ref)).astype(BF16)
    normed_t_ref[...] = normed.T
    for i in range(3):
        projected_ref[i] = mm(normed, w_ref[i]).astype(BF16)


def project(half, tokens, gain, w_qkv, carried):
    count, width = tokens.shape
    out = w_qkv.shape[2]
    inputs = [tokens, gain, w_qkv]
    return pl.pallas_call(
        functools.partial(project_kernel, len(carried)),
        grid=(1,),
        in_specs=[whole(v.shape) for v in inputs] + [pl.BlockSpec(memory_space=pl.ANY)] * len(carried),
        out_specs=[
            pl.BlockSpec((width, count), lambda *_: (0, half)),
            pl.BlockSpec((3, count, out), lambda *_: (0, half, 0)),
        ],
        out_shape=[
            jax.ShapeDtypeStruct((width, 2 * count), BF16),
            jax.ShapeDtypeStruct((3, 2 * count, out), BF16),
        ],
        input_output_aliases={len(inputs) + i: i for i in range(len(carried))},
        cost_estimate=cost(6 * count * width * out, 4 * count * width),
        compiler_params=pltpu.CompilerParams(vmem_limit_bytes=8 * MIB),
        name="project",
    )(*inputs, *carried)


def key_lines(slot_ref, mask_ref, core):
    slot, mask = as_line(slot_ref), as_line(mask_ref)
    length = mask.shape[1]
    turned = lambda values: pltpu.roll(values, length // 2, 1)
    live = mask + (turned(mask) - mask) * core
    same = jnp.where(slot == turned(slot), live, 0)
    first = lax.broadcasted_iota(jnp.int32, (1, length), 1) < length // 2
    for_own = jnp.where(jnp.where(first, live, same) > 0, 0.0, NEGATIVE)
    for_other = jnp.where(jnp.where(first, same, live) > 0, 0.0, NEGATIVE)
    return for_own, for_other, live.astype(F32)


def column(line):
    return jnp.broadcast_to(line, (LANES, line.shape[1])).T


def attention_kernel(qkv_ref, slot_ref, mask_ref, own_ref, other_ref, kept_ref, keys_ref, held, *, block):
    lane = lax.broadcasted_iota(jnp.int32, (1, LANES), 1)
    lows = (lane < DH, lane >= DH)
    within = jnp.bitwise_and(lane, DH - 1)

    @pl.when(pl.program_id(0) == 0)
    def _():
        ones = jnp.where((within >= 2) & (within < 5), 1.0, 0.0)
        for_own, for_other, live = key_lines(slot_ref, mask_ref, lax.axis_index("narrow"))
        bias = jnp.where(within == 1, column(for_other), jnp.where(within == LIVE, column(live), ones))
        keys_ref[...] = jnp.where(within == 0, column(for_own), bias).astype(BF16)

    for head in range(2):
        held[head] = jnp.where(lows[head], qkv_ref[1], keys_ref[...])
        held[2 + head] = jnp.where(lows[head], qkv_ref[2], jnp.ones((1, LANES), BF16))
    half = own_ref.shape[0]
    for part, out_ref in enumerate((own_ref, other_ref)):

        def step(i, carry, part=part, out_ref=out_ref):
            inside = pl.ds(pl.multiple_of(i * block, block), block)
            rows = pl.ds(pl.multiple_of(part * half + i * block, block), block)
            queries = qkv_ref[0, rows, :] * jnp.asarray(1.0 / math.sqrt(DH), BF16)
            constants = jnp.where(within == part, 1.0, 0.0).astype(BF16)
            results = []
            for head in range(2):
                scores = mm_nt(jnp.where(lows[head], queries, constants), held[head])
                highest = jnp.max(scores, axis=1, keepdims=True)
                weights = jnp.exp(scores - highest).astype(BF16)
                mixed = mm(weights, held[2 + head])
                results.append(mixed / pltpu.roll(mixed, DH, 1))
                high, middle, low = three_terms(highest + jnp.log(mixed))
                base = DH * (1 - head)
                constants_back = jnp.where(
                    lane == base + 2,
                    -high,
                    jnp.where(lane == base + 3, -middle, jnp.where(lane == base + 4, -low, constants)),
                )
                kept_ref[head, rows, :] = jnp.where(lows[head], queries, constants_back)
            out_ref[inside, :] = jnp.where(lows[0], results[0], results[1]).astype(BF16)
            return carry

        lax.fori_loop(0, half // block, step, 0)


def attention(qkv, plot_slot, patch_mask, block=512):
    length, width = qkv.shape[1:]
    pairs, half = width // LANES, length // 2
    return pl.pallas_call(
        functools.partial(attention_kernel, block=block),
        grid=(pairs,),
        in_specs=[
            pl.BlockSpec((3, length, LANES), lambda p: (0, 0, p)),
            whole(plot_slot.shape),
            whole(patch_mask.shape),
        ],
        out_specs=[
            pl.BlockSpec((half, LANES), lambda p: (0, p)),
            pl.BlockSpec((half, LANES), lambda p: (0, p)),
            pl.BlockSpec((2, length, LANES), lambda p: (p, 0, 0)),
            whole((length, LANES)),
        ],
        scratch_shapes=[pltpu.VMEM((4, length, LANES), BF16)],
        out_shape=[
            jax.ShapeDtypeStruct((half, width), BF16),
            jax.ShapeDtypeStruct((half, width), BF16),
            jax.ShapeDtypeStruct((2 * pairs, length, LANES), BF16),
            jax.ShapeDtypeStruct((length, LANES), BF16),
        ],
        cost_estimate=cost(16 * pairs * length * length * LANES, 10 * length * width),
        compiler_params=pltpu.CompilerParams(vmem_limit_bytes=11 * MIB),
        name="attention",
    )(qkv, plot_slot, patch_mask)


def middle_kernel(first, last, rows_each, n_wide, *refs):
    refs = list(refs)
    take = lambda n: [refs.pop(0) for _ in range(n)]
    if first:
        (tokens_ref, own_ref, recv_ref, w_own_ref, w_recv_ref, gain_ref, cot_ref, keys_ref) = take(8)
    else:
        (normed, normed_t, seed, seed_t, total_in, back_in) = take(6)
        if last:
            (middle_ref, gain_ref) = take(2)
    (gu_ref, down_ref) = take(2)
    if first:
        (middle_ref, normed, normed_t, seed, seed_t) = take(5)
    if last:
        (out_ref, grad_ref, attn_seed_ref, gain_part_ref) = take(4)
    else:
        (total_ref, back_ref) = take(2)
    part_refs = take(len(refs) - (3 if last else 1))
    (held,) = take(1)
    if last:
        (total_ref, back_ref) = take(2)
    step = pl.program_id(0)

    @pl.when(step == 0)
    def _():
        if first:
            middle = tokens_ref[...].astype(F32) + (
                mm(own_ref[...], w_own_ref[...]) + mm(recv_ref[...], w_recv_ref[...])
            )
            middle_ref[...] = middle
            total_ref[...] = middle
            back_ref[...] = jnp.zeros_like(back_ref)
            live = keys_ref[...].astype(F32)[:, LIVE : LIVE + 1]
            seed_value = (cot_ref[...].astype(F32) * live).astype(BF16)
            seed[...] = seed_value
            seed_t[...] = seed_value.T
            value = (middle * inverse_rms(middle) * as_line(gain_ref)).astype(BF16)
            normed[...] = value
            normed_t[...] = value.T
        else:
            total_ref[...] = total_in[...]
            back_ref[...] = back_in[...]

    gate = mm(normed[...], gu_ref[0])
    up = mm(normed[...], gu_ref[1])
    bent = jnp.tanh(ROOT * (gate + CUBE * gate * gate * gate))
    soft = 0.5 * gate * (1.0 + bent)
    slope = 0.5 * (1.0 + bent) + 0.5 * gate * (1.0 - bent * bent) * (ROOT * (1.0 + 3.0 * CUBE * gate * gate))
    hidden = (soft * up).astype(BF16)
    hidden_grad = mm_nt(seed[...], down_ref[...])
    gate_grad = (hidden_grad * up * slope).astype(BF16)
    up_grad = (hidden_grad * soft).astype(BF16)
    total_ref[...] += mm(hidden, down_ref[...])
    back_ref[...] += mm_nt(gate_grad, gu_ref[0]) + mm_nt(up_grad, gu_ref[1])
    chunk = gate.shape[1]
    held[:, 0:chunk] = mm(normed_t[...], gate_grad)
    held[:, chunk : 2 * chunk] = mm(normed_t[...], up_grad)
    held[:, 2 * chunk : 3 * chunk] = mm(seed_t[...], hidden)
    write_slots(WIDE, int(last is None), n_wide, held, part_refs, rows_each)

    if last:

        @pl.when(step == pl.num_programs(0) - 1)
        def _():
            out_ref[...] = total_ref[...].astype(BF16)
            middle = middle_ref[...]
            factor = inverse_rms(middle)
            back = back_ref[...]
            scaled = back * as_line(gain_ref)
            inner = jnp.mean(scaled * middle, axis=-1, keepdims=True)
            grad = seed[...].astype(F32) + factor * scaled - middle * (factor * factor * factor * inner)
            grad_ref[...] = grad
            attn_seed_ref[...] = grad.astype(BF16)
            gain_part_ref[...] = jnp.sum(back * middle * factor, axis=0, keepdims=True)


def middle_call(first, last, inputs, w_gu, w_down, at, steps, n_wide, chunk):
    count, width = inputs[0].shape
    rows_each = width // n_wide
    tall = rows_each % 16 == 0
    rows, turned = (count, width), (width, count)
    columns = 3 * chunk * steps
    if tall:
        part_specs = [pl.BlockSpec((n_wide, rows_each, 3 * chunk), lambda j, *_: (0, 0, j))]
        part_shapes = [jax.ShapeDtypeStruct((n_wide, rows_each, columns), BF16)]
    else:
        part_specs = [pl.BlockSpec((width, 3 * chunk), lambda j, *_: (0, j))]
        part_shapes = [jax.ShapeDtypeStruct((width, columns), BF16)]
    in_specs = [whole((count, LANES) if v.shape[1:] == (LANES,) else v.shape) for v in inputs] + [
        pl.BlockSpec((2, width, chunk), lambda j, *_: (0, 0, at + j)),
        pl.BlockSpec((chunk, width), lambda j, *_: (at + j, 0)),
    ]
    inputs = [*inputs, w_gu, w_down]
    shape = jax.ShapeDtypeStruct
    scratch = [pltpu.VMEM((width, 3 * chunk), F32)]
    out_shape = []
    if first:
        out_shape += [shape(rows, F32), shape(rows, BF16), shape(turned, BF16), shape(rows, BF16), shape(turned, BF16)]
    if last:
        out_shape += [shape(rows, BF16), shape(rows, F32), shape(rows, BF16), shape((1, width), F32)]
        scratch += [pltpu.VMEM(rows, F32)] * 2
    else:
        out_shape += [shape(rows, F32)] * 2
    outs = pl.pallas_call(
        functools.partial(middle_kernel, first, last, rows_each, n_wide),
        grid=(steps,),
        in_specs=in_specs,
        out_specs=[whole(s.shape) for s in out_shape] + part_specs,
        scratch_shapes=scratch,
        out_shape=out_shape + part_shapes,
        compiler_params=pltpu.CompilerParams(vmem_limit_bytes=(20 if last else 14) * MIB),
        cost_estimate=cost((1 if last else 36) * count * width * chunk * steps, width * chunk * steps),
        name="middle",
    )(*inputs)
    return outs[: len(out_shape)], outs[-1]


def slotted(part, n_wide):
    return part if part.ndim == 3 else in_slots(part, n_wide, WIDE)


def seeds_kernel(own_ref, other_ref, w_ref, grad_ref, seed_t_ref):
    count = own_ref.shape[0]
    for half, seed_ref in enumerate((own_ref, other_ref)):
        at = slice(half * count, (half + 1) * count)
        grad_ref[at, :] = mm_nt(seed_ref[...], w_ref[...]).astype(BF16)
        seed_t_ref[:, at] = seed_ref[...].T


def seeds_call(own, other, w_out):
    count, width = own.shape
    out = w_out.shape[0]
    return pl.pallas_call(
        seeds_kernel,
        out_shape=[
            jax.ShapeDtypeStruct((2 * count, out), BF16),
            jax.ShapeDtypeStruct((width, 2 * count), BF16),
        ],
        cost_estimate=cost(16 * count * width * width, 8 * count),
        compiler_params=pltpu.CompilerParams(vmem_limit_bytes=4 * MIB),
        name="seeds",
    )(own, other, w_out)


def attention_back_kernel(block, rows_each, n_wide, split, carried, *refs):
    refs = list(refs)
    (qkv_ref, grad_ref, mixed_own_ref, mixed_other_ref, kept_ref, keys_ref) = refs[:6]
    (normed_t_ref, seed_t_ref) = refs[6:8]
    refs = refs[8 + carried :]
    pieces = refs.pop(0)
    part_refs = [refs.pop(0) for _ in range(split)]
    grads, queries, query_total, mixed, held = refs
    lane = lax.broadcasted_iota(jnp.int32, (1, LANES), 1)
    lows = (lane < DH, lane >= DH)
    nothing = jnp.zeros((1, LANES), BF16)
    length = grad_ref.shape[0]
    half = length // 2
    mixed[0:half, :] = mixed_own_ref[...]
    mixed[half:length, :] = mixed_other_ref[...]
    product = grad_ref[...].astype(F32) * mixed[...].astype(F32)
    for head in range(2):
        base = DH * (1 - head)
        dots = jnp.sum(jnp.where(lows[head], product, 0.0), axis=1, keepdims=True)
        high, middle, low = three_terms(dots)
        constants = jnp.where(
            lane == base + 2,
            -high,
            jnp.where(lane == base + 3, -middle, jnp.where(lane == base + 4, -low, nothing)),
        )
        grads[head] = jnp.where(lows[head], grad_ref[...], constants)
        grads[2 + head] = jnp.where(lows[head], grad_ref[...], nothing)
        queries[head] = jnp.where(lows[head], kept_ref[head], nothing)
    query_total[...] = jnp.zeros_like(query_total)

    def step(i, carry):
        rows = pl.ds(pl.multiple_of(i * block, block), block)
        keys, values, constants = qkv_ref[1, rows, :], qkv_ref[2, rows, :], keys_ref[rows, :]
        key_grad, value_grad = [], []
        for head in range(2):
            base = DH * (1 - head)
            ones = jnp.where((lane >= base + 2) & (lane < base + 5), 1.0, 0.0).astype(BF16)
            keys_only = jnp.where(lows[head], keys, nothing) * jnp.asarray(1.0 / math.sqrt(DH), BF16)
            weights = jnp.exp(mm_nt(jnp.where(lows[head], keys, constants), kept_ref[head]))
            score_grads = weights * mm_nt(jnp.where(lows[head], values, ones), grads[head])
            score_grads = score_grads.astype(BF16)
            value_grad.append(mm(weights.astype(BF16), grads[2 + head]))
            key_grad.append(mm(score_grads, queries[head]))
            query_total[...] += mm(keys_only.T, score_grads)
        pieces[rows, LANES : 2 * LANES] = (key_grad[0] + key_grad[1]).astype(BF16)
        pieces[rows, 2 * LANES : 3 * LANES] = (value_grad[0] + value_grad[1]).astype(BF16)
        return carry

    lax.fori_loop(0, length // block, step, 0)
    pieces[:, 0:LANES] = query_total[...].T.astype(BF16)
    held[:, 0 : 3 * LANES] = mm(normed_t_ref[...], pieces[...])
    held[:, 3 * LANES : 4 * LANES] = mm(seed_t_ref[...], mixed[...])
    write_slots(PAIRS, 0, n_wide, held, part_refs, rows_each)


def attention_back(pair, at, total, carried, qkv, grad, mixed_own, mixed_other, kept, keys, normed_t, seed_t, n_wide, block=512):
    length = qkv.shape[1]
    half = length // 2
    width = normed_t.shape[0]
    rows_each = width // n_wide
    tall = rows_each % 16 == 0
    columns = 4 * LANES
    if tall:
        part_specs = [pl.BlockSpec((n_wide // 2, rows_each, columns), lambda p, *_: (0, 0, at))] * 2
        part_shapes = [jax.ShapeDtypeStruct((n_wide // 2, rows_each, total * columns), BF16)] * 2
    else:
        part_specs = [pl.BlockSpec((width, columns), lambda p, *_: (0, at))]
        part_shapes = [jax.ShapeDtypeStruct((width, total * columns), BF16)]
    in_specs = [
        pl.BlockSpec((3, length, LANES), lambda p, *_: (0, 0, pair)),
        pl.BlockSpec((length, LANES), lambda p, *_: (0, pair)),
        pl.BlockSpec((half, LANES), lambda p, *_: (0, pair)),
        pl.BlockSpec((half, LANES), lambda p, *_: (0, pair)),
        pl.BlockSpec((2, length, LANES), lambda p, *_: (pair, 0, 0)),
        whole((length, LANES)),
        whole((width, length)),
        whole((width, length)),
    ]
    inputs = [qkv, grad, mixed_own, mixed_other, kept, keys, normed_t, seed_t]
    aliases = {len(inputs) + i: 1 + i for i in range(len(carried))}
    outs = pl.pallas_call(
        functools.partial(attention_back_kernel, block, rows_each, n_wide, len(part_specs), len(carried)),
        grid=(1,),
        in_specs=in_specs + [pl.BlockSpec(memory_space=pl.ANY)] * len(carried),
        out_specs=[whole((length, 3 * LANES))] + part_specs,
        scratch_shapes=[
            pltpu.VMEM((4, length, LANES), BF16),
            pltpu.VMEM((2, length, LANES), BF16),
            pltpu.VMEM((LANES, length), F32),
            pltpu.VMEM((length, LANES), BF16),
            pltpu.VMEM((width, columns), F32),
        ],
        out_shape=[jax.ShapeDtypeStruct((length, 3 * LANES), BF16)] + part_shapes,
        input_output_aliases=aliases,
        compiler_params=pltpu.CompilerParams(vmem_limit_bytes=15 * MIB),
        cost_estimate=cost(50 * length * length * LANES, 16 * length * LANES),
        name="attention_back",
    )(*inputs, *carried)
    return outs[0], list(outs[1:])


def kept_and_sent(parts, n_wide):
    if len(parts) == 2:
        return parts
    slots = in_slots(parts[0], n_wide, PAIRS)
    return slots[: n_wide // 2], slots[n_wide // 2 :]


def turn_kernel(counts, *refs):
    *refs, out_ref = refs
    groups = [[refs.pop(0) for _ in range(count)] for count in counts]

    def step(slot, carry):
        at = 0
        for group in groups:
            columns = slice(at, at + group[0].shape[2])
            total = 0.0
            for ref in group:
                total = total + ref[slot].astype(F32)
            for ref in refs:
                total = total + ref[slot, :, columns].astype(F32)
            out_ref[slot, :, columns] = total.astype(BF16)
            at = columns.stop
        return carry

    lax.fori_loop(0, out_ref.shape[0], step, 0)


class Scatter:
    def __init__(self, kind, groups, n_wide, stage):
        self.kind, self.groups, self.joint, self.n_wide, self.stage, self.slots = kind, groups, [], n_wide, stage, n_wide >> stage

    def turn(self, *earlier):
        self.slots //= 2
        pieces = [a for group in self.groups for a in group] + self.joint
        if earlier:
            pieces[-1] = after(pieces[-1], *earlier)
        rows = pieces[0].shape[1]
        shape = (self.slots, rows, sum(group[0].shape[2] for group in self.groups))
        self.send = pl.pallas_call(
            functools.partial(turn_kernel, [len(group) for group in self.groups]),
            grid=(1,),
            in_specs=[pl.BlockSpec((self.slots,) + a.shape[1:], lambda *_: (1, 0, 0)) for a in pieces],
            out_specs=whole(shape),
            out_shape=jax.ShapeDtypeStruct(shape, BF16),
            compiler_params=pltpu.CompilerParams(vmem_limit_bytes=8 * MIB),
            cost_estimate=cost(math.prod(shape), 4 * math.prod(shape)),
            name="turn",
        )(*pieces)
        return self.send

    def go(self):
        self.joint.append(stage_exchange(self.send, self.stage, self.n_wide, self.kind))
        self.stage += 1

    def finish(self, other):
        while other.slots > 1:
            earlier = []
            if self.slots > 1:
                earlier = [self.turn()]
                self.go()
            other.turn(*earlier)
            other.go()
        return [(batch.groups, batch.joint) for batch in (self, other)]


def input_other_kernel(pairs, *refs):
    *piece_refs, w_ref, out_ref = refs
    back = 0.0
    for i in range(3):
        columns = slice(i * LANES, (i + 1) * LANES)
        back = back + mm_nt(jnp.concatenate([ref[:, columns] for ref in piece_refs], axis=1), w_ref[i])
    out_ref[...] = back.astype(BF16)


def input_other(pieces, w_qkv):
    length, columns = pieces[0].shape
    half, width = length // 2, w_qkv.shape[1]
    return pl.pallas_call(
        functools.partial(input_other_kernel, len(pieces)),
        grid=(1,),
        in_specs=[pl.BlockSpec((half, columns), lambda *_: (1, 0))] * len(pieces) + [whole(w_qkv.shape)],
        out_specs=whole((half, width)),
        out_shape=jax.ShapeDtypeStruct((half, width), BF16),
        compiler_params=pltpu.CompilerParams(vmem_limit_bytes=5 * MIB),
        cost_estimate=cost(2 * half * width * columns * len(pieces), 4 << 20),
        name="input_other",
    )(*pieces, w_qkv)


def input_grad_kernel(pairs, *refs):
    piece_refs, refs = refs[:pairs], refs[pairs:]
    w_ref, recv_ref, tokens_ref, gain_ref, middle_grad_ref, out_ref, part_ref = refs
    back = recv_ref[...].astype(F32)
    for i in range(3):
        columns = slice(i * LANES, (i + 1) * LANES)
        back = back + mm_nt(jnp.concatenate([ref[:, columns] for ref in piece_refs], axis=1), w_ref[i])
    rows = tokens_ref[...].astype(F32)
    factor = inverse_rms(rows)
    scaled = back * as_line(gain_ref)
    inner = jnp.mean(scaled * rows, axis=-1, keepdims=True)
    out_ref[...] = middle_grad_ref[...] + factor * scaled - rows * (factor * factor * factor * inner)
    part_ref[...] = jnp.sum(back * rows * factor, axis=0, keepdims=True)


def input_grad(pieces, w_qkv, recv, tokens, gain_line, middle_grad):
    count, width = tokens.shape
    columns = pieces[0].shape[1]
    rest = [w_qkv, recv, tokens, gain_line, middle_grad]
    return pl.pallas_call(
        functools.partial(input_grad_kernel, len(pieces)),
        grid=(1,),
        in_specs=[pl.BlockSpec((count, columns), lambda *_: (0, 0))] * len(pieces) + [whole(v.shape) for v in rest],
        out_specs=[whole((count, width)), whole((1, width))],
        out_shape=[jax.ShapeDtypeStruct((count, width), F32), jax.ShapeDtypeStruct((1, width), F32)],
        compiler_params=pltpu.CompilerParams(vmem_limit_bytes=10 * MIB),
        cost_estimate=cost(2 * count * width * columns * len(pieces), 8 << 20),
        name="input_grad",
    )(*pieces, *rest)


def padded(rows):
    return -(-rows // 8) * 8


def gather_kernel(counts, chunk, *refs):
    refs = list(refs)
    sums = []
    for group_counts, joint_count in counts:
        groups = [[refs.pop(0) for _ in range(count)] for count in group_counts]
        joint = [refs.pop(0) for _ in range(joint_count)]
        parts, at = [], 0
        for group in groups:
            columns = slice(at, at + group[0].shape[2])
            total = 0.0
            for ref in group:
                total = total + ref[0].astype(F32)
            for ref in joint:
                total = total + ref[0, :, columns].astype(F32)
            parts.append(total)
            at = columns.stop
        sums.append(jnp.concatenate(parts, axis=1))
    attn_gain_ref, mlp_gain_ref, sums_ref = refs[:3]
    qkv_ref, out_ref, gu_ref, down_ref, columns_ref, pair_ref = refs[3:]
    wide_part, pair_part = sums
    pairs = [pair_part[:, i : i + 4 * LANES] for i in range(0, pair_part.shape[1], 4 * LANES)]
    mats = [
        jnp.concatenate([pair[:, i * LANES : (i + 1) * LANES] for pair in pairs], axis=1) for i in range(4)
    ]
    kinds = [
        jnp.concatenate(
            [
                wide_part[:, j + i * chunk : j + (i + 1) * chunk]
                for j in range(0, wide_part.shape[1], 3 * chunk)
            ],
            axis=1,
        )
        for i in range(3)
    ]
    rows = wide_part.shape[0]
    for i in range(3):
        qkv_ref[i] = mats[i]
    for i in range(2):
        gu_ref[i] = kinds[i]
    out_ref[...] = mats[3]
    down_ref[...] = kinds[2]
    columns_ref[...] = jnp.zeros_like(columns_ref)
    lane = lax.broadcasted_iota(jnp.int32, (1, LANES), 1)
    row_sums = jnp.zeros((rows, LANES), F32)
    for i, value in enumerate((mats[0], mats[1], mats[2], mats[3], kinds[0], kinds[1], kinds[2])):
        squares = value * value
        columns_ref[i : i + 1, 0 : value.shape[1]] = jnp.sum(squares, axis=0, keepdims=True)
        row_sums = jnp.where(lane == i, jnp.sum(squares, axis=1, keepdims=True), row_sums)
    pair_ref[...] = jnp.zeros_like(pair_ref)
    pair_ref[0:rows, :] = row_sums
    at = padded(rows)
    for ref in (attn_gain_ref, mlp_gain_ref):
        for i in range(0, ref.shape[1], LANES):
            pair_ref[at : at + 1, :] = ref[:, i : i + LANES]
            at += 1
    pair_ref[at : at + 1, :] = sums_ref[...]


def gather_own(batches, attn_gain_part, mlp_gain_part, local_sums, heads_width, units, chunk):
    rows = batches[0][0][0][0].shape[1]
    width = attn_gain_part.shape[1]
    pieces = [a for groups, joint in batches for group in [*groups, joint] for a in group]
    counts = [([len(group) for group in groups], len(joint)) for groups, joint in batches]
    lines = [attn_gain_part, mlp_gain_part, local_sums]
    shapes = [(3, rows, heads_width), (rows, heads_width), (2, rows, units), (rows, units)]
    shapes += [(8, max(heads_width, units, width)), (padded(rows) + padded(2 * width // LANES + 1), LANES)]
    return pl.pallas_call(
        functools.partial(gather_kernel, counts, chunk),
        grid=(1,),
        in_specs=[pl.BlockSpec((1,) + a.shape[1:], lambda *_: (0, 0, 0)) for a in pieces]
        + [whole(a.shape) for a in lines],
        out_specs=[whole(s) for s in shapes],
        out_shape=[jax.ShapeDtypeStruct(s, F32) for s in shapes],
        compiler_params=pltpu.CompilerParams(vmem_limit_bytes=5 * MIB),
        cost_estimate=cost(1 << 20, 4 << 20),
        name="gather_own",
    )(*pieces, *lines)


def sum_place(i, narrow, count):
    if i < 4:
        return slice(3 + i // 2, 4 + i // 2), slice(i % 2 * narrow, (i % 2 + 1) * narrow)
    return slice(i - 4, i - 3), slice(0, count)


def combine_kernel(rows, width, narrow, columns_ref, own_ref, recv_ref, summed_ref, pair_ref):
    pair = own_ref[...] + recv_ref[...]
    pair_ref[...] = pair
    summed_ref[...] = jnp.zeros_like(summed_ref)
    summed_ref[0:3, :] = columns_ref[4:7, :]
    for i in range(4):
        place = sum_place(i, narrow, 0)
        summed_ref[place] = columns_ref[i : i + 1, 0:narrow]
    summed_ref[3:4, 2 * narrow : 2 * narrow + LANES] = jnp.sum(pair[0:rows, :], axis=0, keepdims=True)
    at = padded(rows)
    for line in (5, 6):
        for i in range(0, width, LANES):
            summed_ref[line : line + 1, i : i + LANES] = pair[at : at + 1, :]
            at += 1


def combine(columns, own, recv, rows, width, narrow):
    shapes = [columns.shape, own.shape]
    return pl.pallas_call(
        functools.partial(combine_kernel, rows, width, narrow),
        out_shape=[jax.ShapeDtypeStruct(s, F32) for s in shapes],
        compiler_params=pltpu.CompilerParams(vmem_limit_bytes=4 * MIB),
        name="combine",
    )(columns, own, recv)


def update_kernel(sizes, *refs):
    (scalar_ref, qkv_ref, out_ref, gu_ref, down_ref, summed_ref, pair_ref) = refs[:7]
    prior_refs, refs = refs[7:11], refs[2:]
    (qkv_cols, out_rows, gu_cols, down_rows, w_qkv, w_out, w_gu, w_down) = refs[9:17]
    (qkv_new, out_new, gu_new, down_new, qkv_cols_new, out_rows_new, gu_cols_new, down_rows_new) = refs[17:25]
    (qkv_rows_new, out_cols_new, gu_rows_new, down_cols_new, attn_gain_ref, mlp_gain_ref, turned, prior_rows_ref) = refs[25:]
    rows = qkv_ref.shape[1]
    width = sizes[0]
    lane = lax.broadcasted_iota(jnp.int32, (1, LANES), 1)
    scalars = as_line(scalar_ref)
    beta = 1.0 - lax.rsqrt(scalars[:, 0:1])
    fresh = 1.0 - beta
    start = lax.rem(width - lax.axis_index("wide") * rows, width)
    prior_rows_ref[...] = jnp.zeros_like(prior_rows_ref)
    at = 0
    for ref in prior_refs:
        value = as_line(ref) if len(ref.shape) == 1 else ref[...]
        prior_rows_ref[at : at + value.shape[0], :] = value
        at += value.shape[0]
    own = pltpu.roll(prior_rows_ref[...], start, 1)[:, 0:LANES]
    turned[...] = jnp.zeros_like(turned)
    turned[0:8, :] = own
    prior_columns = turned[...].T
    gains = pltpu.roll(summed_ref[:, 0:width], start, 1)
    attn_gain_ref[...] = jnp.reshape(gains[5:6, 0:rows], (rows,))
    mlp_gain_ref[...] = jnp.reshape(gains[6:7, 0:rows], (rows,))
    sums = pair_ref[pl.ds(padded(rows) + 2 * width // LANES, 1), :]
    narrow = out_ref.shape[1]
    totals = summed_ref[3:4, 2 * narrow : 2 * narrow + LANES]
    all_rows = jnp.zeros((rows, LANES), F32)
    priors = [qkv_cols[0:1], qkv_cols[1:2], qkv_cols[2:3], as_line(out_rows), gu_cols[0:1], gu_cols[1:2], as_line(down_rows)]
    for i in range(7):
        across = sizes[1 + i]
        entries = float(across * width)
        row_new = beta * prior_columns[0:rows, i : i + 1] + fresh * (pair_ref[0:rows, i : i + 1] / across + TINIEST)
        count = priors[i].shape[1]
        col_new = beta * priors[i] + fresh * (summed_ref[sum_place(i, narrow, count)] / width + TINIEST)
        all_rows = jnp.where(lane == i, row_new, all_rows)
        if i in (3, 6):
            at = 7 + (i == 6)
            prior_mean = sums[:, at : at + 1] / across
        else:
            prior_mean = jnp.mean(prior_rows_ref[i : i + 1, :], axis=1, keepdims=True)
        mean = beta * prior_mean + fresh * (totals[:, i : i + 1] / entries + TINIEST)
        rate = scalars[:, 1:2] * jnp.sqrt(sums[:, i : i + 1] / entries)
        step = lax.rsqrt(row_new * col_new / mean)
        if i in (3, 6):
            gradient_ref, weight_ref, new_ref = ((out_ref, w_out, out_new), (down_ref, w_down, down_new))[i == 6]
            new_ref[...] = (weight_ref[...].astype(F32) - rate * (gradient_ref[...] * step)).astype(BF16)
            (out_rows_new, down_rows_new)[i == 6][...] = jnp.reshape(col_new, (count,))
        else:
            at = i if i < 3 else i - 4
            gradient_ref, weight_ref, new_ref = (qkv_ref, w_qkv, qkv_new) if i < 3 else (gu_ref, w_gu, gu_new)
            new_ref[at] = (weight_ref[at].astype(F32) - rate * (gradient_ref[at] * step)).astype(BF16)
            (qkv_cols_new if i < 3 else gu_cols_new)[at : at + 1] = col_new
    turned[0:rows, :] = all_rows
    rows_new = turned[...].T
    qkv_rows_new[...] = rows_new[0:3, 0:rows]
    out_cols_new[...] = jnp.reshape(rows_new[3:4, 0:rows], (rows,))
    gu_rows_new[...] = rows_new[4:6, 0:rows]
    down_cols_new[...] = jnp.reshape(rows_new[6:7, 0:rows], (rows,))


def update(step_count, learn_rate, grads, summed, pair, prior_rows, col_priors, weights, sizes):
    rows = grads[0].shape[1]
    scalars = jnp.where(jnp.arange(LANES) == 0, step_count.astype(F32), learn_rate)
    inputs = [scalars, *grads, summed, pair, *prior_rows, *col_priors, *weights]
    shapes = [(3, sizes[1] // 2), (sizes[4] // 2,), (2, sizes[5] // 2), (sizes[7] // 2,)]
    shapes += [(3, rows), (rows,), (2, rows), (rows,), (rows,), (rows,)]
    out_shape = [jax.ShapeDtypeStruct(w.shape, BF16) for w in weights]
    out_shape += [jax.ShapeDtypeStruct(s, F32) for s in shapes]
    return pl.pallas_call(
        functools.partial(update_kernel, sizes),
        grid=(1,),
        in_specs=[whole(a.shape) for a in inputs],
        out_specs=[whole(s.shape) for s in out_shape],
        scratch_shapes=[pltpu.VMEM((LANES, LANES), F32), pltpu.VMEM((8, sizes[0]), F32)],
        out_shape=out_shape,
        compiler_params=pltpu.CompilerParams(vmem_limit_bytes=8 * MIB),
        cost_estimate=cost(1 << 20, 4 << 20),
        name="update",
    )(*inputs)


def weights_kernel(rows, qkv_ref, out_ref, gu_ref, down_ref, out_rows_ref, down_rows_ref, line_ref, *refs):
    qkv_own, out_own, gu_own, down_own, sums, qkv_total, gu_total = refs
    step = pl.program_id(0)
    values = [qkv_ref.at[0], qkv_ref.at[1], qkv_ref.at[2], out_ref, gu_ref.at[0], gu_ref.at[1], down_ref]
    width = out_ref.shape[1]
    block = qkv_ref.shape[1]
    start = lax.axis_index("wide") * rows

    @pl.when(step == 0)
    def _():
        for ref in (sums, qkv_total, gu_total):
            ref[...] = jnp.zeros_like(ref)

    def chosen(first, count):
        shape = (qkv_total.shape[1], count)
        own = lax.broadcasted_iota(jnp.int32, shape, 0) + start
        return jnp.where(lax.broadcasted_iota(jnp.int32, shape, 1) + first == own, 1.0, 0.0).astype(BF16)

    for i, ref in enumerate(values):
        count = ref.shape[1]
        value = ref[...].astype(F32)
        sums[i : i + 1, 0:count] += jnp.sum(value * value, axis=0, keepdims=True)
    across = chosen(0, width)
    for ref, own_ref in ((out_ref, out_own), (down_ref, down_own)):
        own_ref[...] = mm_nt(across, ref[...])[0:rows].astype(BF16)
    below = chosen(step * block, block)
    for ref, total in ((qkv_ref, qkv_total), (gu_ref, gu_total)):
        for i in range(ref.shape[0]):
            total[i] += mm(below, ref[i])

    @pl.when(step == pl.num_programs(0) - 1)
    def _():
        lane = lax.broadcasted_iota(jnp.int32, (1, LANES), 1)
        line = jnp.zeros((1, LANES), F32)
        for i in range(7):
            line = jnp.where(lane == i, jnp.sum(sums[i : i + 1, :], axis=1, keepdims=True), line)
        for i, ref in enumerate((out_rows_ref, down_rows_ref)):
            line = jnp.where(lane == 7 + i, jnp.sum(as_line(ref), axis=1, keepdims=True), line)
        line_ref[...] = line
        qkv_own[...] = qkv_total[:, 0:rows, :].astype(BF16)
        gu_own[...] = gu_total[:, 0:rows, :].astype(BF16)


def weights_call(w_qkv, w_out, w_gu, w_down, out_rows, down_rows, n_wide):
    width = w_out.shape[1]
    rows, held = width // n_wide, -(-(width // n_wide) // 16) * 16
    heads_width, units = w_qkv.shape[2], w_gu.shape[2]
    steps = 3 if heads_width % (3 * LANES) == 0 and units % (3 * LANES) == 0 else 1
    each = lambda n: n // steps
    shapes = [(3, rows, heads_width), (rows, heads_width), (2, rows, units), (rows, units)]
    line, *own = pl.pallas_call(
        functools.partial(weights_kernel, rows),
        grid=(steps,),
        in_specs=[
            pl.BlockSpec((3, each(width), heads_width), lambda j: (0, j, 0)),
            pl.BlockSpec((each(heads_width), width), lambda j: (j, 0)),
            pl.BlockSpec((2, each(width), units), lambda j: (0, j, 0)),
            pl.BlockSpec((each(units), width), lambda j: (j, 0)),
            whole(out_rows.shape),
            whole(down_rows.shape),
        ],
        out_specs=[
            whole((1, LANES)),
            whole(shapes[0]),
            pl.BlockSpec((rows, each(heads_width)), lambda j: (0, j)),
            whole(shapes[2]),
            pl.BlockSpec((rows, each(units)), lambda j: (0, j)),
        ],
        out_shape=[jax.ShapeDtypeStruct((1, LANES), F32)] + [jax.ShapeDtypeStruct(shape, BF16) for shape in shapes],
        scratch_shapes=[
            pltpu.VMEM((8, max(width, units)), F32),
            pltpu.VMEM((3, held, heads_width), F32),
            pltpu.VMEM((2, held, units), F32),
        ],
        compiler_params=pltpu.CompilerParams(vmem_limit_bytes=20 * MIB),
        cost_estimate=cost(1 << 20, 7 << 20),
        name="weights",
    )(w_qkv, w_out, w_gu, w_down, out_rows, down_rows)
    return line, own


def after(values, *others):
    return lax.optimization_barrier((values, *others))[0]


def far(values):
    return pltpu.with_memory_space_constraint(values, pltpu.HBM)


def body(
    n_wide,
    tokens,
    plot_slot,
    patch_mask,
    cotangent,
    gain_attn,
    w_qkv,
    w_out,
    gain_mlp,
    w_gu,
    w_down,
    qkv_rows,
    qkv_cols,
    out_rows,
    out_cols,
    gu_rows,
    gu_cols,
    down_rows,
    down_cols,
    step_count,
    learn_rate,
):
    width = tokens.shape[1]
    heads_width, units = w_out.shape[0], w_down.shape[0]
    rows_each = width // n_wide
    chunk = 256
    tokens_other = swap(tokens)
    carried = project(0, far(tokens), far(gain_attn), far(w_qkv), [])
    normed_t, qkv = project(1, tokens_other, gain_attn, w_qkv, carried)
    sent = after((w_out, w_gu, w_down), tokens_other, *carried)
    w_out_other, w_gu_other, w_down_other = swap(sent[0]), swap(sent[1]), swap(sent[2])
    mixed_own, mixed_other, kept, keys = attention(qkv, plot_slot, patch_mask)
    mixed_recv = swap(mixed_other)
    steps = units // chunk // 2

    inputs = [tokens, mixed_own, mixed_recv, w_out, w_out_other, gain_mlp, cotangent, keys]
    wide_parts = []
    for i in range(2):
        at = i * steps
        outs, part_other = middle_call(i == 0, None, inputs, w_gu_other, w_down_other, at, steps, n_wide, chunk)
        if i == 0:
            middle, *inputs = outs
        else:
            inputs = [*inputs[:4], *outs, middle, gain_mlp]
        outs, part = middle_call(False, i == 1, inputs, w_gu, w_down, at, steps, n_wide, chunk)
        one = Scatter(WIDE, [[slotted(part, n_wide), slotted(swap(part_other), n_wide)]], n_wide, 0)
        wide_parts.append(one)
        if i == 1:
            mixed_out, middle_grad, attn_seed, mlp_gain_part = outs
            attn_seed = after(attn_seed, wide_parts[0].turn())
            wide_parts[0].go()
            mixed_grad, seed_t = seeds_call(attn_seed, swap(attn_seed), w_out)
            mixed_grad = after(mixed_grad, one.turn(mixed_grad))
        else:
            one.turn()
        one.go()
        inputs = [after(inputs[0], one.send), *inputs[1:4], *outs[:2]]

    pairs = heads_width // LANES
    back = functools.partial(
        attention_back,
        qkv=qkv,
        mixed_own=mixed_own,
        mixed_other=mixed_other,
        kept=kept,
        keys=keys,
        normed_t=normed_t,
        seed_t=seed_t,
        n_wide=n_wide,
    )
    pieces = []
    piece, carried = back(0, 0, pairs - 1, [], grad=mixed_grad)
    pieces.append(piece)
    weights = after((w_qkv, w_out, w_gu, w_down, out_rows, down_rows), piece)
    local_sums, own_weights = weights_call(*weights, n_wide)
    mixed_grad = after(mixed_grad, local_sums)
    for pair in range(1, pairs - 1):
        piece, carried = back(pair, pair, pairs - 1, carried, grad=mixed_grad)
        pieces.append(piece)
    keep, send = kept_and_sent(carried, n_wide)
    first = [keep, stage_exchange(send, 0, n_wide, PAIRS)]
    mixed_grad = after(mixed_grad, send, wide_parts[1].turn(piece))
    wide_parts[1].go()
    piece, carried = back(pairs - 1, 0, 1, [], grad=mixed_grad)
    pieces.append(piece)
    keep, send = kept_and_sent(carried, n_wide)
    last = [keep, stage_exchange(send, 0, n_wide, PAIRS)]
    pair_batch = Scatter(PAIRS, [first, last], n_wide, 1)
    wide_batch = Scatter(WIDE, [one.groups[0] + one.joint for one in wide_parts], n_wide, 2)
    batches = wide_batch.finish(pair_batch)
    back_other = swap(input_other(pieces, w_qkv))
    tokens_grad, attn_gain_part = input_grad(pieces, w_qkv, back_other, tokens, gain_attn, middle_grad)

    *grads, columns, pair = gather_own(
        batches, attn_gain_part, mlp_gain_part, local_sums, heads_width, units, chunk
    )
    summed, pair = combine(columns, pair, swap(pair), rows_each, width, heads_width)
    for stage in range(n_wide.bit_length() - 1):
        summed = summed + stage_exchange(summed, stage, n_wide, PAIRS)
    outs = update(
        step_count,
        learn_rate,
        [far(grad) for grad in grads],
        summed,
        pair,
        [qkv_rows, out_cols, gu_rows, down_cols],
        [qkv_cols, out_rows, gu_cols, down_rows],
        own_weights,
        [width] + [2 * heads_width] * 4 + [2 * units] * 3,
    )
    qkv_new, out_new, gu_new, down_new, qkv_cols_new, out_rows_new, gu_cols_new, down_rows_new = outs[:8]
    qkv_rows_new, out_cols_new, gu_rows_new, down_cols_new, attn_gain_grad, mlp_gain_grad = outs[8:]
    qkv_grad, out_grad, gu_grad, down_grad = grads
    return (
        mixed_out,
        tokens_grad,
        attn_gain_grad,
        qkv_grad,
        out_grad.T,
        mlp_gain_grad,
        gu_grad,
        down_grad.T,
        qkv_new,
        out_new.T,
        gu_new,
        down_new.T,
        qkv_rows_new,
        qkv_cols_new,
        out_rows_new,
        out_cols_new,
        gu_rows_new,
        gu_cols_new,
        down_rows_new,
        down_cols_new,
    )


def solution(mesh):
    in_specs = (
        P(("wide", "narrow"), None),
        P("wide"),
        P("wide"),
        P(("wide", "narrow"), None),
        P(),
        P(None, None, "narrow"),
        P("narrow", None),
        P(),
        P(None, None, "narrow"),
        P("narrow", None),
        P(),
        P(None, "narrow"),
        P("narrow"),
        P(),
        P(),
        P(None, "narrow"),
        P("narrow"),
        P(),
        P(),
        P(),
    )
    out_specs = (
        P(("wide", "narrow"), None),
        P(("wide", "narrow"), None),
        P("wide"),
        P(None, "wide", "narrow"),
        P("narrow", "wide"),
        P("wide"),
        P(None, "wide", "narrow"),
        P("narrow", "wide"),
        P(None, "wide", "narrow"),
        P("narrow", "wide"),
        P(None, "wide", "narrow"),
        P("narrow", "wide"),
        P(None, "wide"),
        P(None, "narrow"),
        P("narrow"),
        P("wide"),
        P(None, "wide"),
        P(None, "narrow"),
        P("narrow"),
        P("wide"),
    )
    return jax.shard_map(
        functools.partial(body, mesh.shape["wide"]),
        mesh=mesh,
        in_specs=in_specs,
        out_specs=out_specs,
        check_vma=False,
    )
```

```python
import functools
import math

import jax
import jax.numpy as jnp
from jax import lax
from jax.experimental import pallas as pl
from jax.experimental.pallas import tpu as pltpu
from jax.sharding import PartitionSpec as P

DH = 64
LANES = 128
EPSILON = 1e-06
TINIEST = 1e-30
NEGATIVE = -1e30
F32 = jnp.float32
BF16 = jnp.bfloat16
ROOT = math.sqrt(2.0 / math.pi)
CUBE = 0.044715
MIB = 1024 * 1024
LIVE = 5


def mm(a, b):
    return jnp.dot(a, b, preferred_element_type=F32)


def mm_nt(a, b):
    return lax.dot_general(a, b, (((1,), (1,)), ((), ())), preferred_element_type=F32)


def whole(shape):
    return pl.BlockSpec(shape, lambda *_: (0,) * len(shape))


def cost(flops, nbytes):
    return pl.CostEstimate(flops=int(flops), bytes_accessed=int(nbytes), transcendentals=0)


def inverse_rms(rows):
    return lax.rsqrt(jnp.mean(rows * rows, axis=-1, keepdims=True) + EPSILON)


def three_terms(values):
    high = values.astype(BF16)
    rest = values - high.astype(F32)
    middle = rest.astype(BF16)
    return high, middle, (rest - middle.astype(F32)).astype(BF16)


WIDE, PAIRS = 0, 1


def bit_orders(n_wide, kind):
    bits = n_wide.bit_length() - 1
    straight = list(range(bits))
    if bits <= 2:
        return straight, straight
    if kind == WIDE:
        return straight, [1, 0] + straight[2:]
    return straight, straight[1:-1] + straight[:1] + straight[-1:]


def slot_masks(n_wide, kind):
    bits = n_wide.bit_length() - 1
    return [
        [sum(1 << bit for stage, bit in enumerate(order) if slot >> (bits - 1 - stage) & 1) for slot in range(n_wide)]
        for order in bit_orders(n_wide, kind)
    ]


def slot_row(slot, n_wide, kind, turned=0):
    masks = slot_masks(n_wide, kind)
    wide, core = lax.axis_index("wide"), lax.axis_index("narrow")
    first, second = masks[turned][slot], masks[1 - turned][slot]
    return jnp.bitwise_xor(wide, first + (second - first) * core)


def stage_exchange(values, stage, n_wide, kind):
    orders = bit_orders(n_wide, kind)
    pairs = []
    for wide in range(n_wide):
        for core in range(2):
            pairs.append((wide * 2 + core, (wide ^ (1 << orders[core][stage])) * 2 + core))
    return lax.ppermute(values, ("wide", "narrow"), pairs)


def swap(values):
    return lax.ppermute(values, "narrow", [(0, 1), (1, 0)])


def write_slots(kind, turned, n_wide, held_ref, targets, rows_each):
    if targets[0].ndim == 2:
        targets[0][...] = held_ref[...].astype(BF16)
        return
    slot = 0
    for target in targets:
        for at in range(target.shape[0]):
            start = pl.multiple_of(slot_row(slot, n_wide, kind, turned) * rows_each, 16)
            target[at] = held_ref[pl.ds(start, rows_each), :].astype(BF16)
            slot += 1


def in_slots(part, n_wide, kind):
    rows = jnp.stack([slot_row(slot, n_wide, kind) for slot in range(n_wide)])
    return jnp.take(part.reshape(n_wide, -1, part.shape[-1]), rows, axis=0)


def as_line(ref):
    return jnp.reshape(ref[...], (1, ref.shape[0]))


def project_kernel(carried, rows_ref, gain_ref, w_ref, *refs):
    normed_t_ref, projected_ref = refs[carried:]
    rows = rows_ref[...].astype(F32)
    normed = (rows * inverse_rms(rows) * as_line(gain_ref)).astype(BF16)
    normed_t_ref[...] = normed.T
    for i in range(3):
        projected_ref[i] = mm(normed, w_ref[i]).astype(BF16)


def project(half, tokens, gain, w_qkv, carried):
    count, width = tokens.shape
    out = w_qkv.shape[2]
    inputs = [tokens, gain, w_qkv]
    return pl.pallas_call(
        functools.partial(project_kernel, len(carried)),
        grid=(1,),
        in_specs=[whole(v.shape) for v in inputs] + [pl.BlockSpec(memory_space=pl.ANY)] * len(carried),
        out_specs=[
            pl.BlockSpec((width, count), lambda *_: (0, half)),
            pl.BlockSpec((3, count, out), lambda *_: (0, half, 0)),
        ],
        out_shape=[
            jax.ShapeDtypeStruct((width, 2 * count), BF16),
            jax.ShapeDtypeStruct((3, 2 * count, out), BF16),
        ],
        input_output_aliases={len(inputs) + i: i for i in range(len(carried))},
        cost_estimate=cost(6 * count * width * out, 4 * count * width),
        compiler_params=pltpu.CompilerParams(vmem_limit_bytes=8 * MIB),
        name="project",
    )(*inputs, *carried)


def key_lines(slot_ref, mask_ref, core):
    slot, mask = as_line(slot_ref), as_line(mask_ref)
    length = mask.shape[1]
    turned = lambda values: pltpu.roll(values, length // 2, 1)
    live = mask + (turned(mask) - mask) * core
    same = jnp.where(slot == turned(slot), live, 0)
    first = lax.broadcasted_iota(jnp.int32, (1, length), 1) < length // 2
    for_own = jnp.where(jnp.where(first, live, same) > 0, 0.0, NEGATIVE)
    for_other = jnp.where(jnp.where(first, same, live) > 0, 0.0, NEGATIVE)
    return for_own, for_other, live.astype(F32)


def column(line):
    return jnp.broadcast_to(line, (LANES, line.shape[1])).T


def attention_kernel(qkv_ref, slot_ref, mask_ref, own_ref, other_ref, kept_ref, keys_ref, held, *, block):
    lane = lax.broadcasted_iota(jnp.int32, (1, LANES), 1)
    lows = (lane < DH, lane >= DH)
    within = jnp.bitwise_and(lane, DH - 1)

    @pl.when(pl.program_id(0) == 0)
    def _():
        ones = jnp.where((within >= 2) & (within < 5), 1.0, 0.0)
        for_own, for_other, live = key_lines(slot_ref, mask_ref, lax.axis_index("narrow"))
        bias = jnp.where(within == 1, column(for_other), jnp.where(within == LIVE, column(live), ones))
        keys_ref[...] = jnp.where(within == 0, column(for_own), bias).astype(BF16)

    for head in range(2):
        held[head] = jnp.where(lows[head], qkv_ref[1], keys_ref[...])
        held[2 + head] = jnp.where(lows[head], qkv_ref[2], jnp.ones((1, LANES), BF16))
    half = own_ref.shape[0]
    for part, out_ref in enumerate((own_ref, other_ref)):

        def step(i, carry, part=part, out_ref=out_ref):
            inside = pl.ds(pl.multiple_of(i * block, block), block)
            rows = pl.ds(pl.multiple_of(part * half + i * block, block), block)
            queries = qkv_ref[0, rows, :] * jnp.asarray(1.0 / math.sqrt(DH), BF16)
            constants = jnp.where(within == part, 1.0, 0.0).astype(BF16)
            results = []
            for head in range(2):
                scores = mm_nt(jnp.where(lows[head], queries, constants), held[head])
                highest = jnp.max(scores, axis=1, keepdims=True)
                weights = jnp.exp(scores - highest).astype(BF16)
                mixed = mm(weights, held[2 + head])
                results.append(mixed / pltpu.roll(mixed, DH, 1))
                high, middle, low = three_terms(highest + jnp.log(mixed))
                base = DH * (1 - head)
                constants_back = jnp.where(
                    lane == base + 2,
                    -high,
                    jnp.where(lane == base + 3, -middle, jnp.where(lane == base + 4, -low, constants)),
                )
                kept_ref[head, rows, :] = jnp.where(lows[head], queries, constants_back)
            out_ref[inside, :] = jnp.where(lows[0], results[0], results[1]).astype(BF16)
            return carry

        lax.fori_loop(0, half // block, step, 0)


def attention(qkv, plot_slot, patch_mask, block=512):
    length, width = qkv.shape[1:]
    pairs, half = width // LANES, length // 2
    return pl.pallas_call(
        functools.partial(attention_kernel, block=block),
        grid=(pairs,),
        in_specs=[
            pl.BlockSpec((3, length, LANES), lambda p: (0, 0, p)),
            whole(plot_slot.shape),
            whole(patch_mask.shape),
        ],
        out_specs=[
            pl.BlockSpec((half, LANES), lambda p: (0, p)),
            pl.BlockSpec((half, LANES), lambda p: (0, p)),
            pl.BlockSpec((2, length, LANES), lambda p: (p, 0, 0)),
            whole((length, LANES)),
        ],
        scratch_shapes=[pltpu.VMEM((4, length, LANES), BF16)],
        out_shape=[
            jax.ShapeDtypeStruct((half, width), BF16),
            jax.ShapeDtypeStruct((half, width), BF16),
            jax.ShapeDtypeStruct((2 * pairs, length, LANES), BF16),
            jax.ShapeDtypeStruct((length, LANES), BF16),
        ],
        cost_estimate=cost(16 * pairs * length * length * LANES, 10 * length * width),
        compiler_params=pltpu.CompilerParams(vmem_limit_bytes=11 * MIB),
        name="attention",
    )(qkv, plot_slot, patch_mask)


def middle_kernel(first, last, rows_each, n_wide, *refs):
    refs = list(refs)
    take = lambda n: [refs.pop(0) for _ in range(n)]
    if first:
        (tokens_ref, own_ref, recv_ref, w_own_ref, w_recv_ref, gain_ref, cot_ref, keys_ref) = take(8)
    else:
        (normed, normed_t, seed, seed_t, total_in, back_in) = take(6)
        if last:
            (middle_ref, gain_ref) = take(2)
    (gu_ref, down_ref) = take(2)
    if first:
        (middle_ref, normed, normed_t, seed, seed_t) = take(5)
    if last:
        (out_ref, grad_ref, attn_seed_ref, gain_part_ref) = take(4)
    else:
        (total_ref, back_ref) = take(2)
    part_refs = take(len(refs) - (3 if last else 1))
    (held,) = take(1)
    if last:
        (total_ref, back_ref) = take(2)
    step = pl.program_id(0)

    @pl.when(step == 0)
    def _():
        if first:
            middle = tokens_ref[...].astype(F32) + (
                mm(own_ref[...], w_own_ref[...]) + mm(recv_ref[...], w_recv_ref[...])
            )
            middle_ref[...] = middle
            total_ref[...] = middle
            back_ref[...] = jnp.zeros_like(back_ref)
            live = keys_ref[...].astype(F32)[:, LIVE : LIVE + 1]
            seed_value = (cot_ref[...].astype(F32) * live).astype(BF16)
            seed[...] = seed_value
            seed_t[...] = seed_value.T
            value = (middle * inverse_rms(middle) * as_line(gain_ref)).astype(BF16)
            normed[...] = value
            normed_t[...] = value.T
        else:
            total_ref[...] = total_in[...]
            back_ref[...] = back_in[...]

    gate = mm(normed[...], gu_ref[0])
    up = mm(normed[...], gu_ref[1])
    bent = jnp.tanh(ROOT * (gate + CUBE * gate * gate * gate))
    soft = 0.5 * gate * (1.0 + bent)
    slope = 0.5 * (1.0 + bent) + 0.5 * gate * (1.0 - bent * bent) * (ROOT * (1.0 + 3.0 * CUBE * gate * gate))
    hidden = (soft * up).astype(BF16)
    hidden_grad = mm_nt(seed[...], down_ref[...])
    gate_grad = (hidden_grad * up * slope).astype(BF16)
    up_grad = (hidden_grad * soft).astype(BF16)
    total_ref[...] += mm(hidden, down_ref[...])
    back_ref[...] += mm_nt(gate_grad, gu_ref[0]) + mm_nt(up_grad, gu_ref[1])
    chunk = gate.shape[1]
    held[:, 0:chunk] = mm(normed_t[...], gate_grad)
    held[:, chunk : 2 * chunk] = mm(normed_t[...], up_grad)
    held[:, 2 * chunk : 3 * chunk] = mm(seed_t[...], hidden)
    write_slots(WIDE, int(last is None), n_wide, held, part_refs, rows_each)

    if last:

        @pl.when(step == pl.num_programs(0) - 1)
        def _():
            out_ref[...] = total_ref[...].astype(BF16)
            middle = middle_ref[...]
            factor = inverse_rms(middle)
            back = back_ref[...]
            scaled = back * as_line(gain_ref)
            inner = jnp.mean(scaled * middle, axis=-1, keepdims=True)
            grad = seed[...].astype(F32) + factor * scaled - middle * (factor * factor * factor * inner)
            grad_ref[...] = grad
            attn_seed_ref[...] = grad.astype(BF16)
            gain_part_ref[...] = jnp.sum(back * middle * factor, axis=0, keepdims=True)


def middle_call(first, last, inputs, w_gu, w_down, at, steps, n_wide, chunk):
    count, width = inputs[0].shape
    rows_each = width // n_wide
    tall = rows_each % 16 == 0
    rows, turned = (count, width), (width, count)
    columns = 3 * chunk * steps
    if tall:
        part_specs = [pl.BlockSpec((n_wide, rows_each, 3 * chunk), lambda j, *_: (0, 0, j))]
        part_shapes = [jax.ShapeDtypeStruct((n_wide, rows_each, columns), BF16)]
    else:
        part_specs = [pl.BlockSpec((width, 3 * chunk), lambda j, *_: (0, j))]
        part_shapes = [jax.ShapeDtypeStruct((width, columns), BF16)]
    in_specs = [whole((count, LANES) if v.shape[1:] == (LANES,) else v.shape) for v in inputs] + [
        pl.BlockSpec((2, width, chunk), lambda j, *_: (0, 0, at + j)),
        pl.BlockSpec((chunk, width), lambda j, *_: (at + j, 0)),
    ]
    inputs = [*inputs, w_gu, w_down]
    shape = jax.ShapeDtypeStruct
    scratch = [pltpu.VMEM((width, 3 * chunk), F32)]
    out_shape = []
    if first:
        out_shape += [shape(rows, F32), shape(rows, BF16), shape(turned, BF16), shape(rows, BF16), shape(turned, BF16)]
    if last:
        out_shape += [shape(rows, BF16), shape(rows, F32), shape(rows, BF16), shape((1, width), F32)]
        scratch += [pltpu.VMEM(rows, F32)] * 2
    else:
        out_shape += [shape(rows, F32)] * 2
    outs = pl.pallas_call(
        functools.partial(middle_kernel, first, last, rows_each, n_wide),
        grid=(steps,),
        in_specs=in_specs,
        out_specs=[whole(s.shape) for s in out_shape] + part_specs,
        scratch_shapes=scratch,
        out_shape=out_shape + part_shapes,
        compiler_params=pltpu.CompilerParams(vmem_limit_bytes=(20 if last else 14) * MIB),
        cost_estimate=cost((1 if last else 36) * count * width * chunk * steps, width * chunk * steps),
        name="middle",
    )(*inputs)
    return outs[: len(out_shape)], outs[-1]


def slotted(part, n_wide):
    return part if part.ndim == 3 else in_slots(part, n_wide, WIDE)


def seeds_kernel(own_ref, other_ref, w_ref, grad_ref, seed_t_ref):
    count = own_ref.shape[0]
    for half, seed_ref in enumerate((own_ref, other_ref)):
        at = slice(half * count, (half + 1) * count)
        grad_ref[at, :] = mm_nt(seed_ref[...], w_ref[...]).astype(BF16)
        seed_t_ref[:, at] = seed_ref[...].T


def seeds_call(own, other, w_out):
    count, width = own.shape
    out = w_out.shape[0]
    return pl.pallas_call(
        seeds_kernel,
        out_shape=[
            jax.ShapeDtypeStruct((2 * count, out), BF16),
            jax.ShapeDtypeStruct((width, 2 * count), BF16),
        ],
        cost_estimate=cost(16 * count * width * width, 8 * count),
        compiler_params=pltpu.CompilerParams(vmem_limit_bytes=4 * MIB),
        name="seeds",
    )(own, other, w_out)


def attention_back_kernel(block, rows_each, n_wide, split, carried, *refs):
    refs = list(refs)
    (qkv_ref, grad_ref, mixed_own_ref, mixed_other_ref, kept_ref, keys_ref) = refs[:6]
    (normed_t_ref, seed_t_ref) = refs[6:8]
    refs = refs[8 + carried :]
    pieces = refs.pop(0)
    part_refs = [refs.pop(0) for _ in range(split)]
    grads, queries, query_total, mixed, held = refs
    lane = lax.broadcasted_iota(jnp.int32, (1, LANES), 1)
    lows = (lane < DH, lane >= DH)
    nothing = jnp.zeros((1, LANES), BF16)
    length = grad_ref.shape[0]
    half = length // 2
    mixed[0:half, :] = mixed_own_ref[...]
    mixed[half:length, :] = mixed_other_ref[...]
    product = grad_ref[...].astype(F32) * mixed[...].astype(F32)
    for head in range(2):
        base = DH * (1 - head)
        dots = jnp.sum(jnp.where(lows[head], product, 0.0), axis=1, keepdims=True)
        high, middle, low = three_terms(dots)
        constants = jnp.where(
            lane == base + 2,
            -high,
            jnp.where(lane == base + 3, -middle, jnp.where(lane == base + 4, -low, nothing)),
        )
        grads[head] = jnp.where(lows[head], grad_ref[...], constants)
        grads[2 + head] = jnp.where(lows[head], grad_ref[...], nothing)
        queries[head] = jnp.where(lows[head], kept_ref[head], nothing)
    query_total[...] = jnp.zeros_like(query_total)

    def step(i, carry):
        rows = pl.ds(pl.multiple_of(i * block, block), block)
        keys, values, constants = qkv_ref[1, rows, :], qkv_ref[2, rows, :], keys_ref[rows, :]
        key_grad, value_grad = [], []
        for head in range(2):
            base = DH * (1 - head)
            ones = jnp.where((lane >= base + 2) & (lane < base + 5), 1.0, 0.0).astype(BF16)
            keys_only = jnp.where(lows[head], keys, nothing) * jnp.asarray(1.0 / math.sqrt(DH), BF16)
            weights = jnp.exp(mm_nt(jnp.where(lows[head], keys, constants), kept_ref[head]))
            score_grads = weights * mm_nt(jnp.where(lows[head], values, ones), grads[head])
            score_grads = score_grads.astype(BF16)
            value_grad.append(mm(weights.astype(BF16), grads[2 + head]))
            key_grad.append(mm(score_grads, queries[head]))
            query_total[...] += mm(keys_only.T, score_grads)
        pieces[rows, LANES : 2 * LANES] = (key_grad[0] + key_grad[1]).astype(BF16)
        pieces[rows, 2 * LANES : 3 * LANES] = (value_grad[0] + value_grad[1]).astype(BF16)
        return carry

    lax.fori_loop(0, length // block, step, 0)
    pieces[:, 0:LANES] = query_total[...].T.astype(BF16)
    held[:, 0 : 3 * LANES] = mm(normed_t_ref[...], pieces[...])
    held[:, 3 * LANES : 4 * LANES] = mm(seed_t_ref[...], mixed[...])
    write_slots(PAIRS, 0, n_wide, held, part_refs, rows_each)


def attention_back(pair, at, total, carried, qkv, grad, mixed_own, mixed_other, kept, keys, normed_t, seed_t, n_wide, block=512):
    length = qkv.shape[1]
    half = length // 2
    width = normed_t.shape[0]
    rows_each = width // n_wide
    tall = rows_each % 16 == 0
    columns = 4 * LANES
    if tall:
        part_specs = [pl.BlockSpec((n_wide // 2, rows_each, columns), lambda p, *_: (0, 0, at))] * 2
        part_shapes = [jax.ShapeDtypeStruct((n_wide // 2, rows_each, total * columns), BF16)] * 2
    else:
        part_specs = [pl.BlockSpec((width, columns), lambda p, *_: (0, at))]
        part_shapes = [jax.ShapeDtypeStruct((width, total * columns), BF16)]
    in_specs = [
        pl.BlockSpec((3, length, LANES), lambda p, *_: (0, 0, pair)),
        pl.BlockSpec((length, LANES), lambda p, *_: (0, pair)),
        pl.BlockSpec((half, LANES), lambda p, *_: (0, pair)),
        pl.BlockSpec((half, LANES), lambda p, *_: (0, pair)),
        pl.BlockSpec((2, length, LANES), lambda p, *_: (pair, 0, 0)),
        whole((length, LANES)),
        whole((width, length)),
        whole((width, length)),
    ]
    inputs = [qkv, grad, mixed_own, mixed_other, kept, keys, normed_t, seed_t]
    aliases = {len(inputs) + i: 1 + i for i in range(len(carried))}
    outs = pl.pallas_call(
        functools.partial(attention_back_kernel, block, rows_each, n_wide, len(part_specs), len(carried)),
        grid=(1,),
        in_specs=in_specs + [pl.BlockSpec(memory_space=pl.ANY)] * len(carried),
        out_specs=[whole((length, 3 * LANES))] + part_specs,
        scratch_shapes=[
            pltpu.VMEM((4, length, LANES), BF16),
            pltpu.VMEM((2, length, LANES), BF16),
            pltpu.VMEM((LANES, length), F32),
            pltpu.VMEM((length, LANES), BF16),
            pltpu.VMEM((width, columns), F32),
        ],
        out_shape=[jax.ShapeDtypeStruct((length, 3 * LANES), BF16)] + part_shapes,
        input_output_aliases=aliases,
        compiler_params=pltpu.CompilerParams(vmem_limit_bytes=15 * MIB),
        cost_estimate=cost(50 * length * length * LANES, 16 * length * LANES),
        name="attention_back",
    )(*inputs, *carried)
    return outs[0], list(outs[1:])


def kept_and_sent(parts, n_wide):
    if len(parts) == 2:
        return parts
    slots = in_slots(parts[0], n_wide, PAIRS)
    return slots[: n_wide // 2], slots[n_wide // 2 :]


def turn_kernel(counts, *refs):
    *refs, out_ref = refs
    groups = [[refs.pop(0) for _ in range(count)] for count in counts]

    def step(slot, carry):
        at = 0
        for group in groups:
            columns = slice(at, at + group[0].shape[2])
            total = 0.0
            for ref in group:
                total = total + ref[slot].astype(F32)
            for ref in refs:
                total = total + ref[slot, :, columns].astype(F32)
            out_ref[slot, :, columns] = total.astype(BF16)
            at = columns.stop
        return carry

    lax.fori_loop(0, out_ref.shape[0], step, 0)


class Scatter:
    def __init__(self, kind, groups, n_wide, stage):
        self.kind, self.groups, self.joint, self.n_wide, self.stage, self.slots = kind, groups, [], n_wide, stage, n_wide >> stage

    def turn(self, *earlier):
        self.slots //= 2
        pieces = [a for group in self.groups for a in group] + self.joint
        if earlier:
            pieces[-1] = after(pieces[-1], *earlier)
        rows = pieces[0].shape[1]
        shape = (self.slots, rows, sum(group[0].shape[2] for group in self.groups))
        self.send = pl.pallas_call(
            functools.partial(turn_kernel, [len(group) for group in self.groups]),
            grid=(1,),
            in_specs=[pl.BlockSpec((self.slots,) + a.shape[1:], lambda *_: (1, 0, 0)) for a in pieces],
            out_specs=whole(shape),
            out_shape=jax.ShapeDtypeStruct(shape, BF16),
            compiler_params=pltpu.CompilerParams(vmem_limit_bytes=8 * MIB),
            cost_estimate=cost(math.prod(shape), 4 * math.prod(shape)),
            name="turn",
        )(*pieces)
        return self.send

    def go(self):
        self.joint.append(stage_exchange(self.send, self.stage, self.n_wide, self.kind))
        self.stage += 1

    def finish(self, other):
        while other.slots > 1:
            earlier = []
            if self.slots > 1:
                earlier = [self.turn()]
                self.go()
            other.turn(*earlier)
            other.go()
        return [(batch.groups, batch.joint) for batch in (self, other)]


def input_other_kernel(pairs, *refs):
    *piece_refs, w_ref, out_ref = refs
    back = 0.0
    for i in range(3):
        columns = slice(i * LANES, (i + 1) * LANES)
        back = back + mm_nt(jnp.concatenate([ref[:, columns] for ref in piece_refs], axis=1), w_ref[i])
    out_ref[...] = back.astype(BF16)


def input_other(pieces, w_qkv):
    length, columns = pieces[0].shape
    half, width = length // 2, w_qkv.shape[1]
    return pl.pallas_call(
        functools.partial(input_other_kernel, len(pieces)),
        grid=(1,),
        in_specs=[pl.BlockSpec((half, columns), lambda *_: (1, 0))] * len(pieces) + [whole(w_qkv.shape)],
        out_specs=whole((half, width)),
        out_shape=jax.ShapeDtypeStruct((half, width), BF16),
        compiler_params=pltpu.CompilerParams(vmem_limit_bytes=5 * MIB),
        cost_estimate=cost(2 * half * width * columns * len(pieces), 4 << 20),
        name="input_other",
    )(*pieces, w_qkv)


def input_grad_kernel(pairs, *refs):
    piece_refs, refs = refs[:pairs], refs[pairs:]
    w_ref, recv_ref, tokens_ref, gain_ref, middle_grad_ref, out_ref, part_ref = refs
    back = recv_ref[...].astype(F32)
    for i in range(3):
        columns = slice(i * LANES, (i + 1) * LANES)
        back = back + mm_nt(jnp.concatenate([ref[:, columns] for ref in piece_refs], axis=1), w_ref[i])
    rows = tokens_ref[...].astype(F32)
    factor = inverse_rms(rows)
    scaled = back * as_line(gain_ref)
    inner = jnp.mean(scaled * rows, axis=-1, keepdims=True)
    out_ref[...] = middle_grad_ref[...] + factor * scaled - rows * (factor * factor * factor * inner)
    part_ref[...] = jnp.sum(back * rows * factor, axis=0, keepdims=True)


def input_grad(pieces, w_qkv, recv, tokens, gain_line, middle_grad):
    count, width = tokens.shape
    columns = pieces[0].shape[1]
    rest = [w_qkv, recv, tokens, gain_line, middle_grad]
    return pl.pallas_call(
        functools.partial(input_grad_kernel, len(pieces)),
        grid=(1,),
        in_specs=[pl.BlockSpec((count, columns), lambda *_: (0, 0))] * len(pieces) + [whole(v.shape) for v in rest],
        out_specs=[whole((count, width)), whole((1, width))],
        out_shape=[jax.ShapeDtypeStruct((count, width), F32), jax.ShapeDtypeStruct((1, width), F32)],
        compiler_params=pltpu.CompilerParams(vmem_limit_bytes=10 * MIB),
        cost_estimate=cost(2 * count * width * columns * len(pieces), 8 << 20),
        name="input_grad",
    )(*pieces, *rest)


def padded(rows):
    return -(-rows // 8) * 8


def gather_kernel(counts, chunk, *refs):
    refs = list(refs)
    sums = []
    for group_counts, joint_count in counts:
        groups = [[refs.pop(0) for _ in range(count)] for count in group_counts]
        joint = [refs.pop(0) for _ in range(joint_count)]
        parts, at = [], 0
        for group in groups:
            columns = slice(at, at + group[0].shape[2])
            total = 0.0
            for ref in group:
                total = total + ref[0].astype(F32)
            for ref in joint:
                total = total + ref[0, :, columns].astype(F32)
            parts.append(total)
            at = columns.stop
        sums.append(jnp.concatenate(parts, axis=1))
    attn_gain_ref, mlp_gain_ref, sums_ref = refs[:3]
    qkv_ref, out_ref, gu_ref, down_ref, columns_ref, pair_ref = refs[3:]
    wide_part, pair_part = sums
    pairs = [pair_part[:, i : i + 4 * LANES] for i in range(0, pair_part.shape[1], 4 * LANES)]
    mats = [
        jnp.concatenate([pair[:, i * LANES : (i + 1) * LANES] for pair in pairs], axis=1) for i in range(4)
    ]
    kinds = [
        jnp.concatenate(
            [
                wide_part[:, j + i * chunk : j + (i + 1) * chunk]
                for j in range(0, wide_part.shape[1], 3 * chunk)
            ],
            axis=1,
        )
        for i in range(3)
    ]
    rows = wide_part.shape[0]
    for i in range(3):
        qkv_ref[i] = mats[i]
    for i in range(2):
        gu_ref[i] = kinds[i]
    out_ref[...] = mats[3]
    down_ref[...] = kinds[2]
    columns_ref[...] = jnp.zeros_like(columns_ref)
    lane = lax.broadcasted_iota(jnp.int32, (1, LANES), 1)
    row_sums = jnp.zeros((rows, LANES), F32)
    for i, value in enumerate((mats[0], mats[1], mats[2], mats[3], kinds[0], kinds[1], kinds[2])):
        squares = value * value
        columns_ref[i : i + 1, 0 : value.shape[1]] = jnp.sum(squares, axis=0, keepdims=True)
        row_sums = jnp.where(lane == i, jnp.sum(squares, axis=1, keepdims=True), row_sums)
    pair_ref[...] = jnp.zeros_like(pair_ref)
    pair_ref[0:rows, :] = row_sums
    at = padded(rows)
    for ref in (attn_gain_ref, mlp_gain_ref):
        for i in range(0, ref.shape[1], LANES):
            pair_ref[at : at + 1, :] = ref[:, i : i + LANES]
            at += 1
    pair_ref[at : at + 1, :] = sums_ref[...]


def gather_own(batches, attn_gain_part, mlp_gain_part, local_sums, heads_width, units, chunk):
    rows = batches[0][0][0][0].shape[1]
    width = attn_gain_part.shape[1]
    pieces = [a for groups, joint in batches for group in [*groups, joint] for a in group]
    counts = [([len(group) for group in groups], len(joint)) for groups, joint in batches]
    lines = [attn_gain_part, mlp_gain_part, local_sums]
    shapes = [(3, rows, heads_width), (rows, heads_width), (2, rows, units), (rows, units)]
    shapes += [(8, max(heads_width, units, width)), (padded(rows) + padded(2 * width // LANES + 1), LANES)]
    return pl.pallas_call(
        functools.partial(gather_kernel, counts, chunk),
        grid=(1,),
        in_specs=[pl.BlockSpec((1,) + a.shape[1:], lambda *_: (0, 0, 0)) for a in pieces]
        + [whole(a.shape) for a in lines],
        out_specs=[whole(s) for s in shapes],
        out_shape=[jax.ShapeDtypeStruct(s, F32) for s in shapes],
        compiler_params=pltpu.CompilerParams(vmem_limit_bytes=5 * MIB),
        cost_estimate=cost(1 << 20, 4 << 20),
        name="gather_own",
    )(*pieces, *lines)


def sum_place(i, narrow, count):
    if i < 4:
        return slice(3 + i // 2, 4 + i // 2), slice(i % 2 * narrow, (i % 2 + 1) * narrow)
    return slice(i - 4, i - 3), slice(0, count)


def combine_kernel(rows, width, narrow, columns_ref, own_ref, recv_ref, summed_ref, pair_ref):
    pair = own_ref[...] + recv_ref[...]
    pair_ref[...] = pair
    summed_ref[...] = jnp.zeros_like(summed_ref)
    summed_ref[0:3, :] = columns_ref[4:7, :]
    for i in range(4):
        place = sum_place(i, narrow, 0)
        summed_ref[place] = columns_ref[i : i + 1, 0:narrow]
    summed_ref[3:4, 2 * narrow : 2 * narrow + LANES] = jnp.sum(pair[0:rows, :], axis=0, keepdims=True)
    at = padded(rows)
    for line in (5, 6):
        for i in range(0, width, LANES):
            summed_ref[line : line + 1, i : i + LANES] = pair[at : at + 1, :]
            at += 1


def combine(columns, own, recv, rows, width, narrow):
    shapes = [columns.shape, own.shape]
    return pl.pallas_call(
        functools.partial(combine_kernel, rows, width, narrow),
        out_shape=[jax.ShapeDtypeStruct(s, F32) for s in shapes],
        compiler_params=pltpu.CompilerParams(vmem_limit_bytes=4 * MIB),
        name="combine",
    )(columns, own, recv)


def update_kernel(sizes, *refs):
    (scalar_ref, qkv_ref, out_ref, gu_ref, down_ref, summed_ref, pair_ref) = refs[:7]
    prior_refs, refs = refs[7:11], refs[2:]
    (qkv_cols, out_rows, gu_cols, down_rows, w_qkv, w_out, w_gu, w_down) = refs[9:17]
    (qkv_new, out_new, gu_new, down_new, qkv_cols_new, out_rows_new, gu_cols_new, down_rows_new) = refs[17:25]
    (qkv_rows_new, out_cols_new, gu_rows_new, down_cols_new, attn_gain_ref, mlp_gain_ref, turned, prior_rows_ref) = refs[25:]
    rows = qkv_ref.shape[1]
    width = sizes[0]
    lane = lax.broadcasted_iota(jnp.int32, (1, LANES), 1)
    scalars = as_line(scalar_ref)
    beta = 1.0 - lax.rsqrt(scalars[:, 0:1])
    fresh = 1.0 - beta
    start = lax.rem(width - lax.axis_index("wide") * rows, width)
    prior_rows_ref[...] = jnp.zeros_like(prior_rows_ref)
    at = 0
    for ref in prior_refs:
        value = as_line(ref) if len(ref.shape) == 1 else ref[...]
        prior_rows_ref[at : at + value.shape[0], :] = value
        at += value.shape[0]
    own = pltpu.roll(prior_rows_ref[...], start, 1)[:, 0:LANES]
    turned[...] = jnp.zeros_like(turned)
    turned[0:8, :] = own
    prior_columns = turned[...].T
    gains = pltpu.roll(summed_ref[:, 0:width], start, 1)
    attn_gain_ref[...] = jnp.reshape(gains[5:6, 0:rows], (rows,))
    mlp_gain_ref[...] = jnp.reshape(gains[6:7, 0:rows], (rows,))
    sums = pair_ref[pl.ds(padded(rows) + 2 * width // LANES, 1), :]
    narrow = out_ref.shape[1]
    totals = summed_ref[3:4, 2 * narrow : 2 * narrow + LANES]
    all_rows = jnp.zeros((rows, LANES), F32)
    priors = [qkv_cols[0:1], qkv_cols[1:2], qkv_cols[2:3], as_line(out_rows), gu_cols[0:1], gu_cols[1:2], as_line(down_rows)]
    for i in range(7):
        across = sizes[1 + i]
        entries = float(across * width)
        row_new = beta * prior_columns[0:rows, i : i + 1] + fresh * (pair_ref[0:rows, i : i + 1] / across + TINIEST)
        count = priors[i].shape[1]
        col_new = beta * priors[i] + fresh * (summed_ref[sum_place(i, narrow, count)] / width + TINIEST)
        all_rows = jnp.where(lane == i, row_new, all_rows)
        if i in (3, 6):
            at = 7 + (i == 6)
            prior_mean = sums[:, at : at + 1] / across
        else:
            prior_mean = jnp.mean(prior_rows_ref[i : i + 1, :], axis=1, keepdims=True)
        mean = beta * prior_mean + fresh * (totals[:, i : i + 1] / entries + TINIEST)
        rate = scalars[:, 1:2] * jnp.sqrt(sums[:, i : i + 1] / entries)
        step = lax.rsqrt(row_new * col_new / mean)
        if i in (3, 6):
            gradient_ref, weight_ref, new_ref = ((out_ref, w_out, out_new), (down_ref, w_down, down_new))[i == 6]
            new_ref[...] = (weight_ref[...].astype(F32) - rate * (gradient_ref[...] * step)).astype(BF16)
            (out_rows_new, down_rows_new)[i == 6][...] = jnp.reshape(col_new, (count,))
        else:
            at = i if i < 3 else i - 4
            gradient_ref, weight_ref, new_ref = (qkv_ref, w_qkv, qkv_new) if i < 3 else (gu_ref, w_gu, gu_new)
            new_ref[at] = (weight_ref[at].astype(F32) - rate * (gradient_ref[at] * step)).astype(BF16)
            (qkv_cols_new if i < 3 else gu_cols_new)[at : at + 1] = col_new
    turned[0:rows, :] = all_rows
    rows_new = turned[...].T
    qkv_rows_new[...] = rows_new[0:3, 0:rows]
    out_cols_new[...] = jnp.reshape(rows_new[3:4, 0:rows], (rows,))
    gu_rows_new[...] = rows_new[4:6, 0:rows]
    down_cols_new[...] = jnp.reshape(rows_new[6:7, 0:rows], (rows,))


def update(step_count, learn_rate, grads, summed, pair, prior_rows, col_priors, weights, sizes):
    rows = grads[0].shape[1]
    scalars = jnp.where(jnp.arange(LANES) == 0, step_count.astype(F32), learn_rate)
    inputs = [scalars, *grads, summed, pair, *prior_rows, *col_priors, *weights]
    shapes = [(3, sizes[1] // 2), (sizes[4] // 2,), (2, sizes[5] // 2), (sizes[7] // 2,)]
    shapes += [(3, rows), (rows,), (2, rows), (rows,), (rows,), (rows,)]
    out_shape = [jax.ShapeDtypeStruct(w.shape, BF16) for w in weights]
    out_shape += [jax.ShapeDtypeStruct(s, F32) for s in shapes]
    return pl.pallas_call(
        functools.partial(update_kernel, sizes),
        grid=(1,),
        in_specs=[whole(a.shape) for a in inputs],
        out_specs=[whole(s.shape) for s in out_shape],
        scratch_shapes=[pltpu.VMEM((LANES, LANES), F32), pltpu.VMEM((8, sizes[0]), F32)],
        out_shape=out_shape,
        compiler_params=pltpu.CompilerParams(vmem_limit_bytes=8 * MIB),
        cost_estimate=cost(1 << 20, 4 << 20),
        name="update",
    )(*inputs)


def weights_kernel(rows, qkv_ref, out_ref, gu_ref, down_ref, out_rows_ref, down_rows_ref, line_ref, *refs):
    qkv_own, out_own, gu_own, down_own, sums, qkv_total, gu_total = refs
    step = pl.program_id(0)
    values = [qkv_ref.at[0], qkv_ref.at[1], qkv_ref.at[2], out_ref, gu_ref.at[0], gu_ref.at[1], down_ref]
    width = out_ref.shape[1]
    block = qkv_ref.shape[1]
    start = lax.axis_index("wide") * rows

    @pl.when(step == 0)
    def _():
        for ref in (sums, qkv_total, gu_total):
            ref[...] = jnp.zeros_like(ref)

    def chosen(first, count):
        shape = (qkv_total.shape[1], count)
        own = lax.broadcasted_iota(jnp.int32, shape, 0) + start
        return jnp.where(lax.broadcasted_iota(jnp.int32, shape, 1) + first == own, 1.0, 0.0).astype(BF16)

    for i, ref in enumerate(values):
        count = ref.shape[1]
        value = ref[...].astype(F32)
        sums[i : i + 1, 0:count] += jnp.sum(value * value, axis=0, keepdims=True)
    across = chosen(0, width)
    for ref, own_ref in ((out_ref, out_own), (down_ref, down_own)):
        own_ref[...] = mm_nt(across, ref[...])[0:rows].astype(BF16)
    below = chosen(step * block, block)
    for ref, total in ((qkv_ref, qkv_total), (gu_ref, gu_total)):
        for i in range(ref.shape[0]):
            total[i] += mm(below, ref[i])

    @pl.when(step == pl.num_programs(0) - 1)
    def _():
        lane = lax.broadcasted_iota(jnp.int32, (1, LANES), 1)
        line = jnp.zeros((1, LANES), F32)
        for i in range(7):
            line = jnp.where(lane == i, jnp.sum(sums[i : i + 1, :], axis=1, keepdims=True), line)
        for i, ref in enumerate((out_rows_ref, down_rows_ref)):
            line = jnp.where(lane == 7 + i, jnp.sum(as_line(ref), axis=1, keepdims=True), line)
        line_ref[...] = line
        qkv_own[...] = qkv_total[:, 0:rows, :].astype(BF16)
        gu_own[...] = gu_total[:, 0:rows, :].astype(BF16)


def weights_call(w_qkv, w_out, w_gu, w_down, out_rows, down_rows, n_wide):
    width = w_out.shape[1]
    rows, held = width // n_wide, -(-(width // n_wide) // 16) * 16
    heads_width, units = w_qkv.shape[2], w_gu.shape[2]
    steps = 3 if heads_width % (3 * LANES) == 0 and units % (3 * LANES) == 0 else 1
    each = lambda n: n // steps
    shapes = [(3, rows, heads_width), (rows, heads_width), (2, rows, units), (rows, units)]
    line, *own = pl.pallas_call(
        functools.partial(weights_kernel, rows),
        grid=(steps,),
        in_specs=[
            pl.BlockSpec((3, each(width), heads_width), lambda j: (0, j, 0)),
            pl.BlockSpec((each(heads_width), width), lambda j: (j, 0)),
            pl.BlockSpec((2, each(width), units), lambda j: (0, j, 0)),
            pl.BlockSpec((each(units), width), lambda j: (j, 0)),
            whole(out_rows.shape),
            whole(down_rows.shape),
        ],
        out_specs=[
            whole((1, LANES)),
            whole(shapes[0]),
            pl.BlockSpec((rows, each(heads_width)), lambda j: (0, j)),
            whole(shapes[2]),
            pl.BlockSpec((rows, each(units)), lambda j: (0, j)),
        ],
        out_shape=[jax.ShapeDtypeStruct((1, LANES), F32)] + [jax.ShapeDtypeStruct(shape, BF16) for shape in shapes],
        scratch_shapes=[
            pltpu.VMEM((8, max(width, units)), F32),
            pltpu.VMEM((3, held, heads_width), F32),
            pltpu.VMEM((2, held, units), F32),
        ],
        compiler_params=pltpu.CompilerParams(vmem_limit_bytes=20 * MIB),
        cost_estimate=cost(1 << 20, 7 << 20),
        name="weights",
    )(w_qkv, w_out, w_gu, w_down, out_rows, down_rows)
    return line, own


def after(values, *others):
    return lax.optimization_barrier((values, *others))[0]


def far(values):
    return pltpu.with_memory_space_constraint(values, pltpu.HBM)


def body(
    n_wide,
    tokens,
    plot_slot,
    patch_mask,
    cotangent,
    gain_attn,
    w_qkv,
    w_out,
    gain_mlp,
    w_gu,
    w_down,
    qkv_rows,
    qkv_cols,
    out_rows,
    out_cols,
    gu_rows,
    gu_cols,
    down_rows,
    down_cols,
    step_count,
    learn_rate,
):
    width = tokens.shape[1]
    heads_width, units = w_out.shape[0], w_down.shape[0]
    rows_each = width // n_wide
    chunk = 256
    tokens_other = swap(tokens)
    carried = project(0, far(tokens), far(gain_attn), far(w_qkv), [])
    normed_t, qkv = project(1, tokens_other, gain_attn, w_qkv, carried)
    sent = after((w_out, w_gu, w_down), tokens_other, *carried)
    w_out_other, w_gu_other, w_down_other = swap(sent[0]), swap(sent[1]), swap(sent[2])
    mixed_own, mixed_other, kept, keys = attention(qkv, plot_slot, patch_mask)
    mixed_recv = swap(mixed_other)
    steps = units // chunk // 2

    inputs = [tokens, mixed_own, mixed_recv, w_out, w_out_other, gain_mlp, cotangent, keys]
    wide_parts = []
    for i in range(2):
        at = i * steps
        outs, part_other = middle_call(i == 0, None, inputs, w_gu_other, w_down_other, at, steps, n_wide, chunk)
        if i == 0:
            middle, *inputs = outs
        else:
            inputs = [*inputs[:4], *outs, middle, gain_mlp]
        outs, part = middle_call(False, i == 1, inputs, w_gu, w_down, at, steps, n_wide, chunk)
        one = Scatter(WIDE, [[slotted(part, n_wide), slotted(swap(part_other), n_wide)]], n_wide, 0)
        wide_parts.append(one)
        if i == 1:
            mixed_out, middle_grad, attn_seed, mlp_gain_part = outs
            attn_seed = after(attn_seed, wide_parts[0].turn())
            wide_parts[0].go()
            mixed_grad, seed_t = seeds_call(attn_seed, swap(attn_seed), w_out)
            mixed_grad = after(mixed_grad, one.turn(mixed_grad))
        else:
            one.turn()
        one.go()
        inputs = [after(inputs[0], one.send), *inputs[1:4], *outs[:2]]

    pairs = heads_width // LANES
    back = functools.partial(
        attention_back,
        qkv=qkv,
        mixed_own=mixed_own,
        mixed_other=mixed_other,
        kept=kept,
        keys=keys,
        normed_t=normed_t,
        seed_t=seed_t,
        n_wide=n_wide,
    )
    pieces = []
    piece, carried = back(0, 0, pairs - 1, [], grad=mixed_grad)
    pieces.append(piece)
    weights = after((w_qkv, w_out, w_gu, w_down, out_rows, down_rows), piece)
    local_sums, own_weights = weights_call(*weights, n_wide)
    mixed_grad = after(mixed_grad, local_sums)
    for pair in range(1, pairs - 1):
        piece, carried = back(pair, pair, pairs - 1, carried, grad=mixed_grad)
        pieces.append(piece)
    keep, send = kept_and_sent(carried, n_wide)
    send = after(send, wide_parts[1].turn(piece))
    wide_parts[1].go()
    first = [keep, stage_exchange(send, 0, n_wide, PAIRS)]
    mixed_grad = after(mixed_grad, send)
    piece, carried = back(pairs - 1, 0, 1, [], grad=mixed_grad)
    pieces.append(piece)
    keep, send = kept_and_sent(carried, n_wide)
    last = [keep, stage_exchange(send, 0, n_wide, PAIRS)]
    pair_batch = Scatter(PAIRS, [first, last], n_wide, 1)
    wide_batch = Scatter(WIDE, [one.groups[0] + one.joint for one in wide_parts], n_wide, 2)
    batches = wide_batch.finish(pair_batch)
    back_other = swap(input_other(pieces, w_qkv))
    tokens_grad, attn_gain_part = input_grad(pieces, w_qkv, back_other, tokens, gain_attn, middle_grad)

    *grads, columns, pair = gather_own(
        batches, attn_gain_part, mlp_gain_part, local_sums, heads_width, units, chunk
    )
    summed, pair = combine(columns, pair, swap(pair), rows_each, width, heads_width)
    for stage in range(n_wide.bit_length() - 1):
        summed = summed + stage_exchange(summed, stage, n_wide, PAIRS)
    outs = update(
        step_count,
        learn_rate,
        [far(grad) for grad in grads],
        summed,
        pair,
        [qkv_rows, out_cols, gu_rows, down_cols],
        [qkv_cols, out_rows, gu_cols, down_rows],
        own_weights,
        [width] + [2 * heads_width] * 4 + [2 * units] * 3,
    )
    qkv_new, out_new, gu_new, down_new, qkv_cols_new, out_rows_new, gu_cols_new, down_rows_new = outs[:8]
    qkv_rows_new, out_cols_new, gu_rows_new, down_cols_new, attn_gain_grad, mlp_gain_grad = outs[8:]
    qkv_grad, out_grad, gu_grad, down_grad = grads
    return (
        mixed_out,
        tokens_grad,
        attn_gain_grad,
        qkv_grad,
        out_grad.T,
        mlp_gain_grad,
        gu_grad,
        down_grad.T,
        qkv_new,
        out_new.T,
        gu_new,
        down_new.T,
        qkv_rows_new,
        qkv_cols_new,
        out_rows_new,
        out_cols_new,
        gu_rows_new,
        gu_cols_new,
        down_rows_new,
        down_cols_new,
    )


def solution(mesh):
    in_specs = (
        P(("wide", "narrow"), None),
        P("wide"),
        P("wide"),
        P(("wide", "narrow"), None),
        P(),
        P(None, None, "narrow"),
        P("narrow", None),
        P(),
        P(None, None, "narrow"),
        P("narrow", None),
        P(),
        P(None, "narrow"),
        P("narrow"),
        P(),
        P(),
        P(None, "narrow"),
        P("narrow"),
        P(),
        P(),
        P(),
    )
    out_specs = (
        P(("wide", "narrow"), None),
        P(("wide", "narrow"), None),
        P("wide"),
        P(None, "wide", "narrow"),
        P("narrow", "wide"),
        P("wide"),
        P(None, "wide", "narrow"),
        P("narrow", "wide"),
        P(None, "wide", "narrow"),
        P("narrow", "wide"),
        P(None, "wide", "narrow"),
        P("narrow", "wide"),
        P(None, "wide"),
        P(None, "narrow"),
        P("narrow"),
        P("wide"),
        P(None, "wide"),
        P(None, "narrow"),
        P("narrow"),
        P("wide"),
    )
    return jax.shard_map(
        functools.partial(body, mesh.shape["wide"]),
        mesh=mesh,
        in_specs=in_specs,
        out_specs=out_specs,
        check_vma=False,
    )
```
